32 devices in a mesh: groups: 2 (over y), dap: 4 (over z), chan: 2 (over x), sub: 2 (over core).
Axes of the slice: x: 2, y: 2, z: 4, core: 2. Of those that a mesh axis runs over, the one named last changes fastest.
Arguments:
- pair_input: bfloat16 [768, 384, 128], P(('groups', 'dap'), ('chan', 'sub')), parts along dimension 0, may hold values from -6 to 6
- first_gain: float32 [128], replicated, may hold values from 0.25 to 1.75
- first_project: bfloat16 [128, 512], replicated, may hold values from -0.5 to 0.5
- first_gate: bfloat16 [128, 128], replicated, may hold values from -0.5 to 0.5
- first_norm: float32 [128], replicated, may hold values from 0.25 to 1.75
- first_final: bfloat16 [128, 128], replicated, may hold values from -0.5 to 0.5
- second_gain: float32 [128], replicated, may hold values from 0.25 to 1.75
- second_project: bfloat16 [128, 512], replicated, may hold values from -0.5 to 0.5
- second_gate: bfloat16 [128, 128], replicated, may hold values from -0.5 to 0.5
- second_norm: float32 [128], replicated, may hold values from 0.25 to 1.75
- second_final: bfloat16 [128, 128], replicated, may hold values from -0.5 to 0.5
Outputs:
- pair_output: bfloat16 [768, 384, 128], P(('groups', 'dap'), ('chan', 'sub')), parts along dimension 0
The draws below stay inside these ranges and needn't reach their ends.
There are 2 independent parts, one for each index of `groups`. The reference program is written for one: setup_inputs(seed, part) draws one part's arguments, and reference() takes and returns one part's arrays. A program takes and returns all parts, laid end to end along the dimension named above; an argument that names none is the same for every part. Nothing has to cross between parts.
All inputs are finite; a program needn't handle non-finite values.
Results may differ from the reference program's by a relative error of at most 0.013.
Values may be sent and summed in bfloat16 or wider, within the bound.
No kernel may reach another device: no remote copies, remote signals or barrier semaphores. Data moves between devices by JAX's collectives and lax.ppermute only.
A program may use at most 64 MiB of HBM per device.

```python
import jax
import jax.numpy as jnp
from jax import lax

C = 128
N = 384


def block_levels(key, extent, shards, least, top_value):
    def one(position, blocks):
        draws = jax.random.uniform(jax.random.fold_in(jax.random.fold_in(key, 6), position), (blocks,), jnp.float32, least / len(shards), top_value / len(shards))
        return jnp.repeat(jnp.exp(draws), extent[position] // blocks).reshape((-1,) + (1,) * (len(extent) - position - 1))

    level = one(*shards[0])
    for cut in shards[1:]:
        level = level * one(*cut)
    return level


def noise(stream_key, shape, width, limit, pieces=(), held_as=jnp.bfloat16):
    drawn = jax.random.normal(stream_key, shape, jnp.float32) * width
    if len(pieces) > 0:
        drawn = block_levels(stream_key, shape, pieces, -0.22, 0.18) * drawn
    return jnp.clip(drawn, min=-limit, max=limit).astype(held_as)


def setup_inputs(seed: int = 0, part: int = 0) -> dict:
    splits = jax.random.split(jax.random.key(seed), 12)
    part_keys = jax.random.split(jax.random.fold_in(splits[11], part), 12)
    return {
        "pair_input": noise(part_keys[0], (N, N, C), 1.0, 6.0, ((0, 4), (1, 4))),
        "first_gain": jnp.clip(1.0 + 0.15 * jax.random.normal(splits[1], (C,), jnp.float32), 0.25, 1.75),
        "first_project": noise(splits[2], (C, 4 * C), C ** -0.5, 0.5),
        "first_gate": noise(splits[3], (C, C), C ** -0.5, 0.5),
        "first_norm": jnp.clip(1.0 + 0.15 * jax.random.normal(splits[4], (C,), jnp.float32), 0.25, 1.75),
        "first_final": noise(splits[5], (C, C), C ** -0.5, 0.5),
        "second_gain": jnp.clip(1.0 + 0.15 * jax.random.normal(splits[6], (C,), jnp.float32), 0.25, 1.75),
        "second_project": noise(splits[7], (C, 4 * C), C ** -0.5, 0.5),
        "second_gate": noise(splits[8], (C, C), C ** -0.5, 0.5),
        "second_norm": jnp.clip(1.0 + 0.15 * jax.random.normal(splits[9], (C,), jnp.float32), 0.25, 1.75),
        "second_final": noise(splits[10], (C, C), C ** -0.5, 0.5),
    }


epsilon = 1e-05

def layer_norm(values, norm_gain, reduce_axis):
    average = lax.optimization_barrier(jnp.mean(values, axis=reduce_axis, keepdims=True))
    centred = values - average
    variance = lax.optimization_barrier(jnp.mean(centred * centred, axis=reduce_axis, keepdims=True))
    return centred * lax.rsqrt(variance + epsilon) * norm_gain

def project_all(pair_state, norm_gain, project, gate_matrix):
    flattened = pair_state.reshape(N * N, C).astype(jnp.float32)
    normed = layer_norm(flattened, norm_gain, 1).astype(jnp.bfloat16)
    first_half = jnp.dot(normed, project[:, :2 * C], preferred_element_type=jnp.float32)
    left_part = (jax.nn.sigmoid(first_half[:, :C]) * first_half[:, C:]).astype(jnp.bfloat16)
    second_half = jnp.dot(normed, project[:, 2 * C:], preferred_element_type=jnp.float32)
    right_part = (jax.nn.sigmoid(second_half[:, :C]) * second_half[:, C:]).astype(jnp.bfloat16)
    gating = jax.nn.sigmoid(jnp.dot(normed, gate_matrix, preferred_element_type=jnp.float32))
    return (left_part.T.reshape(C, N, N), right_part.T.reshape(C, N, N), gating)

def finish(pair_state, mixture, gating, out_gain, final_matrix):
    flattened = mixture.reshape(C, N * N).astype(jnp.float32)
    normed = layer_norm(flattened, out_gain[:, None], 0).astype(jnp.bfloat16)
    update = jnp.dot(normed.T, final_matrix, preferred_element_type=jnp.float32)
    result = pair_state.reshape(N * N, C).astype(jnp.float32) + gating * update
    return result.astype(jnp.bfloat16).reshape(N, N, C)

def reference(pair_input, first_gain, first_project, first_gate, first_norm, first_final, second_gain, second_project, second_gate, second_norm, second_final):
    left_part, right_part, gating = project_all(pair_input, first_gain, first_project, first_gate)
    mixture = jnp.einsum('cik,cjk->cij', left_part.astype(jnp.float32), right_part.astype(jnp.float32)).astype(jnp.bfloat16)
    middle = finish(pair_input, mixture, gating, first_norm, first_final)
    left_part, right_part, gating = project_all(middle, second_gain, second_project, second_gate)
    mixture = jnp.einsum('cki,ckj->cij', left_part.astype(jnp.float32), right_part.astype(jnp.float32)).astype(jnp.bfloat16)
    return finish(middle, mixture, gating, second_norm, second_final)
```

```python
import jax
import jax.numpy as jnp
from jax import lax
from jax.sharding import Mesh
from jax.sharding import PartitionSpec as P

epsilon = 1e-05
EVERY = ("near", "chan", "sub")


def layer_norm(values, norm_gain, reduce_axis):
    average = jnp.mean(values, axis=reduce_axis, keepdims=True)
    centred = values - average
    variance = jnp.mean(centred * centred, axis=reduce_axis, keepdims=True)
    return centred * lax.rsqrt(variance + epsilon) * norm_gain


def project_in(pair_state, norm_gain, project, gate_matrix):
    features = pair_state.shape[-1]
    flattened = pair_state.reshape(-1, features).astype(jnp.float32)
    normed = layer_norm(flattened, norm_gain, 1).astype(jnp.bfloat16)
    projected = jnp.einsum("xc,cd->dx", normed, project, preferred_element_type=jnp.float32)
    left_part = jax.nn.sigmoid(projected[:features]) * projected[features : 2 * features]
    right_part = jax.nn.sigmoid(projected[2 * features : 3 * features]) * projected[3 * features :]
    gating = jax.nn.sigmoid(jnp.dot(normed, gate_matrix, preferred_element_type=jnp.float32))
    return left_part.astype(jnp.bfloat16), right_part.astype(jnp.bfloat16), gating


def finish(pair_state, mixture, gating, out_gain, final_matrix):
    features = mixture.shape[0]
    flattened = mixture.astype(jnp.float32)
    normed = layer_norm(flattened, out_gain[:, None], 0).astype(jnp.bfloat16)
    update = jnp.einsum("cx,cd->xd", normed, final_matrix, preferred_element_type=jnp.float32)
    result = pair_state.reshape(-1, features).astype(jnp.float32) + gating * update
    return result.astype(jnp.bfloat16).reshape(pair_state.shape)


def update(incoming, sizes, pair_state, norm_gain, project, gate_matrix, out_gain, final_matrix):
    far, near, col_parts = sizes
    row_count, col_count, features = pair_state.shape
    parts = near * col_parts
    width = features // parts
    left_part, right_part, gating = project_in(pair_state, norm_gain, project, gate_matrix)
    both = jnp.stack([left_part.reshape(parts, width, -1), right_part.reshape(parts, width, -1)], axis=1)
    both = lax.all_to_all(both, EVERY, split_axis=0, concat_axis=0, tiled=True)
    both = both.reshape(near, col_parts, 2, width, row_count, col_count)
    both = both.transpose(2, 3, 0, 4, 1, 5).reshape(2, width, near * row_count, col_parts * col_count)
    left_part, right_part = both[0], both[1]
    if incoming:
        mixture = jnp.einsum("cki,ckj->cij", left_part, right_part, preferred_element_type=jnp.float32)
        if far > 1:
            mixture = lax.psum_scatter(mixture, "far", scatter_dimension=1, tiled=True)
    else:
        if far > 1:
            right_part = lax.all_gather(right_part, "far", axis=1, tiled=True)
        mixture = jnp.einsum("cik,cjk->cij", left_part, right_part, preferred_element_type=jnp.float32)
    mixture = mixture.astype(jnp.bfloat16).reshape(width, near, row_count, col_parts, col_count)
    mixture = mixture.transpose(1, 3, 0, 2, 4).reshape(parts, width, row_count * col_count)
    mixture = lax.all_to_all(mixture, EVERY, split_axis=0, concat_axis=0, tiled=True)
    return finish(pair_state, mixture.reshape(features, -1), gating, out_gain, final_matrix)


def split_rows(row_parts, col_parts, features, least):
    near = row_parts
    while near > 1 and (row_parts % near or features % (near * col_parts) or features < least * near * col_parts):
        near -= 1
    return row_parts // near, near


def solution(mesh):
    row_parts, col_parts = mesh.shape["dap"], mesh.shape["chan"] * mesh.shape["sub"]

    def whole(pair_input, *weights):
        far, near = split_rows(row_parts, col_parts, pair_input.shape[-1], 8)
        sizes = (far, near, col_parts)
        finer = Mesh(
            mesh.devices.reshape(mesh.shape["groups"], far, near, mesh.shape["chan"], mesh.shape["sub"]),
            ("groups", "far", "near", "chan", "sub"),
        )

        def shards(pair_input, *weights):
            middle = update(False, sizes, pair_input, *weights[:5])
            return update(True, sizes, middle, *weights[5:])

        pair_spec = P(("groups", "far", "near"), ("chan", "sub"), None)
        return jax.shard_map(
            shards,
            mesh=finer,
            in_specs=(pair_spec,) + (P(),) * 10,
            out_specs=pair_spec,
            check_vma=False,
        )(pair_input, *weights)

    return whole
```

```python
import functools

import jax
import jax.numpy as jnp
from jax import lax
from jax.experimental import pallas as pl
from jax.experimental.pallas import tpu as pltpu
from jax.sharding import Mesh
from jax.sharding import PartitionSpec as P

epsilon = 1e-05
EVERY = ("near", "chan", "sub")
LANES = 128
BUDGET = 56 << 20


def layer_norm(values, norm_gain, reduce_axis):
    average = jnp.mean(values, axis=reduce_axis, keepdims=True)
    centred = values - average
    variance = jnp.mean(centred * centred, axis=reduce_axis, keepdims=True)
    return centred * lax.rsqrt(variance + epsilon) * norm_gain


def sigmoid(values):
    return 0.5 * jnp.tanh(0.5 * values) + 0.5


def project_in(pair_state, norm_gain, project, gate_matrix):
    features = pair_state.shape[-1]
    flattened = pair_state.reshape(-1, features).astype(jnp.float32)
    normed = layer_norm(flattened, norm_gain, 1).astype(jnp.bfloat16)
    projected = jnp.einsum("xc,cd->dx", normed, project, preferred_element_type=jnp.float32)
    left_part = jax.nn.sigmoid(projected[:features]) * projected[features : 2 * features]
    right_part = jax.nn.sigmoid(projected[2 * features : 3 * features]) * projected[3 * features :]
    gating = jax.nn.sigmoid(jnp.dot(normed, gate_matrix, preferred_element_type=jnp.float32))
    return left_part.astype(jnp.bfloat16), right_part.astype(jnp.bfloat16), gating


def finish(pair_state, mixture, gating, out_gain, final_matrix):
    features = mixture.shape[0]
    flattened = mixture.astype(jnp.float32)
    normed = layer_norm(flattened, out_gain[:, None], 0).astype(jnp.bfloat16)
    update = jnp.einsum("cx,cd->xd", normed, final_matrix, preferred_element_type=jnp.float32)
    result = pair_state.reshape(-1, features).astype(jnp.float32) + gating * update
    return result.astype(jnp.bfloat16).reshape(pair_state.shape)


def update(incoming, sizes, pair_state, norm_gain, project, gate_matrix, out_gain, final_matrix):
    far, near, col_parts = sizes
    row_count, col_count, features = pair_state.shape
    parts = near * col_parts
    width = features // parts
    left_part, right_part, gating = project_in(pair_state, norm_gain, project, gate_matrix)
    both = jnp.stack([left_part.reshape(parts, width, -1), right_part.reshape(parts, width, -1)], axis=1)
    both = lax.all_to_all(both, EVERY, split_axis=0, concat_axis=0, tiled=True)
    both = both.reshape(near, col_parts, 2, width, row_count, col_count)
    both = both.transpose(2, 3, 0, 4, 1, 5).reshape(2, width, near * row_count, col_parts * col_count)
    left_part, right_part = both[0], both[1]
    if incoming:
        mixture = jnp.einsum("cki,ckj->cij", left_part, right_part, preferred_element_type=jnp.float32)
        if far > 1:
            mixture = lax.psum_scatter(mixture, "far", scatter_dimension=1, tiled=True)
    else:
        if far > 1:
            right_part = lax.all_gather(right_part, "far", axis=1, tiled=True)
        mixture = jnp.einsum("cik,cjk->cij", left_part, right_part, preferred_element_type=jnp.float32)
    mixture = mixture.astype(jnp.bfloat16).reshape(width, near, row_count, col_parts, col_count)
    mixture = mixture.transpose(1, 3, 0, 2, 4).reshape(parts, width, row_count * col_count)
    mixture = lax.all_to_all(mixture, EVERY, split_axis=0, concat_axis=0, tiled=True)
    return finish(pair_state, mixture.reshape(features, -1), gating, out_gain, final_matrix)


def split_rows(row_parts, col_parts, features, least):
    near = row_parts
    while near > 1 and (row_parts % near or features % (near * col_parts) or features < least * near * col_parts):
        near -= 1
    return row_parts // near, near


def emit_projections(normed, gate_rows, value_rows, out_refs):
    at = 0
    for ref in out_refs:
        rows = ref.shape[0]
        gates = lax.dot_general(
            gate_rows[at : at + rows, :], normed, (((1,), (1,)), ((), ())), preferred_element_type=jnp.float32
        )
        values = lax.dot_general(
            value_rows[at : at + rows, :], normed, (((1,), (1,)), ((), ())), preferred_element_type=jnp.float32
        )
        ref[...] = (sigmoid(gates) * values).astype(ref.dtype)
        at += rows


def project_kernel(state_ref, gain_ref, gate_rows, value_rows, *out_refs):
    normed = layer_norm(state_ref[...].astype(jnp.float32), gain_ref[...], 1).astype(jnp.bfloat16)
    emit_projections(normed, gate_rows, value_rows, out_refs)


def finish_kernel(pieces, onward, *refs):
    mix_refs, refs = refs[:pieces], refs[pieces:]
    state_ref, gain_ref, gate_ref, out_gain_ref, final_ref = refs[:5]
    state = state_ref[...].astype(jnp.float32)
    normed = layer_norm(state, gain_ref[...], 1).astype(jnp.bfloat16)
    gating = sigmoid(jnp.dot(normed, gate_ref[...], preferred_element_type=jnp.float32))
    mixed = jnp.concatenate([ref[...].astype(jnp.float32) for ref in mix_refs], axis=0)
    mixed = layer_norm(mixed, out_gain_ref[...], 0).astype(jnp.bfloat16)
    change = lax.dot_general(
        mixed, final_ref[...], (((0,), (0,)), ((), ())), preferred_element_type=jnp.float32
    )
    result = (state + gating * change).astype(jnp.bfloat16)
    if onward:
        next_gain, gate_rows, value_rows, middle_ref = refs[5:9]
        middle_ref[...] = result
        normed = layer_norm(result.astype(jnp.float32), next_gain[...], 1).astype(jnp.bfloat16)
        emit_projections(normed, gate_rows, value_rows, refs[9:])
    else:
        refs[5][...] = result


def whole_spec(array):
    return pl.BlockSpec(array.shape, lambda step: (0,) * array.ndim)


def row_step(positions):
    step = positions
    for candidate in range(LANES, 1152 + 1, LANES):
        if positions % candidate == 0:
            step = candidate
    return step


def run_projections(state, gain, gate_rows, value_rows, out_rows):
    positions, features = state.shape
    step = row_step(positions)
    weights = (gain[None, :], gate_rows, value_rows)
    return pl.pallas_call(
        project_kernel,
        grid=(positions // step,),
        in_specs=[pl.BlockSpec((step, features), lambda i: (i, 0))] + [whole_spec(w) for w in weights],
        out_specs=[pl.BlockSpec((rows, step), lambda i: (0, i)) for rows in out_rows],
        out_shape=[jax.ShapeDtypeStruct((rows, positions), jnp.bfloat16) for rows in out_rows],
        compiler_params=pltpu.CompilerParams(vmem_limit_bytes=BUDGET),
        name="project",
    )(state, *weights)


def run_finish(mixes, state, gain, gate_matrix, out_gain, final_matrix, onward=None):
    positions, features = state.shape
    step = row_step(positions)
    weights = (gain[None, :], gate_matrix, out_gain[:, None], final_matrix)
    out_shape = [jax.ShapeDtypeStruct((positions, features), jnp.bfloat16)]
    out_specs = [pl.BlockSpec((step, features), lambda i: (i, 0))]
    if onward is not None:
        next_gain, gate_rows, value_rows, out_rows = onward
        weights += (next_gain[None, :], gate_rows, value_rows)
        out_shape += [jax.ShapeDtypeStruct((rows, positions), jnp.bfloat16) for rows in out_rows]
        out_specs += [pl.BlockSpec((rows, step), lambda i: (0, i)) for rows in out_rows]
    return pl.pallas_call(
        functools.partial(finish_kernel, len(mixes), onward is not None),
        grid=(positions // step,),
        in_specs=[pl.BlockSpec((m.shape[0], step), lambda i: (0, i)) for m in mixes]
        + [pl.BlockSpec((step, features), lambda i: (i, 0))]
        + [whole_spec(w) for w in weights],
        out_specs=out_specs,
        out_shape=out_shape,
        compiler_params=pltpu.CompilerParams(vmem_limit_bytes=BUDGET),
        name="finish",
    )(*mixes, state, *weights)


class Folds:
    def __init__(self, row_count, col_count):
        turn = 1
        while (turn * col_count) % LANES:
            turn *= 2
        self.turn, self.tiles = turn, turn * col_count // LANES
        self.cols, self.rows = col_count, row_count
        self.groups = row_count // turn
        self.lane_rows = row_count * col_count // LANES

    def fits(self):
        return self.cols <= LANES and self.rows % self.turn == 0 and self.groups % 8 == 0

    def split(self, lane_rows):
        lane = lax.broadcasted_iota(jnp.int32, lane_rows[0].shape, 1)
        out = []
        for phase in range(self.turn):
            first, offset = divmod(phase * self.cols, LANES)
            value = lane_rows[first]
            if offset + self.cols > LANES:
                value = jnp.where(lane >= offset, value, lane_rows[first + 1])
            if offset:
                value = pltpu.roll(value, LANES - offset, 1)
            out.append(jnp.where(lane < self.cols, value, 0.0))
        return out

    def join(self, block_rows):
        lane = lax.broadcasted_iota(jnp.int32, block_rows[0].shape, 1)
        rolled = []
        for phase, value in enumerate(block_rows):
            offset = (phase * self.cols) % LANES
            rolled.append(pltpu.roll(value, offset, 1) if offset else value)
        out = []
        for tile in range(self.tiles):
            value = None
            for phase in range(self.turn):
                begin, end = phase * self.cols - tile * LANES, (phase + 1) * self.cols - tile * LANES
                if end <= 0 or begin >= LANES:
                    continue
                value = rolled[phase] if value is None else jnp.where(lane >= begin, rolled[phase], value)
            out.append(value)
        return out


def stage(source_ref, staged):
    rows = source_ref.shape[0]
    for tile in range(source_ref.shape[1] // LANES):
        staged[tile * rows : (tile + 1) * rows, :] = source_ref[:, tile * LANES : (tile + 1) * LANES].astype(
            jnp.float32
        )


def unstage(staged, target_ref):
    rows = target_ref.shape[0]
    for tile in range(target_ref.shape[1] // LANES):
        target_ref[:, tile * LANES : (tile + 1) * LANES] = staged[tile * rows : (tile + 1) * rows, :].astype(
            target_ref.dtype
        )


def lane_rows_of(folds, rows, row):
    return [pl.ds(row + tile * rows, folds.groups, stride=folds.tiles * rows) for tile in range(folds.tiles)]


def mix_out_kernel(folds, near, cols, width, half_ref, left_ref, here_ref, there_ref, mix_ref, staged, left, right):
    parts = near * cols
    rows = parts * width
    block = folds.rows
    far = cols // near

    stage(left_ref, staged)

    @pl.loop(0, rows)
    def _(row):
        pieces = folds.split([staged[at, :] for at in lane_rows_of(folds, rows, row)])
        source, channel = row // width, row % width
        at = (channel * cols + source % cols) * near * block + (source // cols) * block
        left[pl.ds(pl.multiple_of(at, block), block), :] = jnp.concatenate(pieces, axis=0).astype(jnp.bfloat16)

    for which, ref in ((0, here_ref), (1, there_ref)):
        stage(ref, staged)
        half = half_ref[which]

        @pl.loop(0, rows)
        def _(row):
            pieces = folds.split([staged[at, :] for at in lane_rows_of(folds, rows, row)])
            source, channel = row // width, row % width
            at = ((channel * cols + source % cols) * far + half) * near * block + (source // cols) * block
            for phase, piece in enumerate(pieces):
                right[pl.ds(at + phase, folds.groups, stride=folds.turn), :] = piece

    @pl.loop(0, width)
    def _(channel):
        for target in range(cols):
            total = None
            for col in range(cols):
                lhs = left[pl.ds(pl.multiple_of((channel * cols + col) * near * block, block), near * block), :]
                at = ((channel * cols + col) * far * near + target) * block
                rhs = right[pl.ds(pl.multiple_of(at, block), block), :].astype(jnp.bfloat16)
                part = lax.dot_general(lhs, rhs, (((1,), (1,)), ((), ())), preferred_element_type=jnp.float32)
                total = part if total is None else total + part
            total = jnp.concatenate([total, jnp.zeros((near * block, LANES - block), jnp.float32)], axis=1)
            for piece in range(near):
                groups = folds.groups
                base = piece * block
                lane_rows = folds.join(
                    [total[base + phase * groups : base + (phase + 1) * groups, :] for phase in range(folds.turn)]
                )
                out_row = (piece * cols + target) * width + channel
                for at, value in zip(lane_rows_of(folds, rows, out_row), lane_rows):
                    staged[at, :] = value

    unstage(staged, mix_ref)


def mix_in_kernel(folds, near, cols, width, half_ref, both_ref, keep_ref, send_ref, staged, left, right, turned, mixed):
    parts = near * cols
    rows = 2 * parts * width
    block = folds.rows

    stage(both_ref, staged)

    for target, shift in ((left, 0), (right, width)):

        @pl.loop(0, parts * width)
        def _(step):
            source, channel = step // width, step % width
            row = source * 2 * width + shift + channel
            pieces = folds.split([staged[at, :] for at in lane_rows_of(folds, rows, row)])
            at = (channel * cols + source % cols) * near * block + (source // cols) * block
            target[pl.ds(pl.multiple_of(at, block), block), :] = jnp.concatenate(pieces, axis=0).astype(jnp.bfloat16)

    out_rows = parts * width
    tall = near * block

    @pl.loop(0, width)
    def _(channel):
        for upper in range(cols):
            lhs = left[pl.ds(pl.multiple_of((channel * cols + upper) * tall, block), tall), :]
            for target in range(cols):
                rhs = right[pl.ds(pl.multiple_of((channel * cols + target) * tall, block), tall), :]
                turned[target] = lax.dot_general(lhs, rhs, (((0,), (0,)), ((), ())), preferred_element_type=jnp.float32)
                lane_rows = folds.join(
                    [turned[target, pl.ds(phase, folds.groups, stride=folds.turn), :] for phase in range(folds.turn)]
                )
                half, piece = divmod(upper, near)
                out_row = (piece * cols + target) * width + channel
                for at, value in zip(lane_rows_of(folds, out_rows, out_row), lane_rows):
                    mixed[half, at, :] = value

    unstage(mixed.at[half_ref[0]], keep_ref)
    unstage(mixed.at[half_ref[1]], send_ref)


SMEM_SPEC = pl.BlockSpec(memory_space=pltpu.SMEM)
VMEM_SPEC = pl.BlockSpec(memory_space=pltpu.VMEM)


def run_mix_out(folds, near, cols, halves, left, here, there):
    rows, positions = left.shape
    width = rows // (near * cols)
    block = folds.rows
    return pl.pallas_call(
        functools.partial(mix_out_kernel, folds, near, cols, width),
        in_specs=[SMEM_SPEC, VMEM_SPEC, VMEM_SPEC, VMEM_SPEC],
        out_specs=VMEM_SPEC,
        out_shape=jax.ShapeDtypeStruct((rows, positions), jnp.bfloat16),
        scratch_shapes=[
            pltpu.VMEM((rows * folds.lane_rows, LANES), jnp.float32),
            pltpu.VMEM((width * cols * near * block, LANES), jnp.bfloat16),
            pltpu.VMEM((width * cols * cols * block, LANES), jnp.float32),
        ],
        compiler_params=pltpu.CompilerParams(vmem_limit_bytes=BUDGET),
        name="mix_out",
    )(halves, left, here, there)


def run_mix_in(folds, near, cols, halves, both):
    rows, positions = both.shape
    width = rows // (2 * near * cols)
    block = folds.rows
    return pl.pallas_call(
        functools.partial(mix_in_kernel, folds, near, cols, width),
        in_specs=[SMEM_SPEC, VMEM_SPEC],
        out_specs=[VMEM_SPEC, VMEM_SPEC],
        out_shape=[
            jax.ShapeDtypeStruct((rows // 2, positions), jnp.float32),
            jax.ShapeDtypeStruct((rows // 2, positions), jnp.bfloat16),
        ],
        scratch_shapes=[
            pltpu.VMEM((rows * folds.lane_rows, LANES), jnp.float32),
            pltpu.VMEM((width * cols * near * block, LANES), jnp.bfloat16),
            pltpu.VMEM((width * cols * near * block, LANES), jnp.bfloat16),
            pltpu.VMEM((cols, LANES, LANES), jnp.float32),
            pltpu.VMEM((2, rows // 2 * folds.lane_rows, LANES), jnp.float32),
        ],
        compiler_params=pltpu.CompilerParams(vmem_limit_bytes=BUDGET),
        name="mix_in",
    )(halves, both)


PIECES = 2


def exchange(array):
    return lax.all_to_all(array, EVERY, split_axis=0, concat_axis=0, tiled=True)


def across(array):
    return lax.ppermute(array, "far", ((0, 1), (1, 0)))


def in_halves(sizes, pair_input, weights):
    far, near, cols = sizes
    row_count, col_count, features = pair_input.shape
    parts = near * cols
    width = features // parts
    pieces = PIECES
    folds = Folds(row_count, col_count)
    half = lax.axis_index("far")
    halves = jnp.stack([half, 1 - half]).astype(jnp.int32)

    def by_piece(rows):
        return rows.reshape(parts, pieces, width // pieces, -1).transpose(1, 0, 2, 3)

    def rows_of(project, order):
        ga, va, gb, vb = (by_piece(rows) for rows in jnp.split(project.T, 4, axis=0))
        return order(ga, gb).reshape(-1, features), order(va, vb).reshape(-1, features)

    def right_then_left(left, right):
        return jnp.concatenate([right, left], axis=0)

    def side_by_side(left, right):
        return jnp.concatenate([left, right], axis=2)

    def unordered(array):
        return by_piece(array.reshape(features, -1)).reshape(array.shape)

    gain_1, project_1, gate_1, norm_1, final_1, gain_2, project_2, gate_2, norm_2, final_2 = weights
    state = pair_input.reshape(-1, features)
    piece_rows = features // pieces

    out = run_projections(state, gain_1, *rows_of(project_1, right_then_left), (piece_rows,) * (2 * pieces))
    here = [exchange(x) for x in out[:pieces]]
    there = [across(x) for x in here]
    left = [exchange(x) for x in out[pieces:]]
    mixes = [exchange(run_mix_out(folds, near, cols, halves, *x)) for x in zip(left, here, there)]
    onward = (gain_2, *rows_of(project_2, side_by_side), (2 * piece_rows,) * pieces)
    out = run_finish(mixes, state, gain_1, gate_1, unordered(norm_1), unordered(final_1), onward)
    middle, both = out[0], [exchange(x) for x in out[1:]]
    parted = [run_mix_in(folds, near, cols, halves, x) for x in both]
    arrived = [across(sent) for _, sent in parted]
    mixes = [
        exchange((kept + got.astype(jnp.float32)).astype(jnp.bfloat16)) for (kept, _), got in zip(parted, arrived)
    ]
    result = run_finish(mixes, middle, gain_2, gate_2, unordered(norm_2), unordered(final_2))[0]
    return result.reshape(pair_input.shape)


def solution(mesh):
    row_parts, col_parts = mesh.shape["dap"], mesh.shape["chan"] * mesh.shape["sub"]

    def whole(pair_input, *weights):
        features = pair_input.shape[-1]
        block_rows = pair_input.shape[0] // (mesh.shape["groups"] * row_parts)
        block_cols = pair_input.shape[1] // col_parts
        halved = (
            row_parts % 2 == 0
            and row_parts == col_parts
            and block_rows == block_cols
            and Folds(block_rows, block_cols).fits()
            and features == LANES
            and features % (row_parts // 2 * col_parts * 8 * PIECES) == 0
        )
        if halved:
            far, near = 2, row_parts // 2
        else:
            far, near = split_rows(row_parts, col_parts, features, 8)
        sizes = (far, near, col_parts)
        finer = Mesh(
            mesh.devices.reshape(mesh.shape["groups"], far, near, mesh.shape["chan"], mesh.shape["sub"]),
            ("groups", "far", "near", "chan", "sub"),
        )

        def shards(pair_input, *weights):
            if halved:
                return in_halves(sizes, pair_input, weights)
            middle = update(False, sizes, pair_input, *weights[:5])
            return update(True, sizes, middle, *weights[5:])

        pair_spec = P(("groups", "far", "near"), ("chan", "sub"), None)
        return jax.shard_map(
            shards,
            mesh=finer,
            in_specs=(pair_spec,) + (P(),) * 10,
            out_specs=pair_spec,
            check_vma=False,
        )(pair_input, *weights)

    return whole
```

```python
import functools

import jax
import jax.numpy as jnp
from jax import lax
from jax.experimental import pallas as pl
from jax.experimental.pallas import tpu as pltpu
from jax.sharding import Mesh
from jax.sharding import PartitionSpec as P


epsilon = 1e-05
EVERY = ("near", "chan", "sub")
LANES = 128
BUDGET = 56 << 20


def layer_norm(values, norm_gain, reduce_axis):
    average = jnp.mean(values, axis=reduce_axis, keepdims=True)
    centred = values - average
    variance = jnp.mean(centred * centred, axis=reduce_axis, keepdims=True)
    return centred * lax.rsqrt(variance + epsilon) * norm_gain


def sigmoid(values):
    return 0.5 * jnp.tanh(0.5 * values) + 0.5


def project_in(pair_state, norm_gain, project, gate_matrix):
    features = pair_state.shape[-1]
    flattened = pair_state.reshape(-1, features).astype(jnp.float32)
    normed = layer_norm(flattened, norm_gain, 1).astype(jnp.bfloat16)
    projected = jnp.einsum("xc,cd->dx", normed, project, preferred_element_type=jnp.float32)
    left_part = jax.nn.sigmoid(projected[:features]) * projected[features : 2 * features]
    right_part = jax.nn.sigmoid(projected[2 * features : 3 * features]) * projected[3 * features :]
    gating = jax.nn.sigmoid(jnp.dot(normed, gate_matrix, preferred_element_type=jnp.float32))
    return left_part.astype(jnp.bfloat16), right_part.astype(jnp.bfloat16), gating


def finish(pair_state, mixture, gating, out_gain, final_matrix):
    features = mixture.shape[0]
    flattened = mixture.astype(jnp.float32)
    normed = layer_norm(flattened, out_gain[:, None], 0).astype(jnp.bfloat16)
    update = jnp.einsum("cx,cd->xd", normed, final_matrix, preferred_element_type=jnp.float32)
    result = pair_state.reshape(-1, features).astype(jnp.float32) + gating * update
    return result.astype(jnp.bfloat16).reshape(pair_state.shape)


def update(incoming, sizes, pair_state, norm_gain, project, gate_matrix, out_gain, final_matrix):
    far, near, col_parts = sizes
    row_count, col_count, features = pair_state.shape
    parts = near * col_parts
    width = features // parts
    left_part, right_part, gating = project_in(pair_state, norm_gain, project, gate_matrix)
    both = jnp.stack([left_part.reshape(parts, width, -1), right_part.reshape(parts, width, -1)], axis=1)
    both = lax.all_to_all(both, EVERY, split_axis=0, concat_axis=0, tiled=True)
    both = both.reshape(near, col_parts, 2, width, row_count, col_count)
    both = both.transpose(2, 3, 0, 4, 1, 5).reshape(2, width, near * row_count, col_parts * col_count)
    left_part, right_part = both[0], both[1]
    if incoming:
        mixture = jnp.einsum("cki,ckj->cij", left_part, right_part, preferred_element_type=jnp.float32)
        if far > 1:
            mixture = lax.psum_scatter(mixture, "far", scatter_dimension=1, tiled=True)
    else:
        if far > 1:
            right_part = lax.all_gather(right_part, "far", axis=1, tiled=True)
        mixture = jnp.einsum("cik,cjk->cij", left_part, right_part, preferred_element_type=jnp.float32)
    mixture = mixture.astype(jnp.bfloat16).reshape(width, near, row_count, col_parts, col_count)
    mixture = mixture.transpose(1, 3, 0, 2, 4).reshape(parts, width, row_count * col_count)
    mixture = lax.all_to_all(mixture, EVERY, split_axis=0, concat_axis=0, tiled=True)
    return finish(pair_state, mixture.reshape(features, -1), gating, out_gain, final_matrix)


def split_rows(row_parts, col_parts, features, least):
    near = row_parts
    while near > 1 and (row_parts % near or features % (near * col_parts) or features < least * near * col_parts):
        near -= 1
    return row_parts // near, near


def emit_projections(normed, gate_rows, value_rows, out_refs):
    at = 0
    for ref in out_refs:
        rows = ref.shape[0]
        gates = lax.dot_general(
            gate_rows[at : at + rows, :], normed, (((1,), (1,)), ((), ())), preferred_element_type=jnp.float32
        )
        values = lax.dot_general(
            value_rows[at : at + rows, :], normed, (((1,), (1,)), ((), ())), preferred_element_type=jnp.float32
        )
        ref[...] = (sigmoid(gates) * values).astype(ref.dtype)
        at += rows


def project_kernel(state_ref, gain_ref, gate_rows, value_rows, *out_refs):
    normed = layer_norm(state_ref[...].astype(jnp.float32), gain_ref[...], 1).astype(jnp.bfloat16)
    emit_projections(normed, gate_rows, value_rows, out_refs)


def finish_kernel(pieces, onward, *refs):
    mix_refs, refs = refs[:pieces], refs[pieces:]
    state_ref, gain_ref, gate_ref, out_gain_ref, final_ref = refs[:5]
    state = state_ref[...].astype(jnp.float32)
    normed = layer_norm(state, gain_ref[...], 1).astype(jnp.bfloat16)
    gating = sigmoid(jnp.dot(normed, gate_ref[...], preferred_element_type=jnp.float32))
    mixed = jnp.concatenate([ref[...].astype(jnp.float32) for ref in mix_refs], axis=0)
    mixed = layer_norm(mixed, out_gain_ref[...], 0).astype(jnp.bfloat16)
    change = lax.dot_general(
        mixed, final_ref[...], (((0,), (0,)), ((), ())), preferred_element_type=jnp.float32
    )
    result = (state + gating * change).astype(jnp.bfloat16)
    if onward:
        next_gain, gate_rows, value_rows, middle_ref = refs[5:9]
        middle_ref[...] = result
        normed = layer_norm(result.astype(jnp.float32), next_gain[...], 1).astype(jnp.bfloat16)
        emit_projections(normed, gate_rows, value_rows, refs[9:])
    else:
        refs[5][...] = result


def whole_spec(array):
    return pl.BlockSpec(array.shape, lambda step: (0,) * array.ndim)


def row_step(positions):
    step = positions
    for candidate in range(LANES, 1152 + 1, LANES):
        if positions % candidate == 0:
            step = candidate
    return step


def run_projections(state, gain, gate_rows, value_rows, out_rows):
    positions, features = state.shape
    step = row_step(positions)
    weights = (gain[None, :], gate_rows, value_rows)
    return pl.pallas_call(
        project_kernel,
        grid=(positions // step,),
        in_specs=[pl.BlockSpec((step, features), lambda i: (i, 0))] + [whole_spec(w) for w in weights],
        out_specs=[pl.BlockSpec((rows, step), lambda i: (0, i)) for rows in out_rows],
        out_shape=[jax.ShapeDtypeStruct((rows, positions), jnp.bfloat16) for rows in out_rows],
        compiler_params=pltpu.CompilerParams(vmem_limit_bytes=BUDGET),
        name="project",
    )(state, *weights)


def run_finish(mixes, state, gain, gate_matrix, out_gain, final_matrix, onward=None):
    positions, features = state.shape
    step = row_step(positions)
    weights = (gain[None, :], gate_matrix, out_gain[:, None], final_matrix)
    out_shape = [jax.ShapeDtypeStruct((positions, features), jnp.bfloat16)]
    out_specs = [pl.BlockSpec((step, features), lambda i: (i, 0))]
    if onward is not None:
        next_gain, gate_rows, value_rows, out_rows = onward
        weights += (next_gain[None, :], gate_rows, value_rows)
        out_shape += [jax.ShapeDtypeStruct((rows, positions), jnp.bfloat16) for rows in out_rows]
        out_specs += [pl.BlockSpec((rows, step), lambda i: (0, i)) for rows in out_rows]
    return pl.pallas_call(
        functools.partial(finish_kernel, len(mixes), onward is not None),
        grid=(positions // step,),
        in_specs=[pl.BlockSpec((m.shape[0], step), lambda i: (0, i)) for m in mixes]
        + [pl.BlockSpec((step, features), lambda i: (i, 0))]
        + [whole_spec(w) for w in weights],
        out_specs=out_specs,
        out_shape=out_shape,
        compiler_params=pltpu.CompilerParams(vmem_limit_bytes=BUDGET),
        name="finish",
    )(*mixes, state, *weights)


class Folds:
    def __init__(self, row_count, col_count):
        turn = 1
        while (turn * col_count) % LANES:
            turn *= 2
        self.turn, self.tiles = turn, turn * col_count // LANES
        self.cols, self.rows = col_count, row_count
        self.groups = row_count // turn
        self.lane_rows = row_count * col_count // LANES

    def fits(self):
        return self.cols <= LANES and self.rows % self.turn == 0 and self.groups % 8 == 0

    def split(self, lane_rows):
        lane = lax.broadcasted_iota(jnp.int32, lane_rows[0].shape, 1)
        out = []
        for phase in range(self.turn):
            first, offset = divmod(phase * self.cols, LANES)
            value = lane_rows[first]
            if offset + self.cols > LANES:
                value = jnp.where(lane >= offset, value, lane_rows[first + 1])
            if offset:
                value = pltpu.roll(value, LANES - offset, 1)
            out.append(jnp.where(lane < self.cols, value, 0.0))
        return out

    def join(self, block_rows):
        lane = lax.broadcasted_iota(jnp.int32, block_rows[0].shape, 1)
        rolled = []
        for phase, value in enumerate(block_rows):
            offset = (phase * self.cols) % LANES
            rolled.append(pltpu.roll(value, offset, 1) if offset else value)
        out = []
        for tile in range(self.tiles):
            value = None
            for phase in range(self.turn):
                begin, end = phase * self.cols - tile * LANES, (phase + 1) * self.cols - tile * LANES
                if end <= 0 or begin >= LANES:
                    continue
                value = rolled[phase] if value is None else jnp.where(lane >= begin, rolled[phase], value)
            out.append(value)
        return out


def stage(source_ref, staged):
    rows = source_ref.shape[0]
    for tile in range(source_ref.shape[1] // LANES):
        staged[tile * rows : (tile + 1) * rows, :] = source_ref[:, tile * LANES : (tile + 1) * LANES].astype(
            jnp.float32
        )


def unstage(staged, target_ref):
    rows = target_ref.shape[0]
    for tile in range(target_ref.shape[1] // LANES):
        target_ref[:, tile * LANES : (tile + 1) * LANES] = staged[tile * rows : (tile + 1) * rows, :].astype(
            target_ref.dtype
        )


def lane_rows_of(folds, rows, row):
    return [pl.ds(row + tile * rows, folds.groups, stride=folds.tiles * rows) for tile in range(folds.tiles)]


def mix_out_kernel(folds, near, cols, width, half_ref, left_ref, here_ref, there_ref, mix_ref, staged, left, right):
    parts = near * cols
    rows = parts * width
    block = folds.rows
    far = cols // near

    stage(left_ref, staged)

    @pl.loop(0, rows, unroll=8)
    def _(row):
        pieces = folds.split([staged[at, :] for at in lane_rows_of(folds, rows, row)])
        source, channel = row // width, row % width
        at = (channel * cols + source % cols) * near * block + (source // cols) * block
        left[pl.ds(pl.multiple_of(at, block), block), :] = jnp.concatenate(pieces, axis=0).astype(jnp.bfloat16)

    for which, ref in ((0, here_ref), (1, there_ref)):
        stage(ref, staged)
        half = half_ref[which]

        @pl.loop(0, rows, unroll=8)
        def _(row):
            pieces = folds.split([staged[at, :] for at in lane_rows_of(folds, rows, row)])
            source, channel = row // width, row % width
            at = ((channel * cols + source % cols) * far + half) * near * block + (source // cols) * block
            for phase, piece in enumerate(pieces):
                right[pl.ds(at + phase, folds.groups, stride=folds.turn), :] = piece

    @pl.loop(0, width, unroll=2)
    def _(channel):
        for target in range(cols):
            total = None
            for col in range(cols):
                lhs = left[pl.ds(pl.multiple_of((channel * cols + col) * near * block, block), near * block), :]
                at = ((channel * cols + col) * far * near + target) * block
                rhs = right[pl.ds(pl.multiple_of(at, block), block), :].astype(jnp.bfloat16)
                part = lax.dot_general(lhs, rhs, (((1,), (1,)), ((), ())), preferred_element_type=jnp.float32)
                total = part if total is None else total + part
            total = jnp.concatenate([total, jnp.zeros((near * block, LANES - block), jnp.float32)], axis=1)
            for piece in range(near):
                groups = folds.groups
                base = piece * block
                lane_rows = folds.join(
                    [total[base + phase * groups : base + (phase + 1) * groups, :] for phase in range(folds.turn)]
                )
                out_row = (piece * cols + target) * width + channel
                for at, value in zip(lane_rows_of(folds, rows, out_row), lane_rows):
                    staged[at, :] = value

    unstage(staged, mix_ref)


def mix_in_kernel(folds, near, cols, width, half_ref, both_ref, keep_ref, send_ref, staged, left, right, turned, mixed):
    parts = near * cols
    rows = 2 * parts * width
    block = folds.rows

    stage(both_ref, staged)

    for target, shift in ((left, 0), (right, width)):

        @pl.loop(0, parts * width, unroll=8)
        def _(step):
            source, channel = step // width, step % width
            row = source * 2 * width + shift + channel
            pieces = folds.split([staged[at, :] for at in lane_rows_of(folds, rows, row)])
            at = (channel * cols + source % cols) * near * block + (source // cols) * block
            target[pl.ds(pl.multiple_of(at, block), block), :] = jnp.concatenate(pieces, axis=0).astype(jnp.bfloat16)

    out_rows = parts * width
    tall = near * block

    @pl.loop(0, width, unroll=2)
    def _(channel):
        for upper in range(cols):
            lhs = left[pl.ds(pl.multiple_of((channel * cols + upper) * tall, block), tall), :]
            for target in range(cols):
                rhs = right[pl.ds(pl.multiple_of((channel * cols + target) * tall, block), tall), :]
                turned[target] = lax.dot_general(lhs, rhs, (((0,), (0,)), ((), ())), preferred_element_type=jnp.float32)
                lane_rows = folds.join(
                    [turned[target, pl.ds(phase, folds.groups, stride=folds.turn), :] for phase in range(folds.turn)]
                )
                half, piece = divmod(upper, near)
                out_row = (piece * cols + target) * width + channel
                for at, value in zip(lane_rows_of(folds, out_rows, out_row), lane_rows):
                    mixed[half, at, :] = value

    unstage(mixed.at[half_ref[0]], keep_ref)
    unstage(mixed.at[half_ref[1]], send_ref)


SMEM_SPEC = pl.BlockSpec(memory_space=pltpu.SMEM)
VMEM_SPEC = pl.BlockSpec(memory_space=pltpu.VMEM)


def run_mix_out(folds, near, cols, halves, left, here, there):
    rows, positions = left.shape
    width = rows // (near * cols)
    block = folds.rows
    return pl.pallas_call(
        functools.partial(mix_out_kernel, folds, near, cols, width),
        in_specs=[SMEM_SPEC, VMEM_SPEC, VMEM_SPEC, VMEM_SPEC],
        out_specs=VMEM_SPEC,
        out_shape=jax.ShapeDtypeStruct((rows, positions), jnp.bfloat16),
        scratch_shapes=[
            pltpu.VMEM((rows * folds.lane_rows, LANES), jnp.float32),
            pltpu.VMEM((width * cols * near * block, LANES), jnp.bfloat16),
            pltpu.VMEM((width * cols * cols * block, LANES), jnp.float32),
        ],
        compiler_params=pltpu.CompilerParams(vmem_limit_bytes=BUDGET),
        name="mix_out",
    )(halves, left, here, there)


def run_mix_in(folds, near, cols, halves, both):
    rows, positions = both.shape
    width = rows // (2 * near * cols)
    block = folds.rows
    return pl.pallas_call(
        functools.partial(mix_in_kernel, folds, near, cols, width),
        in_specs=[SMEM_SPEC, VMEM_SPEC],
        out_specs=[VMEM_SPEC, VMEM_SPEC],
        out_shape=[
            jax.ShapeDtypeStruct((rows // 2, positions), jnp.float32),
            jax.ShapeDtypeStruct((rows // 2, positions), jnp.bfloat16),
        ],
        scratch_shapes=[
            pltpu.VMEM((rows * folds.lane_rows, LANES), jnp.float32),
            pltpu.VMEM((width * cols * near * block, LANES), jnp.bfloat16),
            pltpu.VMEM((width * cols * near * block, LANES), jnp.bfloat16),
            pltpu.VMEM((cols, LANES, LANES), jnp.float32),
            pltpu.VMEM((2, rows // 2 * folds.lane_rows, LANES), jnp.float32),
        ],
        compiler_params=pltpu.CompilerParams(vmem_limit_bytes=BUDGET),
        name="mix_in",
    )(halves, both)


PIECES = 2


def exchange(array):
    return lax.all_to_all(array, EVERY, split_axis=0, concat_axis=0, tiled=True)


def across(array):
    return lax.ppermute(array, "far", ((0, 1), (1, 0)))


def in_halves(sizes, pair_input, weights):
    _, near, cols = sizes
    row_count, col_count, features = pair_input.shape
    parts = near * cols
    width = features // parts
    pieces = PIECES
    folds = Folds(row_count, col_count)
    half = lax.axis_index("far")
    halves = jnp.stack([half, 1 - half]).astype(jnp.int32)

    def by_piece(rows):
        return rows.reshape(parts, pieces, width // pieces, -1).transpose(1, 0, 2, 3)

    def rows_of(project, order):
        ga, va, gb, vb = (by_piece(rows) for rows in jnp.split(project.T, 4, axis=0))
        return order(ga, gb).reshape(-1, features), order(va, vb).reshape(-1, features)

    def right_then_left(left, right):
        return jnp.concatenate([right, left], axis=0)

    def side_by_side(left, right):
        return jnp.concatenate([left, right], axis=2)

    def unordered(array):
        return by_piece(array.reshape(features, -1)).reshape(array.shape)

    gain_1, project_1, gate_1, norm_1, final_1, gain_2, project_2, gate_2, norm_2, final_2 = weights
    state = pair_input.reshape(-1, features)
    piece_rows = features // pieces

    gates, values = rows_of(project_1, right_then_left)
    here, there, left, mixes = [], [], [], []
    right_out = run_projections(state, gain_1, gates[:features], values[:features], (piece_rows,) * pieces)
    for piece in range(pieces):
        here.append(exchange(right_out[piece]))
        there.append(across(here[piece]))
    left_out = run_projections(state, gain_1, gates[features:], values[features:], (piece_rows,) * pieces)
    for piece in range(pieces):
        left.append(exchange(left_out[piece]))
    for piece in range(pieces):
        mixed = run_mix_out(folds, near, cols, halves, left[piece], here[piece], there[piece])
        mixes.append(exchange(mixed))
    onward = (gain_2, *rows_of(project_2, side_by_side), (2 * piece_rows,) * pieces)
    out = run_finish(mixes, state, gain_1, gate_1, unordered(norm_1), unordered(final_1), onward)
    middle, both, parted, mixes = out[0], [], [], []
    for piece in range(pieces):
        both.append(exchange(out[1 + piece]))
    for piece in range(pieces):
        kept, sent = run_mix_in(folds, near, cols, halves, both[piece])
        parted.append((kept, across(sent)))
    for kept, got in parted:
        mixed = (kept + got.astype(jnp.float32)).astype(jnp.bfloat16)
        mixes.append(exchange(mixed))
    result = run_finish(mixes, middle, gain_2, gate_2, unordered(norm_2), unordered(final_2))[0]
    return result.reshape(pair_input.shape)


def solution(mesh):
    row_parts, col_parts = mesh.shape["dap"], mesh.shape["chan"] * mesh.shape["sub"]

    def whole(pair_input, *weights):
        features = pair_input.shape[-1]
        block_rows = pair_input.shape[0] // (mesh.shape["groups"] * row_parts)
        block_cols = pair_input.shape[1] // col_parts
        halved = (
            row_parts % 2 == 0
            and row_parts == col_parts
            and block_rows == block_cols
            and Folds(block_rows, block_cols).fits()
            and features == LANES
            and features % (row_parts // 2 * col_parts * 8 * PIECES) == 0
        )
        if halved:
            far, near = 2, row_parts // 2
        else:
            far, near = split_rows(row_parts, col_parts, features, 8)
        sizes = (far, near, col_parts)
        finer = Mesh(
            mesh.devices.reshape(mesh.shape["groups"], far, near, mesh.shape["chan"], mesh.shape["sub"]),
            ("groups", "far", "near", "chan", "sub"),
        )

        def shards(pair_input, *weights):
            if halved:
                return in_halves(sizes, pair_input, weights)
            middle = update(False, sizes, pair_input, *weights[:5])
            return update(True, sizes, middle, *weights[5:])

        pair_spec = P(("groups", "far", "near"), ("chan", "sub"), None)
        mapped = jax.shard_map(
            shards,
            mesh=finer,
            in_specs=(pair_spec,) + (P(),) * 10,
            out_specs=pair_spec,
            check_vma=False,
        )
        return mapped(pair_input, *weights)

    return whole
```

```python
import functools

import jax
import jax.numpy as jnp
from jax import lax
from jax.experimental import pallas as pl
from jax.experimental.pallas import tpu as pltpu
from jax.sharding import Mesh
from jax.sharding import PartitionSpec as P


epsilon = 1e-05
EVERY = ("near", "chan", "sub")
LANES = 128
BUDGET = 56 << 20


def layer_norm(values, norm_gain, reduce_axis):
    average = jnp.mean(values, axis=reduce_axis, keepdims=True)
    centred = values - average
    variance = jnp.mean(centred * centred, axis=reduce_axis, keepdims=True)
    return centred * lax.rsqrt(variance + epsilon) * norm_gain


def sigmoid(values):
    return 0.5 * jnp.tanh(0.5 * values) + 0.5


def project_in(pair_state, norm_gain, project, gate_matrix):
    features = pair_state.shape[-1]
    flattened = pair_state.reshape(-1, features).astype(jnp.float32)
    normed = layer_norm(flattened, norm_gain, 1).astype(jnp.bfloat16)
    projected = jnp.einsum("xc,cd->dx", normed, project, preferred_element_type=jnp.float32)
    left_part = jax.nn.sigmoid(projected[:features]) * projected[features : 2 * features]
    right_part = jax.nn.sigmoid(projected[2 * features : 3 * features]) * projected[3 * features :]
    gating = jax.nn.sigmoid(jnp.dot(normed, gate_matrix, preferred_element_type=jnp.float32))
    return left_part.astype(jnp.bfloat16), right_part.astype(jnp.bfloat16), gating


def finish(pair_state, mixture, gating, out_gain, final_matrix):
    features = mixture.shape[0]
    flattened = mixture.astype(jnp.float32)
    normed = layer_norm(flattened, out_gain[:, None], 0).astype(jnp.bfloat16)
    update = jnp.einsum("cx,cd->xd", normed, final_matrix, preferred_element_type=jnp.float32)
    result = pair_state.reshape(-1, features).astype(jnp.float32) + gating * update
    return result.astype(jnp.bfloat16).reshape(pair_state.shape)


def update(incoming, sizes, pair_state, norm_gain, project, gate_matrix, out_gain, final_matrix):
    far, near, col_parts = sizes
    row_count, col_count, features = pair_state.shape
    parts = near * col_parts
    width = features // parts
    left_part, right_part, gating = project_in(pair_state, norm_gain, project, gate_matrix)
    both = jnp.stack([left_part.reshape(parts, width, -1), right_part.reshape(parts, width, -1)], axis=1)
    both = lax.all_to_all(both, EVERY, split_axis=0, concat_axis=0, tiled=True)
    both = both.reshape(near, col_parts, 2, width, row_count, col_count)
    both = both.transpose(2, 3, 0, 4, 1, 5).reshape(2, width, near * row_count, col_parts * col_count)
    left_part, right_part = both[0], both[1]
    if incoming:
        mixture = jnp.einsum("cki,ckj->cij", left_part, right_part, preferred_element_type=jnp.float32)
        if far > 1:
            mixture = lax.psum_scatter(mixture, "far", scatter_dimension=1, tiled=True)
    else:
        if far > 1:
            right_part = lax.all_gather(right_part, "far", axis=1, tiled=True)
        mixture = jnp.einsum("cik,cjk->cij", left_part, right_part, preferred_element_type=jnp.float32)
    mixture = mixture.astype(jnp.bfloat16).reshape(width, near, row_count, col_parts, col_count)
    mixture = mixture.transpose(1, 3, 0, 2, 4).reshape(parts, width, row_count * col_count)
    mixture = lax.all_to_all(mixture, EVERY, split_axis=0, concat_axis=0, tiled=True)
    return finish(pair_state, mixture.reshape(features, -1), gating, out_gain, final_matrix)


def split_rows(row_parts, col_parts, features, least):
    near = row_parts
    while near > 1 and (row_parts % near or features % (near * col_parts) or features < least * near * col_parts):
        near -= 1
    return row_parts // near, near


def emit_projections(normed, gate_rows, value_rows, out_refs):
    at = 0
    for ref in out_refs:
        parts, width, _ = ref.shape
        rows = parts * width
        gates = lax.dot_general(
            gate_rows[at : at + rows, :], normed, (((1,), (1,)), ((), ())), preferred_element_type=jnp.float32
        )
        values = lax.dot_general(
            value_rows[at : at + rows, :], normed, (((1,), (1,)), ((), ())), preferred_element_type=jnp.float32
        )
        gated = sigmoid(gates) * values
        for part in range(parts):
            ref[part] = gated[part * width : (part + 1) * width, :].astype(ref.dtype)
        at += rows


def project_kernel(state_ref, gain_ref, gate_rows, value_rows, *out_refs):
    normed = layer_norm(state_ref[...].astype(jnp.float32), gain_ref[...], 1).astype(jnp.bfloat16)
    emit_projections(normed, gate_rows, value_rows, out_refs)


def finish_kernel(pieces, onward, *refs):
    mix_refs, refs = refs[:pieces], refs[pieces:]
    state_ref, gain_ref, gate_ref, out_gain_ref, final_ref = refs[:5]
    state = state_ref[...].astype(jnp.float32)
    normed = layer_norm(state, gain_ref[...], 1).astype(jnp.bfloat16)
    gating = sigmoid(jnp.dot(normed, gate_ref[...], preferred_element_type=jnp.float32))
    mixed = jnp.concatenate(
        [ref[part].astype(jnp.float32) for ref in mix_refs for part in range(ref.shape[0])], axis=0
    )
    mixed = layer_norm(mixed, out_gain_ref[...], 0).astype(jnp.bfloat16)
    change = lax.dot_general(
        mixed, final_ref[...], (((0,), (0,)), ((), ())), preferred_element_type=jnp.float32
    )
    result = (state + gating * change).astype(jnp.bfloat16)
    if onward:
        next_gain, gate_rows, value_rows, middle_ref = refs[5:9]
        middle_ref[...] = result
        normed = layer_norm(result.astype(jnp.float32), next_gain[...], 1).astype(jnp.bfloat16)
        emit_projections(normed, gate_rows, value_rows, refs[9:])
    else:
        refs[5][...] = result


def whole_spec(array):
    return pl.BlockSpec(array.shape, lambda step: (0,) * array.ndim)


def row_step(positions):
    step = positions
    for candidate in range(LANES, 1152 + 1, LANES):
        if positions % candidate == 0:
            step = candidate
    return step


def run_projections(state, gain, gate_rows, value_rows, out_shapes):
    positions, features = state.shape
    step = row_step(positions)
    weights = (gain[None, :], gate_rows, value_rows)
    return pl.pallas_call(
        project_kernel,
        grid=(positions // step,),
        in_specs=[pl.BlockSpec((step, features), lambda i: (i, 0))] + [whole_spec(w) for w in weights],
        out_specs=[pl.BlockSpec((*shape, step), lambda i: (0, 0, i)) for shape in out_shapes],
        out_shape=[jax.ShapeDtypeStruct((*shape, positions), jnp.bfloat16) for shape in out_shapes],
        compiler_params=pltpu.CompilerParams(vmem_limit_bytes=BUDGET),
        name="project",
    )(state, *weights)


def run_finish(mixes, state, gain, gate_matrix, out_gain, final_matrix, onward=None):
    positions, features = state.shape
    step = row_step(positions)
    weights = (gain[None, :], gate_matrix, out_gain[:, None], final_matrix)
    out_shape = [jax.ShapeDtypeStruct((positions, features), jnp.bfloat16)]
    out_specs = [pl.BlockSpec((step, features), lambda i: (i, 0))]
    if onward is not None:
        next_gain, gate_rows, value_rows, out_shapes = onward
        weights += (next_gain[None, :], gate_rows, value_rows)
        out_shape += [jax.ShapeDtypeStruct((*shape, positions), jnp.bfloat16) for shape in out_shapes]
        out_specs += [pl.BlockSpec((*shape, step), lambda i: (0, 0, i)) for shape in out_shapes]
    return pl.pallas_call(
        functools.partial(finish_kernel, len(mixes), onward is not None),
        grid=(positions // step,),
        in_specs=[pl.BlockSpec((*m.shape[:2], step), lambda i: (0, 0, i)) for m in mixes]
        + [pl.BlockSpec((step, features), lambda i: (i, 0))]
        + [whole_spec(w) for w in weights],
        out_specs=out_specs,
        out_shape=out_shape,
        compiler_params=pltpu.CompilerParams(vmem_limit_bytes=BUDGET),
        name="finish",
    )(*mixes, state, *weights)


class Folds:
    def __init__(self, row_count, col_count):
        turn = 1
        while (turn * col_count) % LANES:
            turn *= 2
        self.turn, self.tiles = turn, turn * col_count // LANES
        self.cols, self.rows = col_count, row_count
        self.groups = row_count // turn
        self.lane_rows = row_count * col_count // LANES

    def fits(self):
        return self.cols <= LANES and self.rows % self.turn == 0 and self.groups % 8 == 0

    def split(self, lane_rows):
        lane = lax.broadcasted_iota(jnp.int32, lane_rows[0].shape, 1)
        out = []
        for phase in range(self.turn):
            first, offset = divmod(phase * self.cols, LANES)
            value = lane_rows[first]
            if offset + self.cols > LANES:
                value = jnp.where(lane >= offset, value, lane_rows[first + 1])
            if offset:
                value = pltpu.roll(value, LANES - offset, 1)
            out.append(jnp.where(lane < self.cols, value, 0.0))
        return out

    def join(self, block_rows):
        lane = lax.broadcasted_iota(jnp.int32, block_rows[0].shape, 1)
        rolled = []
        for phase, value in enumerate(block_rows):
            offset = (phase * self.cols) % LANES
            rolled.append(pltpu.roll(value, offset, 1) if offset else value)
        out = []
        for tile in range(self.tiles):
            value = None
            for phase in range(self.turn):
                begin, end = phase * self.cols - tile * LANES, (phase + 1) * self.cols - tile * LANES
                if end <= 0 or begin >= LANES:
                    continue
                value = rolled[phase] if value is None else jnp.where(lane >= begin, rolled[phase], value)
            out.append(value)
        return out


def stage(source_ref, staged, shift=0, width=None):
    parts, held, positions = source_ref.shape
    width = width or held
    rows = parts * width
    for part in range(parts):
        values = source_ref[part].astype(jnp.float32)[shift : shift + width, :]
        for tile in range(positions // LANES):
            at = tile * rows + part * width
            staged[at : at + width, :] = values[:, tile * LANES : (tile + 1) * LANES]


def unstage(staged, target_ref):
    parts, width, positions = target_ref.shape
    rows = parts * width
    for tile in range(positions // LANES):
        for part in range(parts):
            at = tile * rows + part * width
            target_ref[part, :, tile * LANES : (tile + 1) * LANES] = staged[at : at + width, :].astype(
                target_ref.dtype
            )


def lane_rows_of(folds, rows, row):
    return [pl.ds(row + tile * rows, folds.groups, stride=folds.tiles * rows) for tile in range(folds.tiles)]


def mix_out_kernel(folds, near, cols, width, shift, half_ref, left_ref, here_ref, there_ref, mix_ref, staged, left, right):
    parts = near * cols
    rows = parts * width
    block = folds.rows
    far = cols // near

    stage(left_ref, staged, shift * width, width)

    @pl.loop(0, rows, unroll=8)
    def _(row):
        pieces = folds.split([staged[at, :] for at in lane_rows_of(folds, rows, row)])
        source, channel = row // width, row % width
        at = (channel * cols + source % cols) * near * block + (source // cols) * block
        left[pl.ds(pl.multiple_of(at, block), block), :] = jnp.concatenate(pieces, axis=0).astype(jnp.bfloat16)

    for which, ref in ((0, here_ref), (1, there_ref)):
        stage(ref, staged)
        half = half_ref[which]

        @pl.loop(0, rows, unroll=8)
        def _(row):
            pieces = folds.split([staged[at, :] for at in lane_rows_of(folds, rows, row)])
            source, channel = row // width, row % width
            at = ((channel * cols + source % cols) * far + half) * near * block + (source // cols) * block
            for phase, piece in enumerate(pieces):
                right[pl.ds(at + phase, folds.groups, stride=folds.turn), :] = piece

    @pl.loop(0, width, unroll=2)
    def _(channel):
        for target in range(cols):
            total = None
            for col in range(cols):
                lhs = left[pl.ds(pl.multiple_of((channel * cols + col) * near * block, block), near * block), :]
                at = ((channel * cols + col) * far * near + target) * block
                rhs = right[pl.ds(pl.multiple_of(at, block), block), :].astype(jnp.bfloat16)
                part = lax.dot_general(lhs, rhs, (((1,), (1,)), ((), ())), preferred_element_type=jnp.float32)
                total = part if total is None else total + part
            total = jnp.concatenate([total, jnp.zeros((near * block, LANES - block), jnp.float32)], axis=1)
            for piece in range(near):
                groups = folds.groups
                base = piece * block
                lane_rows = folds.join(
                    [total[base + phase * groups : base + (phase + 1) * groups, :] for phase in range(folds.turn)]
                )
                out_row = (piece * cols + target) * width + channel
                for at, value in zip(lane_rows_of(folds, rows, out_row), lane_rows):
                    staged[at, :] = value

    unstage(staged, mix_ref)


def mix_in_kernel(folds, near, cols, width, half_ref, both_ref, keep_ref, send_ref, staged, left, right, turned, mixed):
    parts = near * cols
    rows = 2 * parts * width
    block = folds.rows

    stage(both_ref, staged)

    for target, shift in ((left, 0), (right, width)):

        @pl.loop(0, parts * width, unroll=8)
        def _(step):
            source, channel = step // width, step % width
            row = source * 2 * width + shift + channel
            pieces = folds.split([staged[at, :] for at in lane_rows_of(folds, rows, row)])
            at = (channel * cols + source % cols) * near * block + (source // cols) * block
            target[pl.ds(pl.multiple_of(at, block), block), :] = jnp.concatenate(pieces, axis=0).astype(jnp.bfloat16)

    out_rows = parts * width
    tall = near * block

    @pl.loop(0, width, unroll=2)
    def _(channel):
        for upper in range(cols):
            lhs = left[pl.ds(pl.multiple_of((channel * cols + upper) * tall, block), tall), :]
            for target in range(cols):
                rhs = right[pl.ds(pl.multiple_of((channel * cols + target) * tall, block), tall), :]
                turned[target] = lax.dot_general(lhs, rhs, (((0,), (0,)), ((), ())), preferred_element_type=jnp.float32)
                lane_rows = folds.join(
                    [turned[target, pl.ds(phase, folds.groups, stride=folds.turn), :] for phase in range(folds.turn)]
                )
                half, piece = divmod(upper, near)
                out_row = (piece * cols + target) * width + channel
                for at, value in zip(lane_rows_of(folds, out_rows, out_row), lane_rows):
                    mixed[half, at, :] = value

    unstage(mixed.at[half_ref[0]], keep_ref)
    unstage(mixed.at[half_ref[1]], send_ref)


SMEM_SPEC = pl.BlockSpec(memory_space=pltpu.SMEM)
VMEM_SPEC = pl.BlockSpec(memory_space=pltpu.VMEM)


def run_mix_out(folds, near, cols, halves, left, here, there, shift):
    parts, width, _ = here.shape
    rows = parts * width
    block = folds.rows
    return pl.pallas_call(
        functools.partial(mix_out_kernel, folds, near, cols, width, shift),
        in_specs=[SMEM_SPEC, VMEM_SPEC, VMEM_SPEC, VMEM_SPEC],
        out_specs=VMEM_SPEC,
        out_shape=jax.ShapeDtypeStruct(here.shape, jnp.bfloat16),
        scratch_shapes=[
            pltpu.VMEM((rows * folds.lane_rows, LANES), jnp.float32),
            pltpu.VMEM((width * cols * near * block, LANES), jnp.bfloat16),
            pltpu.VMEM((width * cols * cols * block, LANES), jnp.float32),
        ],
        compiler_params=pltpu.CompilerParams(vmem_limit_bytes=BUDGET),
        name="mix_out",
    )(halves, left, here, there)


def run_mix_in(folds, near, cols, halves, both):
    parts, width, positions = both.shape
    rows, width = parts * width, width // 2
    block = folds.rows
    return pl.pallas_call(
        functools.partial(mix_in_kernel, folds, near, cols, width),
        in_specs=[SMEM_SPEC, VMEM_SPEC],
        out_specs=[VMEM_SPEC, VMEM_SPEC],
        out_shape=[
            jax.ShapeDtypeStruct((parts, width, positions), jnp.float32),
            jax.ShapeDtypeStruct((parts, width, positions), jnp.bfloat16),
        ],
        scratch_shapes=[
            pltpu.VMEM((rows * folds.lane_rows, LANES), jnp.float32),
            pltpu.VMEM((width * cols * near * block, LANES), jnp.bfloat16),
            pltpu.VMEM((width * cols * near * block, LANES), jnp.bfloat16),
            pltpu.VMEM((cols, LANES, LANES), jnp.float32),
            pltpu.VMEM((2, rows // 2 * folds.lane_rows, LANES), jnp.float32),
        ],
        compiler_params=pltpu.CompilerParams(vmem_limit_bytes=BUDGET),
        name="mix_in",
    )(halves, both)


PIECES = 4


def exchange(array):
    return lax.all_to_all(array, EVERY, split_axis=0, concat_axis=0, tiled=True)


def across(array):
    return lax.ppermute(array, "far", ((0, 1), (1, 0)))


def in_halves(sizes, pair_input, weights):
    _, near, cols = sizes
    row_count, col_count, features = pair_input.shape
    parts = near * cols
    width = features // parts
    pieces = PIECES
    folds = Folds(row_count, col_count)
    half = lax.axis_index("far")
    halves = jnp.stack([half, 1 - half]).astype(jnp.int32)

    def by_piece(rows):
        return rows.reshape(parts, pieces, width // pieces, -1).transpose(1, 0, 2, 3)

    def rows_of(project, order):
        ga, va, gb, vb = (by_piece(rows) for rows in jnp.split(project.T, 4, axis=0))
        return order(ga, gb).reshape(-1, features), order(va, vb).reshape(-1, features)

    def right_then_left(left, right):
        paired = left.reshape(pieces // 2, 2, *left.shape[1:]).transpose(0, 2, 1, 3, 4)
        return jnp.concatenate([right.reshape(-1, features), paired.reshape(-1, features)], axis=0)

    def side_by_side(left, right):
        return jnp.concatenate([left, right], axis=2)

    def unordered(array):
        return by_piece(array.reshape(features, -1)).reshape(array.shape)

    gain_1, project_1, gate_1, norm_1, final_1, gain_2, project_2, gate_2, norm_2, final_2 = weights
    state = pair_input.reshape(-1, features)
    piece_width = width // pieces

    gates, values = rows_of(project_1, right_then_left)
    here, there, left, mixes = [], [], [], []
    out = run_projections(
        state, gain_1, gates, values, ((parts, piece_width),) * pieces + ((parts, 2 * piece_width),) * (pieces // 2)
    )
    for piece in range(pieces):
        here.append(exchange(out[piece]))
        there.append(across(here[piece]))
    for pair in range(pieces // 2):
        left.append(exchange(out[pieces + pair]))
    for piece in range(pieces):
        mixed = run_mix_out(folds, near, cols, halves, left[piece // 2], here[piece], there[piece], piece % 2)
        mixes.append(exchange(mixed))
    onward = (gain_2, *rows_of(project_2, side_by_side), ((parts, 2 * piece_width),) * pieces)
    out = run_finish(mixes, state, gain_1, gate_1, unordered(norm_1), unordered(final_1), onward)
    middle, both, parted, mixes = out[0], [], [], []
    for piece in range(pieces):
        both.append(exchange(out[1 + piece]))
    for piece in range(pieces):
        kept, sent = run_mix_in(folds, near, cols, halves, both[piece])
        parted.append((kept, across(sent)))
    for kept, got in parted:
        mixed = (kept + got.astype(jnp.float32)).astype(jnp.bfloat16)
        mixes.append(exchange(mixed))
    result = run_finish(mixes, middle, gain_2, gate_2, unordered(norm_2), unordered(final_2))[0]
    return result.reshape(pair_input.shape)


def solution(mesh):
    row_parts, col_parts = mesh.shape["dap"], mesh.shape["chan"] * mesh.shape["sub"]

    def whole(pair_input, *weights):
        features = pair_input.shape[-1]
        block_rows = pair_input.shape[0] // (mesh.shape["groups"] * row_parts)
        block_cols = pair_input.shape[1] // col_parts
        halved = (
            row_parts % 2 == 0
            and row_parts == col_parts
            and block_rows == block_cols
            and Folds(block_rows, block_cols).fits()
            and features == LANES
            and features % (row_parts // 2 * col_parts * PIECES) == 0
        )
        if halved:
            far, near = 2, row_parts // 2
        else:
            far, near = split_rows(row_parts, col_parts, features, 8)
        sizes = (far, near, col_parts)
        finer = Mesh(
            mesh.devices.reshape(mesh.shape["groups"], far, near, mesh.shape["chan"], mesh.shape["sub"]),
            ("groups", "far", "near", "chan", "sub"),
        )

        def shards(pair_input, *weights):
            if halved:
                return in_halves(sizes, pair_input, weights)
            middle = update(False, sizes, pair_input, *weights[:5])
            return update(True, sizes, middle, *weights[5:])

        pair_spec = P(("groups", "far", "near"), ("chan", "sub"), None)
        mapped = jax.shard_map(
            shards,
            mesh=finer,
            in_specs=(pair_spec,) + (P(),) * 10,
            out_specs=pair_spec,
            check_vma=False,
        )
        return mapped(pair_input, *weights)

    return whole
```

```python
import functools

import jax
import jax.numpy as jnp
from jax import lax
from jax.experimental import pallas as pl
from jax.experimental.pallas import tpu as pltpu
from jax.sharding import Mesh
from jax.sharding import PartitionSpec as P


epsilon = 1e-05
EVERY = ("near", "chan", "sub")
LANES = 128
BUDGET = 56 << 20


def layer_norm(values, norm_gain, reduce_axis):
    average = jnp.mean(values, axis=reduce_axis, keepdims=True)
    centred = values - average
    variance = jnp.mean(centred * centred, axis=reduce_axis, keepdims=True)
    return centred * lax.rsqrt(variance + epsilon) * norm_gain


def sigmoid(values):
    return 0.5 * jnp.tanh(0.5 * values) + 0.5


def project_in(pair_state, norm_gain, project, gate_matrix):
    features = pair_state.shape[-1]
    flattened = pair_state.reshape(-1, features).astype(jnp.float32)
    normed = layer_norm(flattened, norm_gain, 1).astype(jnp.bfloat16)
    projected = jnp.einsum("xc,cd->dx", normed, project, preferred_element_type=jnp.float32)
    left_part = jax.nn.sigmoid(projected[:features]) * projected[features : 2 * features]
    right_part = jax.nn.sigmoid(projected[2 * features : 3 * features]) * projected[3 * features :]
    gating = jax.nn.sigmoid(jnp.dot(normed, gate_matrix, preferred_element_type=jnp.float32))
    return left_part.astype(jnp.bfloat16), right_part.astype(jnp.bfloat16), gating


def finish(pair_state, mixture, gating, out_gain, final_matrix):
    features = mixture.shape[0]
    flattened = mixture.astype(jnp.float32)
    normed = layer_norm(flattened, out_gain[:, None], 0).astype(jnp.bfloat16)
    update = jnp.einsum("cx,cd->xd", normed, final_matrix, preferred_element_type=jnp.float32)
    result = pair_state.reshape(-1, features).astype(jnp.float32) + gating * update
    return result.astype(jnp.bfloat16).reshape(pair_state.shape)


def update(incoming, sizes, pair_state, norm_gain, project, gate_matrix, out_gain, final_matrix):
    far, near, col_parts = sizes
    row_count, col_count, features = pair_state.shape
    parts = near * col_parts
    width = features // parts
    left_part, right_part, gating = project_in(pair_state, norm_gain, project, gate_matrix)
    both = jnp.stack([left_part.reshape(parts, width, -1), right_part.reshape(parts, width, -1)], axis=1)
    both = lax.all_to_all(both, EVERY, split_axis=0, concat_axis=0, tiled=True)
    both = both.reshape(near, col_parts, 2, width, row_count, col_count)
    both = both.transpose(2, 3, 0, 4, 1, 5).reshape(2, width, near * row_count, col_parts * col_count)
    left_part, right_part = both[0], both[1]
    if incoming:
        mixture = jnp.einsum("cki,ckj->cij", left_part, right_part, preferred_element_type=jnp.float32)
        if far > 1:
            mixture = lax.psum_scatter(mixture, "far", scatter_dimension=1, tiled=True)
    else:
        if far > 1:
            right_part = lax.all_gather(right_part, "far", axis=1, tiled=True)
        mixture = jnp.einsum("cik,cjk->cij", left_part, right_part, preferred_element_type=jnp.float32)
    mixture = mixture.astype(jnp.bfloat16).reshape(width, near, row_count, col_parts, col_count)
    mixture = mixture.transpose(1, 3, 0, 2, 4).reshape(parts, width, row_count * col_count)
    mixture = lax.all_to_all(mixture, EVERY, split_axis=0, concat_axis=0, tiled=True)
    return finish(pair_state, mixture.reshape(features, -1), gating, out_gain, final_matrix)


def split_rows(row_parts, col_parts, features, least):
    near = row_parts
    while near > 1 and (row_parts % near or features % (near * col_parts) or features < least * near * col_parts):
        near -= 1
    return row_parts // near, near


def emit_projections(normed, rows_ref, out_refs):
    step = normed.shape[0]
    half = rows_ref.shape[0] // 2
    group = 256 if step % 256 == 0 else LANES
    for begin in range(0, step, group):
        projected = lax.dot_general(
            rows_ref[...], normed[begin : begin + group, :], (((1,), (1,)), ((), ())), preferred_element_type=jnp.float32
        )
        gated = sigmoid(projected[:half, :]) * projected[half:, :]
        at = 0
        for ref in out_refs:
            parts, width, _ = ref.shape
            for part in range(parts):
                ref[part, :, begin : begin + group] = gated[at : at + width, :].astype(ref.dtype)
                at += width


def project_kernel(state_ref, gain_ref, rows_ref, *out_refs):
    normed = layer_norm(state_ref[...].astype(jnp.float32), gain_ref[...], 1).astype(jnp.bfloat16)
    emit_projections(normed, rows_ref, out_refs)


def finish_kernel(pieces, onward, *refs):
    mix_refs, refs = refs[:pieces], refs[pieces:]
    state_ref, gain_ref, gate_ref, out_gain_ref, final_ref = refs[:5]
    state = state_ref[...].astype(jnp.float32)
    normed = layer_norm(state, gain_ref[...], 1).astype(jnp.bfloat16)
    gating = sigmoid(jnp.dot(normed, gate_ref[...], preferred_element_type=jnp.float32))
    mixed = jnp.concatenate(
        [ref[part].astype(jnp.float32) for ref in mix_refs for part in range(ref.shape[0])], axis=0
    )
    mixed = layer_norm(mixed, out_gain_ref[...], 0).astype(jnp.bfloat16)
    change = lax.dot_general(
        mixed, final_ref[...], (((0,), (0,)), ((), ())), preferred_element_type=jnp.float32
    )
    result = (state + gating * change).astype(jnp.bfloat16)
    if onward:
        next_gain, rows_ref, middle_ref = refs[5:8]
        middle_ref[...] = result
        normed = layer_norm(result.astype(jnp.float32), next_gain[...], 1).astype(jnp.bfloat16)
        emit_projections(normed, rows_ref, refs[8:])
    else:
        refs[5][...] = result


def whole_spec(array):
    return pl.BlockSpec(array.shape, lambda step: (0,) * array.ndim)


def row_step(positions):
    step = positions
    for candidate in range(LANES, 2304 + 1, LANES):
        if positions % candidate == 0:
            step = candidate
    return step


def run_projections(state, gain, rows, out_shapes):
    positions, features = state.shape
    step = row_step(positions)
    weights = (gain[None, :], rows)
    return pl.pallas_call(
        project_kernel,
        grid=(positions // step,),
        in_specs=[pl.BlockSpec((step, features), lambda i: (i, 0))] + [whole_spec(w) for w in weights],
        out_specs=[pl.BlockSpec((*shape, step), lambda i: (0, 0, i)) for shape in out_shapes],
        out_shape=[jax.ShapeDtypeStruct((*shape, positions), jnp.bfloat16) for shape in out_shapes],
        compiler_params=pltpu.CompilerParams(vmem_limit_bytes=BUDGET),
        name="project",
    )(state, *weights)


def run_finish(mixes, state, gain, gate_matrix, out_gain, final_matrix, onward=None):
    positions, features = state.shape
    step = row_step(positions)
    weights = (gain[None, :], gate_matrix, out_gain[:, None], final_matrix)
    out_shape = [jax.ShapeDtypeStruct((positions, features), jnp.bfloat16)]
    out_specs = [pl.BlockSpec((step, features), lambda i: (i, 0))]
    if onward is not None:
        next_gain, rows, out_shapes = onward
        weights += (next_gain[None, :], rows)
        out_shape += [jax.ShapeDtypeStruct((*shape, positions), jnp.bfloat16) for shape in out_shapes]
        out_specs += [pl.BlockSpec((*shape, step), lambda i: (0, 0, i)) for shape in out_shapes]
    return pl.pallas_call(
        functools.partial(finish_kernel, len(mixes), onward is not None),
        grid=(positions // step,),
        in_specs=[pl.BlockSpec((*m.shape[:2], step), lambda i: (0, 0, i)) for m in mixes]
        + [pl.BlockSpec((step, features), lambda i: (i, 0))]
        + [whole_spec(w) for w in weights],
        out_specs=out_specs,
        out_shape=out_shape,
        compiler_params=pltpu.CompilerParams(vmem_limit_bytes=BUDGET),
        name="finish",
    )(*mixes, state, *weights)


class Folds:
    def __init__(self, row_count, col_count):
        turn = 1
        while (turn * col_count) % LANES:
            turn *= 2
        self.turn, self.tiles = turn, turn * col_count // LANES
        self.cols, self.rows = col_count, row_count
        self.groups = row_count // turn
        self.lane_rows = row_count * col_count // LANES

    def fits(self):
        return self.cols <= LANES and self.rows % self.turn == 0 and self.groups % 8 == 0

    def split(self, lane_rows, clear=False):
        lane = lax.broadcasted_iota(jnp.int32, lane_rows[0].shape, 1)
        out = []
        for phase in range(self.turn):
            first, offset = divmod(phase * self.cols, LANES)
            value = lane_rows[first]
            if offset + self.cols > LANES:
                value = jnp.where(lane >= offset, value, lane_rows[first + 1])
            if offset:
                value = pltpu.roll(value, LANES - offset, 1)
            out.append(jnp.where(lane < self.cols, value, 0.0) if clear else value)
        return out

    def join(self, block_rows):
        lane = lax.broadcasted_iota(jnp.int32, block_rows[0].shape, 1)
        rolled = []
        for phase, value in enumerate(block_rows):
            offset = (phase * self.cols) % LANES
            rolled.append(pltpu.roll(value, offset, 1) if offset else value)
        out = []
        for tile in range(self.tiles):
            value = None
            for phase in range(self.turn):
                begin, end = phase * self.cols - tile * LANES, (phase + 1) * self.cols - tile * LANES
                if end <= 0 or begin >= LANES:
                    continue
                value = rolled[phase] if value is None else jnp.where(lane >= begin, rolled[phase], value)
            out.append(value)
        return out


def stage(source_ref, staged, shift=0, width=None):
    parts, held, positions = source_ref.shape
    width = width or held
    rows = parts * width
    for part in range(parts):
        values = source_ref[part].astype(jnp.float32)[shift : shift + width, :]
        for tile in range(positions // LANES):
            at = tile * rows + part * width
            staged[at : at + width, :] = values[:, tile * LANES : (tile + 1) * LANES]


def unstage(staged, target_ref):
    parts, width, positions = target_ref.shape
    rows = parts * width
    for tile in range(positions // LANES):
        for part in range(parts):
            at = tile * rows + part * width
            target_ref[part, :, tile * LANES : (tile + 1) * LANES] = staged[at : at + width, :].astype(
                target_ref.dtype
            )


def lane_rows_of(folds, rows, row):
    return [pl.ds(row + tile * rows, folds.groups, stride=folds.tiles * rows) for tile in range(folds.tiles)]


def mix_out_kernel(folds, near, cols, width, half_ref, both_ref, there_ref, mix_ref, staged, left, right):
    parts = near * cols
    rows = parts * width
    block = folds.rows
    far = cols // near

    stage(both_ref, staged, 0, width)

    @pl.loop(0, rows, unroll=8)
    def _(row):
        pieces = folds.split([staged[at, :] for at in lane_rows_of(folds, rows, row)], clear=True)
        source, channel = row // width, row % width
        at = (channel * cols + source % cols) * near * block + (source // cols) * block
        left[pl.ds(pl.multiple_of(at, block), block), :] = jnp.concatenate(pieces, axis=0).astype(jnp.bfloat16)

    for which, ref, shift in ((0, both_ref, width), (1, there_ref, 0)):
        stage(ref, staged, shift, width)
        half = half_ref[which]

        @pl.loop(0, rows, unroll=8)
        def _(row):
            pieces = folds.split([staged[at, :] for at in lane_rows_of(folds, rows, row)])
            source, channel = row // width, row % width
            at = ((channel * cols + source % cols) * far + half) * near * block + (source // cols) * block
            for phase, piece in enumerate(pieces):
                right[pl.ds(at + phase, folds.groups, stride=folds.turn), :] = piece

    @pl.loop(0, width, unroll=1)
    def _(channel):
        tall = near * block
        lhs = jnp.concatenate(
            [left[pl.ds(pl.multiple_of((channel * cols + col) * tall, block), tall), :] for col in range(cols)], axis=1
        )
        for target in range(cols):
            starts = [((channel * cols + col) * far * near + target) * block for col in range(cols)]
            rhs = jnp.concatenate([right[pl.ds(pl.multiple_of(at, block), block), :] for at in starts], axis=1)
            total = lax.dot_general(
                lhs, rhs.astype(jnp.bfloat16), (((1,), (1,)), ((), ())), preferred_element_type=jnp.float32
            )
            total = jnp.concatenate([total, jnp.zeros((near * block, LANES - block), jnp.float32)], axis=1)
            for piece in range(near):
                groups = folds.groups
                base = piece * block
                lane_rows = folds.join(
                    [total[base + phase * groups : base + (phase + 1) * groups, :] for phase in range(folds.turn)]
                )
                out_row = (piece * cols + target) * width + channel
                for at, value in zip(lane_rows_of(folds, rows, out_row), lane_rows):
                    staged[at, :] = value

    unstage(staged, mix_ref)


def mix_in_kernel(folds, near, cols, width, half_ref, both_ref, keep_ref, send_ref, staged, left, right, turned, mixed):
    parts = near * cols
    rows = 2 * parts * width
    block = folds.rows

    stage(both_ref, staged)

    for target, shift in ((left, 0), (right, width)):

        @pl.loop(0, parts * width, unroll=8)
        def _(step):
            source, channel = step // width, step % width
            row = source * 2 * width + shift + channel
            pieces = folds.split([staged[at, :] for at in lane_rows_of(folds, rows, row)])
            at = (channel * cols + source % cols) * near * block + (source // cols) * block
            target[pl.ds(pl.multiple_of(at, block), block), :] = jnp.concatenate(pieces, axis=0).astype(jnp.bfloat16)

    out_rows = parts * width
    tall = near * block

    @pl.loop(0, width, unroll=1)
    def _(channel):
        rhs = jnp.concatenate(
            [right[pl.ds(pl.multiple_of((channel * cols + col) * tall, block), tall), :] for col in range(cols)], axis=1
        )
        for upper in range(cols):
            lhs = left[pl.ds(pl.multiple_of((channel * cols + upper) * tall, block), tall), :]
            summed = lax.dot_general(lhs, rhs, (((0,), (0,)), ((), ())), preferred_element_type=jnp.float32)
            half, piece = divmod(upper, near)
            for target in range(cols):
                turned[upper, target] = summed[:, target * LANES : (target + 1) * LANES]
                lane_rows = folds.join(
                    [turned[upper, target, pl.ds(phase, folds.groups, stride=folds.turn), :] for phase in range(folds.turn)]
                )
                out_row = (piece * cols + target) * width + channel
                for at, value in zip(lane_rows_of(folds, out_rows, out_row), lane_rows):
                    mixed[half, at, :] = value

    unstage(mixed.at[half_ref[0]], keep_ref)
    unstage(mixed.at[half_ref[1]], send_ref)


SMEM_SPEC = pl.BlockSpec(memory_space=pltpu.SMEM)
VMEM_SPEC = pl.BlockSpec(memory_space=pltpu.VMEM)


def run_mix_out(folds, near, cols, halves, both, there):
    parts, width, _ = there.shape
    rows = parts * width
    block = folds.rows
    return pl.pallas_call(
        functools.partial(mix_out_kernel, folds, near, cols, width),
        in_specs=[SMEM_SPEC, VMEM_SPEC, VMEM_SPEC],
        out_specs=VMEM_SPEC,
        out_shape=jax.ShapeDtypeStruct(there.shape, jnp.bfloat16),
        scratch_shapes=[
            pltpu.VMEM((rows * folds.lane_rows, LANES), jnp.float32),
            pltpu.VMEM((width * cols * near * block, LANES), jnp.bfloat16),
            pltpu.VMEM((width * cols * cols * block, LANES), jnp.float32),
        ],
        compiler_params=pltpu.CompilerParams(vmem_limit_bytes=BUDGET),
        name="mix_out",
    )(halves, both, there)


def run_mix_in(folds, near, cols, halves, both):
    parts, width, positions = both.shape
    rows, width = parts * width, width // 2
    block = folds.rows
    return pl.pallas_call(
        functools.partial(mix_in_kernel, folds, near, cols, width),
        in_specs=[SMEM_SPEC, VMEM_SPEC],
        out_specs=[VMEM_SPEC, VMEM_SPEC],
        out_shape=[
            jax.ShapeDtypeStruct((parts, width, positions), jnp.float32),
            jax.ShapeDtypeStruct((parts, width, positions), jnp.bfloat16),
        ],
        scratch_shapes=[
            pltpu.VMEM((rows * folds.lane_rows, LANES), jnp.float32),
            pltpu.VMEM((width * cols * near * block, LANES), jnp.bfloat16),
            pltpu.VMEM((width * cols * near * block, LANES), jnp.bfloat16),
            pltpu.VMEM((cols, cols, LANES, LANES), jnp.float32),
            pltpu.VMEM((2, rows // 2 * folds.lane_rows, LANES), jnp.float32),
        ],
        compiler_params=pltpu.CompilerParams(vmem_limit_bytes=BUDGET),
        name="mix_in",
    )(halves, both)


PIECES = 4


def exchange(array):
    return lax.all_to_all(array, EVERY, split_axis=0, concat_axis=0, tiled=True)


def across(array):
    return lax.ppermute(array, "far", ((0, 1), (1, 0)))


def in_halves(sizes, pair_input, weights):
    _, near, cols = sizes
    row_count, col_count, features = pair_input.shape
    parts = near * cols
    width = features // parts
    pieces = PIECES
    folds = Folds(row_count, col_count)
    half = lax.axis_index("far")
    halves = jnp.stack([half, 1 - half]).astype(jnp.int32)

    def by_piece(rows):
        return rows.reshape(parts, pieces, width // pieces, -1).transpose(1, 0, 2, 3)

    def rows_of(project, order):
        ga, va, gb, vb = (by_piece(rows) for rows in jnp.split(project.T, 4, axis=0))
        return jnp.concatenate([order(ga, gb).reshape(-1, features), order(va, vb).reshape(-1, features)])

    def side_by_side(left, right):
        return jnp.concatenate([left, right], axis=2)

    def unordered(array):
        return by_piece(array.reshape(features, -1)).reshape(array.shape)

    gain_1, project_1, gate_1, norm_1, final_1, gain_2, project_2, gate_2, norm_2, final_2 = weights
    state = pair_input.reshape(-1, features)
    piece_width = width // pieces

    shapes = ((parts, 2 * piece_width),) * pieces
    both, mixes = [], []
    out = run_projections(state, gain_1, rows_of(project_1, side_by_side), shapes)
    for piece in range(pieces):
        both.append(exchange(out[piece]))
    for piece in range(pieces):
        there = across(both[piece][:, piece_width:, :])
        mixed = run_mix_out(folds, near, cols, halves, both[piece], there)
        mixes.append(exchange(mixed))
    onward = (gain_2, rows_of(project_2, side_by_side), shapes)
    out = run_finish(mixes, state, gain_1, gate_1, unordered(norm_1), unordered(final_1), onward)
    middle, both, parted, mixes = out[0], [], [], []
    for piece in range(pieces):
        both.append(exchange(out[1 + piece]))
    for piece in range(pieces):
        kept, sent = run_mix_in(folds, near, cols, halves, both[piece])
        parted.append((kept, across(sent)))
    for kept, got in parted:
        mixed = (kept + got.astype(jnp.float32)).astype(jnp.bfloat16)
        mixes.append(exchange(mixed))
    result = run_finish(mixes, middle, gain_2, gate_2, unordered(norm_2), unordered(final_2))[0]
    return result.reshape(pair_input.shape)


def solution(mesh):
    row_parts, col_parts = mesh.shape["dap"], mesh.shape["chan"] * mesh.shape["sub"]

    def whole(pair_input, *weights):
        features = pair_input.shape[-1]
        block_rows = pair_input.shape[0] // (mesh.shape["groups"] * row_parts)
        block_cols = pair_input.shape[1] // col_parts
        halved = (
            row_parts % 2 == 0
            and row_parts == col_parts
            and block_rows == block_cols
            and Folds(block_rows, block_cols).fits()
            and features == LANES
            and features % (row_parts // 2 * col_parts * PIECES) == 0
        )
        if halved:
            far, near = 2, row_parts // 2
        else:
            far, near = split_rows(row_parts, col_parts, features, 8)
        sizes = (far, near, col_parts)
        finer = Mesh(
            mesh.devices.reshape(mesh.shape["groups"], far, near, mesh.shape["chan"], mesh.shape["sub"]),
            ("groups", "far", "near", "chan", "sub"),
        )

        def shards(pair_input, *weights):
            if halved:
                return in_halves(sizes, pair_input, weights)
            middle = update(False, sizes, pair_input, *weights[:5])
            return update(True, sizes, middle, *weights[5:])

        pair_spec = P(("groups", "far", "near"), ("chan", "sub"), None)
        mapped = jax.shard_map(
            shards,
            mesh=finer,
            in_specs=(pair_spec,) + (P(),) * 10,
            out_specs=pair_spec,
            check_vma=False,
        )
        return mapped(pair_input, *weights)

    return whole
```

```python
import functools

import jax
import jax.numpy as jnp
from jax import lax
from jax.experimental import pallas as pl
from jax.experimental.pallas import tpu as pltpu
from jax.sharding import Mesh
from jax.sharding import PartitionSpec as P


epsilon = 1e-05
EVERY = ("near", "chan", "sub")
LANES = 128
BUDGET = 56 << 20


def layer_norm(values, norm_gain, reduce_axis):
    average = jnp.mean(values, axis=reduce_axis, keepdims=True)
    centred = values - average
    variance = jnp.mean(centred * centred, axis=reduce_axis, keepdims=True)
    return centred * lax.rsqrt(variance + epsilon) * norm_gain


def sigmoid(values):
    return 0.5 * jnp.tanh(0.5 * values) + 0.5


def project_in(pair_state, norm_gain, project, gate_matrix):
    features = pair_state.shape[-1]
    flattened = pair_state.reshape(-1, features).astype(jnp.float32)
    normed = layer_norm(flattened, norm_gain, 1).astype(jnp.bfloat16)
    projected = jnp.einsum("xc,cd->dx", normed, project, preferred_element_type=jnp.float32)
    left_part = jax.nn.sigmoid(projected[:features]) * projected[features : 2 * features]
    right_part = jax.nn.sigmoid(projected[2 * features : 3 * features]) * projected[3 * features :]
    gating = jax.nn.sigmoid(jnp.dot(normed, gate_matrix, preferred_element_type=jnp.float32))
    return left_part.astype(jnp.bfloat16), right_part.astype(jnp.bfloat16), gating


def finish(pair_state, mixture, gating, out_gain, final_matrix):
    features = mixture.shape[0]
    flattened = mixture.astype(jnp.float32)
    normed = layer_norm(flattened, out_gain[:, None], 0).astype(jnp.bfloat16)
    update = jnp.einsum("cx,cd->xd", normed, final_matrix, preferred_element_type=jnp.float32)
    result = pair_state.reshape(-1, features).astype(jnp.float32) + gating * update
    return result.astype(jnp.bfloat16).reshape(pair_state.shape)


def update(incoming, sizes, pair_state, norm_gain, project, gate_matrix, out_gain, final_matrix):
    far, near, col_parts = sizes
    row_count, col_count, features = pair_state.shape
    parts = near * col_parts
    width = features // parts
    left_part, right_part, gating = project_in(pair_state, norm_gain, project, gate_matrix)
    both = jnp.stack([left_part.reshape(parts, width, -1), right_part.reshape(parts, width, -1)], axis=1)
    both = lax.all_to_all(both, EVERY, split_axis=0, concat_axis=0, tiled=True)
    both = both.reshape(near, col_parts, 2, width, row_count, col_count)
    both = both.transpose(2, 3, 0, 4, 1, 5).reshape(2, width, near * row_count, col_parts * col_count)
    left_part, right_part = both[0], both[1]
    if incoming:
        mixture = jnp.einsum("cki,ckj->cij", left_part, right_part, preferred_element_type=jnp.float32)
        if far > 1:
            mixture = lax.psum_scatter(mixture, "far", scatter_dimension=1, tiled=True)
    else:
        if far > 1:
            right_part = lax.all_gather(right_part, "far", axis=1, tiled=True)
        mixture = jnp.einsum("cik,cjk->cij", left_part, right_part, preferred_element_type=jnp.float32)
    mixture = mixture.astype(jnp.bfloat16).reshape(width, near, row_count, col_parts, col_count)
    mixture = mixture.transpose(1, 3, 0, 2, 4).reshape(parts, width, row_count * col_count)
    mixture = lax.all_to_all(mixture, EVERY, split_axis=0, concat_axis=0, tiled=True)
    return finish(pair_state, mixture.reshape(features, -1), gating, out_gain, final_matrix)


def split_rows(row_parts, col_parts, features, least):
    near = row_parts
    while near > 1 and (row_parts % near or features % (near * col_parts) or features < least * near * col_parts):
        near -= 1
    return row_parts // near, near


def emit_projections(normed, rows_ref, out_refs):
    step = normed.shape[0]
    half = rows_ref.shape[0] // 2
    group = 256 if step % 256 == 0 else LANES
    for begin in range(0, step, group):
        projected = lax.dot_general(
            rows_ref[...], normed[begin : begin + group, :], (((1,), (1,)), ((), ())), preferred_element_type=jnp.float32
        )
        gated = sigmoid(projected[:half, :]) * projected[half:, :]
        at = 0
        for ref in out_refs:
            parts, width, _ = ref.shape
            for part in range(parts):
                ref[part, :, begin : begin + group] = gated[at : at + width, :].astype(ref.dtype)
                at += width


def project_kernel(state_ref, gain_ref, rows_ref, *out_refs):
    normed = layer_norm(state_ref[...].astype(jnp.float32), gain_ref[...], 1).astype(jnp.bfloat16)
    emit_projections(normed, rows_ref, out_refs)


def finish_kernel(pieces, onward, *refs):
    mix_refs, refs = refs[:pieces], refs[pieces:]
    state_ref, gain_ref, gate_ref, out_gain_ref, final_ref = refs[:5]
    state = state_ref[...].astype(jnp.float32)
    normed = layer_norm(state, gain_ref[...], 1).astype(jnp.bfloat16)
    gating = sigmoid(jnp.dot(normed, gate_ref[...], preferred_element_type=jnp.float32))
    mixed = jnp.concatenate(
        [ref[part].astype(jnp.float32) for ref in mix_refs for part in range(ref.shape[0])], axis=0
    )
    mixed = layer_norm(mixed, out_gain_ref[...], 0).astype(jnp.bfloat16)
    change = lax.dot_general(
        mixed, final_ref[...], (((0,), (0,)), ((), ())), preferred_element_type=jnp.float32
    )
    result = (state + gating * change).astype(jnp.bfloat16)
    if onward:
        next_gain, rows_ref, middle_ref = refs[5:8]
        middle_ref[...] = result
        normed = layer_norm(result.astype(jnp.float32), next_gain[...], 1).astype(jnp.bfloat16)
        emit_projections(normed, rows_ref, refs[8:])
    else:
        refs[5][...] = result


def whole_spec(array):
    return pl.BlockSpec(array.shape, lambda step: (0,) * array.ndim)


def row_step(positions):
    step = positions
    for candidate in range(LANES, 2304 + 1, LANES):
        if positions % candidate == 0:
            step = candidate
    return step


def run_projections(state, gain, rows, out_shapes):
    positions, features = state.shape
    step = row_step(positions)
    weights = (gain[None, :], rows)
    return pl.pallas_call(
        project_kernel,
        grid=(positions // step,),
        in_specs=[pl.BlockSpec((step, features), lambda i: (i, 0))] + [whole_spec(w) for w in weights],
        out_specs=[pl.BlockSpec((*shape, step), lambda i: (0, 0, i)) for shape in out_shapes],
        out_shape=[jax.ShapeDtypeStruct((*shape, positions), jnp.bfloat16) for shape in out_shapes],
        compiler_params=pltpu.CompilerParams(vmem_limit_bytes=BUDGET),
        name="project",
    )(state, *weights)


def run_finish(mixes, state, gain, gate_matrix, out_gain, final_matrix, onward=None):
    positions, features = state.shape
    step = row_step(positions)
    weights = (gain[None, :], gate_matrix, out_gain[:, None], final_matrix)
    out_shape = [jax.ShapeDtypeStruct((positions, features), jnp.bfloat16)]
    out_specs = [pl.BlockSpec((step, features), lambda i: (i, 0))]
    if onward is not None:
        next_gain, rows, out_shapes = onward
        weights += (next_gain[None, :], rows)
        out_shape += [jax.ShapeDtypeStruct((*shape, positions), jnp.bfloat16) for shape in out_shapes]
        out_specs += [pl.BlockSpec((*shape, step), lambda i: (0, 0, i)) for shape in out_shapes]
    return pl.pallas_call(
        functools.partial(finish_kernel, len(mixes), onward is not None),
        grid=(positions // step,),
        in_specs=[pl.BlockSpec((*m.shape[:2], step), lambda i: (0, 0, i)) for m in mixes]
        + [pl.BlockSpec((step, features), lambda i: (i, 0))]
        + [whole_spec(w) for w in weights],
        out_specs=out_specs,
        out_shape=out_shape,
        compiler_params=pltpu.CompilerParams(vmem_limit_bytes=BUDGET),
        name="finish",
    )(*mixes, state, *weights)


class Folds:
    def __init__(self, row_count, col_count):
        turn = 1
        while (turn * col_count) % LANES:
            turn *= 2
        self.turn, self.tiles = turn, turn * col_count // LANES
        self.cols, self.rows = col_count, row_count
        self.groups = row_count // turn
        self.lane_rows = row_count * col_count // LANES

    def fits(self):
        return self.cols <= LANES and self.rows % self.turn == 0 and self.groups % 8 == 0

    def split(self, lane_rows, clear=False):
        lane = lax.broadcasted_iota(jnp.int32, lane_rows[0].shape, 1)
        out = []
        for phase in range(self.turn):
            first, offset = divmod(phase * self.cols, LANES)
            value = lane_rows[first]
            if offset + self.cols > LANES:
                value = jnp.where(lane >= offset, value, lane_rows[first + 1])
            if offset:
                value = pltpu.roll(value, LANES - offset, 1)
            out.append(jnp.where(lane < self.cols, value, 0.0) if clear else value)
        return out

    def join(self, block_rows):
        lane = lax.broadcasted_iota(jnp.int32, block_rows[0].shape, 1)
        rolled = []
        for phase, value in enumerate(block_rows):
            offset = (phase * self.cols) % LANES
            rolled.append(pltpu.roll(value, offset, 1) if offset else value)
        out = []
        for tile in range(self.tiles):
            value = None
            for phase in range(self.turn):
                begin, end = phase * self.cols - tile * LANES, (phase + 1) * self.cols - tile * LANES
                if end <= 0 or begin >= LANES:
                    continue
                value = rolled[phase] if value is None else jnp.where(lane >= begin, rolled[phase], value)
            out.append(value)
        return out


def stage(source_ref, staged, shift=0, width=None):
    parts, held, positions = source_ref.shape
    width = width or held
    rows = parts * width
    for part in range(parts):
        values = source_ref[part].astype(jnp.float32)[shift : shift + width, :]
        for tile in range(positions // LANES):
            at = tile * rows + part * width
            staged[at : at + width, :] = values[:, tile * LANES : (tile + 1) * LANES]


def unstage(staged, target_ref, earlier_ref=None):
    parts, height, positions = target_ref.shape
    width = height if earlier_ref is None else height // 2
    rows = parts * width
    for tile in range(positions // LANES):
        lanes = slice(tile * LANES, (tile + 1) * LANES)
        for part in range(parts):
            at = tile * rows + part * width
            values = staged[at : at + width, :]
            if earlier_ref is not None:
                values = jnp.concatenate([earlier_ref[part, :, lanes].astype(jnp.float32), values], axis=0)
            target_ref[part, :, lanes] = values.astype(target_ref.dtype)


def lane_rows_of(folds, rows, row):
    return [pl.ds(row + tile * rows, folds.groups, stride=folds.tiles * rows) for tile in range(folds.tiles)]


def mix_out_kernel(folds, near, cols, width, half_ref, both_ref, there_ref, *refs):
    earlier_ref, (mix_ref, staged, left, right) = (refs[0] if len(refs) == 5 else None), refs[-4:]
    parts = near * cols
    rows = parts * width
    block = folds.rows
    far = cols // near

    stage(both_ref, staged)

    @pl.loop(0, rows, unroll=8)
    def _(step):
        source, channel = step // width, step % width
        row = source * 2 * width + channel
        pieces = folds.split([staged[at, :] for at in lane_rows_of(folds, 2 * rows, row)], clear=True)
        at = (channel * cols + source % cols) * near * block + (source // cols) * block
        left[pl.ds(pl.multiple_of(at, block), block), :] = jnp.concatenate(pieces, axis=0).astype(jnp.bfloat16)

    def place(half, total, shift, height):
        @pl.loop(0, rows, unroll=8)
        def _(step):
            source, channel = step // width, step % width
            row = source * height + shift + channel
            pieces = folds.split([staged[at, :] for at in lane_rows_of(folds, total, row)])
            at = ((channel * cols + source % cols) * far + half) * near * block + (source // cols) * block
            for phase, piece in enumerate(pieces):
                right[pl.ds(at + phase, folds.groups, stride=folds.turn), :] = piece

    place(half_ref[0], 2 * rows, width, 2 * width)
    stage(there_ref, staged)
    place(half_ref[1], rows, 0, width)

    @pl.loop(0, width, unroll=1)
    def _(channel):
        tall = near * block
        lhs = jnp.concatenate(
            [left[pl.ds(pl.multiple_of((channel * cols + col) * tall, block), tall), :] for col in range(cols)], axis=1
        )
        for target in range(cols):
            starts = [((channel * cols + col) * far * near + target) * block for col in range(cols)]
            rhs = jnp.concatenate([right[pl.ds(pl.multiple_of(at, block), block), :] for at in starts], axis=1)
            total = lax.dot_general(
                lhs, rhs.astype(jnp.bfloat16), (((1,), (1,)), ((), ())), preferred_element_type=jnp.float32
            )
            total = jnp.concatenate([total, jnp.zeros((near * block, LANES - block), jnp.float32)], axis=1)
            for piece in range(near):
                groups = folds.groups
                base = piece * block
                lane_rows = folds.join(
                    [total[base + phase * groups : base + (phase + 1) * groups, :] for phase in range(folds.turn)]
                )
                out_row = (piece * cols + target) * width + channel
                for at, value in zip(lane_rows_of(folds, rows, out_row), lane_rows):
                    staged[at, :] = value

    if earlier_ref is None:
        unstage(staged, mix_ref)
    else:
        unstage(staged, mix_ref, earlier_ref)


def mix_in_kernel(folds, near, cols, width, half_ref, both_ref, keep_ref, send_ref, staged, left, right, turned, mixed):
    parts = near * cols
    rows = 2 * parts * width
    block = folds.rows

    stage(both_ref, staged)

    for target, shift in ((left, 0), (right, width)):

        @pl.loop(0, parts * width, unroll=8)
        def _(step):
            source, channel = step // width, step % width
            row = source * 2 * width + shift + channel
            pieces = folds.split([staged[at, :] for at in lane_rows_of(folds, rows, row)])
            at = (channel * cols + source % cols) * near * block + (source // cols) * block
            target[pl.ds(pl.multiple_of(at, block), block), :] = jnp.concatenate(pieces, axis=0).astype(jnp.bfloat16)

    out_rows = parts * width
    tall = near * block

    @pl.loop(0, width, unroll=1)
    def _(channel):
        rhs = jnp.concatenate(
            [right[pl.ds(pl.multiple_of((channel * cols + col) * tall, block), tall), :] for col in range(cols)], axis=1
        )
        for upper in range(cols):
            lhs = left[pl.ds(pl.multiple_of((channel * cols + upper) * tall, block), tall), :]
            summed = lax.dot_general(lhs, rhs, (((0,), (0,)), ((), ())), preferred_element_type=jnp.float32)
            half, piece = divmod(upper, near)
            for target in range(cols):
                turned[upper, target] = summed[:, target * LANES : (target + 1) * LANES]
                lane_rows = folds.join(
                    [turned[upper, target, pl.ds(phase, folds.groups, stride=folds.turn), :] for phase in range(folds.turn)]
                )
                out_row = (piece * cols + target) * width + channel
                for at, value in zip(lane_rows_of(folds, out_rows, out_row), lane_rows):
                    mixed[half, at, :] = value

    unstage(mixed.at[half_ref[0]], keep_ref)
    unstage(mixed.at[half_ref[1]], send_ref)


SMEM_SPEC = pl.BlockSpec(memory_space=pltpu.SMEM)
VMEM_SPEC = pl.BlockSpec(memory_space=pltpu.VMEM)


def run_mix_out(folds, near, cols, halves, both, there, earlier=()):
    parts, width, positions = there.shape
    rows = parts * width
    block = folds.rows
    return pl.pallas_call(
        functools.partial(mix_out_kernel, folds, near, cols, width),
        in_specs=[SMEM_SPEC] + [VMEM_SPEC] * (2 + len(earlier)),
        out_specs=VMEM_SPEC,
        out_shape=jax.ShapeDtypeStruct((parts, width * (1 + len(earlier)), positions), jnp.bfloat16),
        scratch_shapes=[
            pltpu.VMEM((2 * rows * folds.lane_rows, LANES), jnp.float32),
            pltpu.VMEM((width * cols * near * block, LANES), jnp.bfloat16),
            pltpu.VMEM((width * cols * cols * block, LANES), jnp.float32),
        ],
        compiler_params=pltpu.CompilerParams(vmem_limit_bytes=BUDGET),
        name="mix_out",
    )(halves, both, there, *earlier)


def add_kernel(*refs):
    target_ref = refs[-1]
    parts = target_ref.shape[0]
    for part in range(parts):
        sums = [kept[part] + got[part].astype(jnp.float32) for kept, got in zip(refs[:-1:2], refs[1:-1:2])]
        target_ref[part] = jnp.concatenate(sums, axis=0).astype(target_ref.dtype)


def run_add(*arrays):
    parts, width, positions = arrays[0].shape
    step = row_step(positions)
    height = width * len(arrays) // 2
    return pl.pallas_call(
        add_kernel,
        grid=(positions // step,),
        in_specs=[pl.BlockSpec((parts, width, step), lambda i: (0, 0, i))] * len(arrays),
        out_specs=pl.BlockSpec((parts, height, step), lambda i: (0, 0, i)),
        out_shape=jax.ShapeDtypeStruct((parts, height, positions), jnp.bfloat16),
        compiler_params=pltpu.CompilerParams(vmem_limit_bytes=BUDGET),
        name="add",
    )(*arrays)


def run_mix_in(folds, near, cols, halves, both):
    parts, width, positions = both.shape
    rows, width = parts * width, width // 2
    block = folds.rows
    return pl.pallas_call(
        functools.partial(mix_in_kernel, folds, near, cols, width),
        in_specs=[SMEM_SPEC, VMEM_SPEC],
        out_specs=[VMEM_SPEC, VMEM_SPEC],
        out_shape=[
            jax.ShapeDtypeStruct((parts, width, positions), jnp.float32),
            jax.ShapeDtypeStruct((parts, width, positions), jnp.bfloat16),
        ],
        scratch_shapes=[
            pltpu.VMEM((rows * folds.lane_rows, LANES), jnp.float32),
            pltpu.VMEM((width * cols * near * block, LANES), jnp.bfloat16),
            pltpu.VMEM((width * cols * near * block, LANES), jnp.bfloat16),
            pltpu.VMEM((cols, cols, LANES, LANES), jnp.float32),
            pltpu.VMEM((2, rows // 2 * folds.lane_rows, LANES), jnp.float32),
        ],
        compiler_params=pltpu.CompilerParams(vmem_limit_bytes=BUDGET),
        name="mix_in",
    )(halves, both)


PIECES = 4


def exchange(array):
    return lax.all_to_all(array, EVERY, split_axis=0, concat_axis=0, tiled=True)


def across(array):
    return lax.ppermute(array, "far", ((0, 1), (1, 0)))


def in_halves(sizes, pair_input, weights):
    _, near, cols = sizes
    row_count, col_count, features = pair_input.shape
    parts = near * cols
    width = features // parts
    pieces = PIECES
    piece_width = width // pieces
    folds = Folds(row_count, col_count)
    half = lax.axis_index("far")
    halves = jnp.stack([half, 1 - half]).astype(jnp.int32)

    def by_piece(rows):
        return rows.reshape(parts, pieces, width // pieces, -1).transpose(1, 0, 2, 3)

    def rows_of(project, order):
        ga, va, gb, vb = (by_piece(rows) for rows in jnp.split(project.T, 4, axis=0))
        return jnp.concatenate([order(ga, gb).reshape(-1, features), order(va, vb).reshape(-1, features)])

    def side_by_side(left, right):
        return jnp.concatenate([left, right], axis=2)

    def unordered(array):
        rows = array.reshape(parts, pieces // 2, 2 * piece_width, -1)
        return rows.transpose(1, 0, 2, 3).reshape(array.shape)

    gain_1, project_1, gate_1, norm_1, final_1, gain_2, project_2, gate_2, norm_2, final_2 = weights
    state = pair_input.reshape(-1, features)

    shapes = ((parts, 2 * piece_width),) * pieces
    both, mixes = [], []
    out = run_projections(state, gain_1, rows_of(project_1, side_by_side), shapes)
    for piece in range(pieces):
        both.append(exchange(out[piece]))
    for piece in range(pieces):
        there = across(both[piece][:, piece_width:, :])
        mixed = run_mix_out(folds, near, cols, halves, both[piece], there, (mixed,) if piece % 2 else ())
        if piece % 2:
            mixes.append(exchange(mixed))
    onward = (gain_2, rows_of(project_2, side_by_side), shapes)
    out = run_finish(mixes, state, gain_1, gate_1, unordered(norm_1), unordered(final_1), onward)
    middle, both, parted, mixes = out[0], [], [], []
    for piece in range(pieces):
        both.append(exchange(out[1 + piece]))
    for piece in range(pieces):
        kept, sent = run_mix_in(folds, near, cols, halves, both[piece])
        parted.append((kept, across(sent)))
    for pair in range(pieces // 2):
        mixed = run_add(*parted[2 * pair], *parted[2 * pair + 1])
        mixes.append(exchange(mixed))
    result = run_finish(mixes, middle, gain_2, gate_2, unordered(norm_2), unordered(final_2))[0]
    return result.reshape(pair_input.shape)


def solution(mesh):
    row_parts, col_parts = mesh.shape["dap"], mesh.shape["chan"] * mesh.shape["sub"]

    def whole(pair_input, *weights):
        features = pair_input.shape[-1]
        block_rows = pair_input.shape[0] // (mesh.shape["groups"] * row_parts)
        block_cols = pair_input.shape[1] // col_parts
        halved = (
            row_parts % 2 == 0
            and row_parts == col_parts
            and block_rows == block_cols
            and Folds(block_rows, block_cols).fits()
            and features == LANES
            and features % (row_parts // 2 * col_parts * PIECES) == 0
        )
        if halved:
            far, near = 2, row_parts // 2
        else:
            far, near = split_rows(row_parts, col_parts, features, 8)
        sizes = (far, near, col_parts)
        finer = Mesh(
            mesh.devices.reshape(mesh.shape["groups"], far, near, mesh.shape["chan"], mesh.shape["sub"]),
            ("groups", "far", "near", "chan", "sub"),
        )

        def shards(pair_input, *weights):
            if halved:
                return in_halves(sizes, pair_input, weights)
            middle = update(False, sizes, pair_input, *weights[:5])
            return update(True, sizes, middle, *weights[5:])

        pair_spec = P(("groups", "far", "near"), ("chan", "sub"), None)
        mapped = jax.shard_map(
            shards,
            mesh=finer,
            in_specs=(pair_spec,) + (P(),) * 10,
            out_specs=pair_spec,
            check_vma=False,
        )
        return mapped(pair_input, *weights)

    return whole
```

```python
import functools

import jax
import jax.numpy as jnp
from jax import lax
from jax.experimental import pallas as pl
from jax.experimental.pallas import tpu as pltpu
from jax.sharding import Mesh
from jax.sharding import PartitionSpec as P


epsilon = 1e-05
EVERY = ("near", "chan", "sub")
LANES = 128
BUDGET = 56 << 20


def layer_norm(values, norm_gain, reduce_axis):
    average = jnp.mean(values, axis=reduce_axis, keepdims=True)
    centred = values - average
    variance = jnp.mean(centred * centred, axis=reduce_axis, keepdims=True)
    return centred * lax.rsqrt(variance + epsilon) * norm_gain


def sigmoid(values):
    return 0.5 * jnp.tanh(0.5 * values) + 0.5


def project_in(pair_state, norm_gain, project, gate_matrix):
    features = pair_state.shape[-1]
    flattened = pair_state.reshape(-1, features).astype(jnp.float32)
    normed = layer_norm(flattened, norm_gain, 1).astype(jnp.bfloat16)
    projected = jnp.einsum("xc,cd->dx", normed, project, preferred_element_type=jnp.float32)
    left_part = jax.nn.sigmoid(projected[:features]) * projected[features : 2 * features]
    right_part = jax.nn.sigmoid(projected[2 * features : 3 * features]) * projected[3 * features :]
    gating = jax.nn.sigmoid(jnp.dot(normed, gate_matrix, preferred_element_type=jnp.float32))
    return left_part.astype(jnp.bfloat16), right_part.astype(jnp.bfloat16), gating


def finish(pair_state, mixture, gating, out_gain, final_matrix):
    features = mixture.shape[0]
    flattened = mixture.astype(jnp.float32)
    normed = layer_norm(flattened, out_gain[:, None], 0).astype(jnp.bfloat16)
    update = jnp.einsum("cx,cd->xd", normed, final_matrix, preferred_element_type=jnp.float32)
    result = pair_state.reshape(-1, features).astype(jnp.float32) + gating * update
    return result.astype(jnp.bfloat16).reshape(pair_state.shape)


def update(incoming, sizes, pair_state, norm_gain, project, gate_matrix, out_gain, final_matrix):
    far, near, col_parts = sizes
    row_count, col_count, features = pair_state.shape
    parts = near * col_parts
    width = features // parts
    left_part, right_part, gating = project_in(pair_state, norm_gain, project, gate_matrix)
    both = jnp.stack([left_part.reshape(parts, width, -1), right_part.reshape(parts, width, -1)], axis=1)
    both = lax.all_to_all(both, EVERY, split_axis=0, concat_axis=0, tiled=True)
    both = both.reshape(near, col_parts, 2, width, row_count, col_count)
    both = both.transpose(2, 3, 0, 4, 1, 5).reshape(2, width, near * row_count, col_parts * col_count)
    left_part, right_part = both[0], both[1]
    if incoming:
        mixture = jnp.einsum("cki,ckj->cij", left_part, right_part, preferred_element_type=jnp.float32)
        if far > 1:
            mixture = lax.psum_scatter(mixture, "far", scatter_dimension=1, tiled=True)
    else:
        if far > 1:
            right_part = lax.all_gather(right_part, "far", axis=1, tiled=True)
        mixture = jnp.einsum("cik,cjk->cij", left_part, right_part, preferred_element_type=jnp.float32)
    mixture = mixture.astype(jnp.bfloat16).reshape(width, near, row_count, col_parts, col_count)
    mixture = mixture.transpose(1, 3, 0, 2, 4).reshape(parts, width, row_count * col_count)
    mixture = lax.all_to_all(mixture, EVERY, split_axis=0, concat_axis=0, tiled=True)
    return finish(pair_state, mixture.reshape(features, -1), gating, out_gain, final_matrix)


def split_rows(row_parts, col_parts, features, least):
    near = row_parts
    while near > 1 and (row_parts % near or features % (near * col_parts) or features < least * near * col_parts):
        near -= 1
    return row_parts // near, near


def lane_mean(values):
    lanes = values.shape[1]
    return jnp.dot(values, jnp.full((lanes, lanes), 1 / lanes, jnp.bfloat16), preferred_element_type=jnp.float32)


def lane_norm(values, norm_gain):
    centred = values.astype(jnp.float32) - lane_mean(values)
    squares = centred * centred
    high = squares.astype(jnp.bfloat16)
    low = (squares - high.astype(jnp.float32)).astype(jnp.bfloat16)
    variance = lane_mean(high) + lane_mean(low)
    return centred * lax.rsqrt(variance + epsilon) * norm_gain


def emit_projections(normed, rows_ref, out_refs):
    step = normed.shape[0]
    half = rows_ref.shape[0] // 2
    group = 256 if step % 256 == 0 else LANES
    for begin in range(0, step, group):
        projected = lax.dot_general(
            rows_ref[...], normed[begin : begin + group, :], (((1,), (1,)), ((), ())), preferred_element_type=jnp.float32
        )
        gated = sigmoid(projected[:half, :]) * projected[half:, :]
        at = 0
        for ref in out_refs:
            parts, width, _ = ref.shape
            for part in range(parts):
                ref[part, :, begin : begin + group] = gated[at : at + width, :].astype(ref.dtype)
                at += width


def project_kernel(state_ref, gain_ref, rows_ref, *out_refs):
    normed = lane_norm(state_ref[...], gain_ref[...]).astype(jnp.bfloat16)
    emit_projections(normed, rows_ref, out_refs)


def finish_kernel(pieces, onward, *refs):
    mix_refs, refs = refs[:pieces], refs[pieces:]
    state_ref, gain_ref, gate_ref, out_gain_ref, final_ref = refs[:5]
    state = state_ref[...].astype(jnp.float32)
    normed = lane_norm(state_ref[...], gain_ref[...]).astype(jnp.bfloat16)
    gating = sigmoid(jnp.dot(normed, gate_ref[...], preferred_element_type=jnp.float32))
    mixed = jnp.concatenate(
        [ref[part].astype(jnp.float32) for ref in mix_refs for part in range(ref.shape[0])], axis=0
    )
    mixed = layer_norm(mixed, out_gain_ref[...], 0).astype(jnp.bfloat16)
    change = lax.dot_general(
        mixed, final_ref[...], (((0,), (0,)), ((), ())), preferred_element_type=jnp.float32
    )
    result = (state + gating * change).astype(jnp.bfloat16)
    if onward:
        next_gain, rows_ref, middle_ref = refs[5:8]
        middle_ref[...] = result
        normed = lane_norm(result, next_gain[...]).astype(jnp.bfloat16)
        emit_projections(normed, rows_ref, refs[8:])
    else:
        refs[5][...] = result


def whole_spec(array):
    return pl.BlockSpec(array.shape, lambda step: (0,) * array.ndim)


def row_step(positions):
    step = positions
    for candidate in range(LANES, 2304 + 1, LANES):
        if positions % candidate == 0:
            step = candidate
    return step


def run_projections(state, gain, rows, out_shapes):
    positions, features = state.shape
    step = row_step(positions)
    weights = (gain[None, :], rows)
    return pl.pallas_call(
        project_kernel,
        grid=(positions // step,),
        in_specs=[pl.BlockSpec((step, features), lambda i: (i, 0))] + [whole_spec(w) for w in weights],
        out_specs=[pl.BlockSpec((*shape, step), lambda i: (0, 0, i)) for shape in out_shapes],
        out_shape=[jax.ShapeDtypeStruct((*shape, positions), jnp.bfloat16) for shape in out_shapes],
        compiler_params=pltpu.CompilerParams(vmem_limit_bytes=BUDGET),
        name="project",
    )(state, *weights)


def run_finish(mixes, state, gain, gate_matrix, out_gain, final_matrix, onward=None):
    positions, features = state.shape
    step = row_step(positions)
    weights = (gain[None, :], gate_matrix, out_gain[:, None], final_matrix)
    out_shape = [jax.ShapeDtypeStruct((positions, features), jnp.bfloat16)]
    out_specs = [pl.BlockSpec((step, features), lambda i: (i, 0))]
    if onward is not None:
        next_gain, rows, out_shapes = onward
        weights += (next_gain[None, :], rows)
        out_shape += [jax.ShapeDtypeStruct((*shape, positions), jnp.bfloat16) for shape in out_shapes]
        out_specs += [pl.BlockSpec((*shape, step), lambda i: (0, 0, i)) for shape in out_shapes]
    return pl.pallas_call(
        functools.partial(finish_kernel, len(mixes), onward is not None),
        grid=(positions // step,),
        in_specs=[pl.BlockSpec((*m.shape[:2], step), lambda i: (0, 0, i)) for m in mixes]
        + [pl.BlockSpec((step, features), lambda i: (i, 0))]
        + [whole_spec(w) for w in weights],
        out_specs=out_specs,
        out_shape=out_shape,
        compiler_params=pltpu.CompilerParams(vmem_limit_bytes=BUDGET),
        name="finish",
    )(*(pltpu.with_memory_space_constraint(m, pltpu.HBM) for m in mixes), state, *weights)


class Folds:
    def __init__(self, row_count, col_count):
        turn = 1
        while (turn * col_count) % LANES:
            turn *= 2
        self.turn, self.tiles = turn, turn * col_count // LANES
        self.cols, self.rows = col_count, row_count
        self.groups = row_count // turn
        self.lane_rows = row_count * col_count // LANES

    def fits(self):
        return self.cols <= LANES and self.rows % self.turn == 0 and self.groups % 8 == 0

    def split(self, lane_rows, clear=False):
        lane = lax.broadcasted_iota(jnp.int32, lane_rows[0].shape, 1)
        out = []
        for phase in range(self.turn):
            first, offset = divmod(phase * self.cols, LANES)
            value = lane_rows[first]
            if offset + self.cols > LANES:
                value = jnp.where(lane >= offset, value, lane_rows[first + 1])
            if offset:
                value = pltpu.roll(value, LANES - offset, 1)
            out.append(jnp.where(lane < self.cols, value, 0.0) if clear else value)
        return out

    def join(self, block_rows):
        lane = lax.broadcasted_iota(jnp.int32, block_rows[0].shape, 1)
        rolled = []
        for phase, value in enumerate(block_rows):
            offset = (phase * self.cols) % LANES
            rolled.append(pltpu.roll(value, offset, 1) if offset else value)
        out = []
        for tile in range(self.tiles):
            value = None
            for phase in range(self.turn):
                begin, end = phase * self.cols - tile * LANES, (phase + 1) * self.cols - tile * LANES
                if end <= 0 or begin >= LANES:
                    continue
                value = rolled[phase] if value is None else jnp.where(lane >= begin, rolled[phase], value)
            out.append(value)
        return out


def stage(source_ref, staged, shift=0, width=None):
    parts, held, positions = source_ref.shape
    width = width or held
    rows = parts * width
    for part in range(parts):
        values = source_ref[part].astype(jnp.float32)[shift : shift + width, :]
        for tile in range(positions // LANES):
            at = tile * rows + part * width
            staged[at : at + width, :] = values[:, tile * LANES : (tile + 1) * LANES]


def unstage(staged, target_ref, earlier_ref=None):
    parts, height, positions = target_ref.shape
    width = height if earlier_ref is None else height // 2
    rows = parts * width
    for tile in range(positions // LANES):
        lanes = slice(tile * LANES, (tile + 1) * LANES)
        for part in range(parts):
            at = tile * rows + part * width
            values = staged[at : at + width, :]
            if earlier_ref is not None:
                values = jnp.concatenate([earlier_ref[part, :, lanes].astype(jnp.float32), values], axis=0)
            target_ref[part, :, lanes] = values.astype(target_ref.dtype)


def lane_rows_of(folds, rows, row):
    return [pl.ds(row + tile * rows, folds.groups, stride=folds.tiles * rows) for tile in range(folds.tiles)]


def mix_out_kernel(folds, near, cols, width, half_ref, both_ref, there_ref, *refs):
    earlier_ref, (mix_ref, staged, left, right) = (refs[0] if len(refs) == 5 else None), refs[-4:]
    parts = near * cols
    rows = parts * width
    block = folds.rows
    far = cols // near

    stage(both_ref, staged)

    @pl.loop(0, rows, unroll=8)
    def _(step):
        source, channel = step // width, step % width
        row = source * 2 * width + channel
        pieces = folds.split([staged[at, :] for at in lane_rows_of(folds, 2 * rows, row)], clear=True)
        at = (channel * cols + source % cols) * near * block + (source // cols) * block
        left[pl.ds(pl.multiple_of(at, block), block), :] = jnp.concatenate(pieces, axis=0).astype(jnp.bfloat16)

    def place(half, total, shift, height):
        @pl.loop(0, rows, unroll=8)
        def _(step):
            source, channel = step // width, step % width
            row = source * height + shift + channel
            pieces = folds.split([staged[at, :] for at in lane_rows_of(folds, total, row)])
            at = ((channel * cols + source % cols) * far + half) * near * block + (source // cols) * block
            for phase, piece in enumerate(pieces):
                right[pl.ds(at + phase, folds.groups, stride=folds.turn), :] = piece

    place(half_ref[0], 2 * rows, width, 2 * width)
    stage(there_ref, staged)
    place(half_ref[1], rows, 0, width)

    @pl.loop(0, width, unroll=1)
    def _(channel):
        tall = near * block
        lhs = jnp.concatenate(
            [left[pl.ds(pl.multiple_of((channel * cols + col) * tall, block), tall), :] for col in range(cols)], axis=1
        )
        for target in range(cols):
            starts = [((channel * cols + col) * far * near + target) * block for col in range(cols)]
            rhs = jnp.concatenate([right[pl.ds(pl.multiple_of(at, block), block), :] for at in starts], axis=1)
            total = lax.dot_general(
                lhs, rhs.astype(jnp.bfloat16), (((1,), (1,)), ((), ())), preferred_element_type=jnp.float32
            )
            total = jnp.concatenate([total, jnp.zeros((near * block, LANES - block), jnp.float32)], axis=1)
            for piece in range(near):
                groups = folds.groups
                base = piece * block
                lane_rows = folds.join(
                    [total[base + phase * groups : base + (phase + 1) * groups, :] for phase in range(folds.turn)]
                )
                out_row = (piece * cols + target) * width + channel
                for at, value in zip(lane_rows_of(folds, rows, out_row), lane_rows):
                    staged[at, :] = value

    if earlier_ref is None:
        unstage(staged, mix_ref)
    else:
        unstage(staged, mix_ref, earlier_ref)


def mix_in_kernel(folds, near, cols, width, half_ref, both_ref, keep_ref, send_ref, staged, left, right, turned, mixed):
    parts = near * cols
    rows = 2 * parts * width
    block = folds.rows

    stage(both_ref, staged)

    for target, shift in ((left, 0), (right, width)):

        @pl.loop(0, parts * width, unroll=8)
        def _(step):
            source, channel = step // width, step % width
            row = source * 2 * width + shift + channel
            pieces = folds.split([staged[at, :] for at in lane_rows_of(folds, rows, row)])
            at = (channel * cols + source % cols) * near * block + (source // cols) * block
            target[pl.ds(pl.multiple_of(at, block), block), :] = jnp.concatenate(pieces, axis=0).astype(jnp.bfloat16)

    out_rows = parts * width
    tall = near * block

    @pl.loop(0, width, unroll=1)
    def _(channel):
        rhs = jnp.concatenate(
            [right[pl.ds(pl.multiple_of((channel * cols + col) * tall, block), tall), :] for col in range(cols)], axis=1
        )
        for upper in range(cols):
            lhs = left[pl.ds(pl.multiple_of((channel * cols + upper) * tall, block), tall), :]
            summed = lax.dot_general(lhs, rhs, (((0,), (0,)), ((), ())), preferred_element_type=jnp.float32)
            half, piece = divmod(upper, near)
            for target in range(cols):
                turned[upper, target] = summed[:, target * LANES : (target + 1) * LANES]
                lane_rows = folds.join(
                    [turned[upper, target, pl.ds(phase, folds.groups, stride=folds.turn), :] for phase in range(folds.turn)]
                )
                out_row = (piece * cols + target) * width + channel
                for at, value in zip(lane_rows_of(folds, out_rows, out_row), lane_rows):
                    mixed[half, at, :] = value

    unstage(mixed.at[half_ref[0]], keep_ref)
    unstage(mixed.at[half_ref[1]], send_ref)


SMEM_SPEC = pl.BlockSpec(memory_space=pltpu.SMEM)
VMEM_SPEC = pl.BlockSpec(memory_space=pltpu.VMEM)


def run_mix_out(folds, near, cols, halves, both, there, earlier=()):
    parts, width, positions = there.shape
    rows = parts * width
    block = folds.rows
    return pl.pallas_call(
        functools.partial(mix_out_kernel, folds, near, cols, width),
        in_specs=[SMEM_SPEC] + [VMEM_SPEC] * (2 + len(earlier)),
        out_specs=VMEM_SPEC,
        out_shape=jax.ShapeDtypeStruct((parts, width * (1 + len(earlier)), positions), jnp.bfloat16),
        scratch_shapes=[
            pltpu.VMEM((2 * rows * folds.lane_rows, LANES), jnp.float32),
            pltpu.VMEM((width * cols * near * block, LANES), jnp.bfloat16),
            pltpu.VMEM((width * cols * cols * block, LANES), jnp.float32),
        ],
        compiler_params=pltpu.CompilerParams(vmem_limit_bytes=BUDGET),
        name="mix_out",
    )(halves, both, there, *earlier)


def add_kernel(*refs):
    target_ref = refs[-1]
    parts = target_ref.shape[0]
    for part in range(parts):
        sums = [kept[part] + got[part].astype(jnp.float32) for kept, got in zip(refs[:-1:2], refs[1:-1:2])]
        target_ref[part] = jnp.concatenate(sums, axis=0).astype(target_ref.dtype)


def run_add(*arrays):
    parts, width, positions = arrays[0].shape
    step = row_step(positions)
    height = width * len(arrays) // 2
    return pl.pallas_call(
        add_kernel,
        grid=(positions // step,),
        in_specs=[pl.BlockSpec((parts, width, step), lambda i: (0, 0, i))] * len(arrays),
        out_specs=pl.BlockSpec((parts, height, step), lambda i: (0, 0, i)),
        out_shape=jax.ShapeDtypeStruct((parts, height, positions), jnp.bfloat16),
        compiler_params=pltpu.CompilerParams(vmem_limit_bytes=BUDGET),
        name="add",
    )(*arrays)


def run_mix_in(folds, near, cols, halves, both):
    parts, width, positions = both.shape
    rows, width = parts * width, width // 2
    block = folds.rows
    return pl.pallas_call(
        functools.partial(mix_in_kernel, folds, near, cols, width),
        in_specs=[SMEM_SPEC, VMEM_SPEC],
        out_specs=[VMEM_SPEC, VMEM_SPEC],
        out_shape=[
            jax.ShapeDtypeStruct((parts, width, positions), jnp.float32),
            jax.ShapeDtypeStruct((parts, width, positions), jnp.bfloat16),
        ],
        scratch_shapes=[
            pltpu.VMEM((rows * folds.lane_rows, LANES), jnp.float32),
            pltpu.VMEM((width * cols * near * block, LANES), jnp.bfloat16),
            pltpu.VMEM((width * cols * near * block, LANES), jnp.bfloat16),
            pltpu.VMEM((cols, cols, LANES, LANES), jnp.float32),
            pltpu.VMEM((2, rows // 2 * folds.lane_rows, LANES), jnp.float32),
        ],
        compiler_params=pltpu.CompilerParams(vmem_limit_bytes=BUDGET),
        name="mix_in",
    )(halves, both)


PIECES = 4
OUT_GROUPS = ((0, 2), (2, 1), (3, 1))
IN_GROUPS = ((0, 2), (2, 2))


def group_of(groups, piece):
    return next((begin, count, at) for at, (begin, count) in enumerate(groups) if begin <= piece < begin + count)


def exchange(array):
    return lax.all_to_all(array, EVERY, split_axis=0, concat_axis=0, tiled=True)


def across(array):
    return lax.ppermute(array, "far", ((0, 1), (1, 0)))


def in_halves(sizes, pair_input, weights):
    _, near, cols = sizes
    row_count, col_count, features = pair_input.shape
    parts = near * cols
    width = features // parts
    pieces = PIECES
    piece_width = width // pieces
    folds = Folds(row_count, col_count)
    half = lax.axis_index("far")
    halves = jnp.stack([half, 1 - half]).astype(jnp.int32)

    def by_piece(rows):
        return rows.reshape(parts, pieces, width // pieces, -1).transpose(1, 0, 2, 3)

    def rows_of(project, begin, end):
        ga, va, gb, vb = (by_piece(rows)[begin:end] for rows in jnp.split(project.T, 4, axis=0))
        gates, values = jnp.concatenate([ga, gb], axis=2), jnp.concatenate([va, vb], axis=2)
        return jnp.concatenate([gates.reshape(-1, features), values.reshape(-1, features)])

    def in_groups(array, groups):
        rows = by_piece(array.reshape(features, -1))
        ordered = [rows[begin : begin + count].transpose(1, 0, 2, 3).reshape(-1, rows.shape[-1]) for begin, count in groups]
        return jnp.concatenate(ordered).reshape(array.shape)

    gain_1, project_1, gate_1, norm_1, final_1, gain_2, project_2, gate_2, norm_2, final_2 = weights
    state = pair_input.reshape(-1, features)

    shapes = ((parts, 2 * piece_width),) * pieces
    mixed, both, mixes = None, [], []
    out = run_projections(state, gain_1, rows_of(project_1, 0, 1), shapes[:1])
    out += run_projections(state, gain_1, rows_of(project_1, 1, pieces), shapes[1:])
    for piece in range(pieces):
        both.append(exchange(out[piece]))
    for piece in range(pieces):
        begin, count, _ = group_of(OUT_GROUPS, piece)
        there = across(both[piece][:, piece_width:, :])
        mixed = run_mix_out(folds, near, cols, halves, both[piece], there, (mixed,) if piece > begin else ())
        if piece == begin + count - 1:
            mixes.append(exchange(mixed))
    onward = (gain_2, rows_of(project_2, 0, 1), shapes[:1])
    norm, final = in_groups(norm_1, OUT_GROUPS), in_groups(final_1, OUT_GROUPS)
    middle, *out = run_finish(mixes, state, gain_1, gate_1, norm, final, onward)
    out += run_projections(middle, gain_2, rows_of(project_2, 1, pieces), shapes[1:])
    both, parted, mixes = [], [], []
    for piece in range(pieces):
        both.append(exchange(out[piece]))
    for piece in range(pieces):
        kept, sent = run_mix_in(folds, near, cols, halves, both[piece])
        parted.append((kept, across(sent)))
    for begin, count in IN_GROUPS:
        last = begin + count - 1
        mixed = run_add(*(array for pair in parted[begin : last + 1] for array in pair))
        mixes.append(exchange(mixed))
    norm, final = in_groups(norm_2, IN_GROUPS), in_groups(final_2, IN_GROUPS)
    result = run_finish(mixes, middle, gain_2, gate_2, norm, final)[0]
    return result.reshape(pair_input.shape)


def solution(mesh):
    row_parts, col_parts = mesh.shape["dap"], mesh.shape["chan"] * mesh.shape["sub"]

    def whole(pair_input, *weights):
        features = pair_input.shape[-1]
        block_rows = pair_input.shape[0] // (mesh.shape["groups"] * row_parts)
        block_cols = pair_input.shape[1] // col_parts
        halved = (
            row_parts % 2 == 0
            and row_parts == col_parts
            and block_rows == block_cols
            and Folds(block_rows, block_cols).fits()
            and features == LANES
            and features % (row_parts // 2 * col_parts * PIECES) == 0
        )
        if halved:
            far, near = 2, row_parts // 2
        else:
            far, near = split_rows(row_parts, col_parts, features, 8)
        sizes = (far, near, col_parts)
        finer = Mesh(
            mesh.devices.reshape(mesh.shape["groups"], far, near, mesh.shape["chan"], mesh.shape["sub"]),
            ("groups", "far", "near", "chan", "sub"),
        )

        def shards(pair_input, *weights):
            if halved:
                return in_halves(sizes, pair_input, weights)
            middle = update(False, sizes, pair_input, *weights[:5])
            return update(True, sizes, middle, *weights[5:])

        pair_spec = P(("groups", "far", "near"), ("chan", "sub"), None)
        mapped = jax.shard_map(
            shards,
            mesh=finer,
            in_specs=(pair_spec,) + (P(),) * 10,
            out_specs=pair_spec,
            check_vma=False,
        )
        return mapped(pair_input, *weights)

    return whole
```

```python
import functools

import jax
import jax.numpy as jnp
from jax import lax
from jax.experimental import pallas as pl
from jax.experimental.pallas import tpu as pltpu
from jax.sharding import Mesh
from jax.sharding import PartitionSpec as P


epsilon = 1e-05
EVERY = ("near", "chan", "sub")
LANES = 128
BUDGET = 56 << 20


def layer_norm(values, norm_gain, reduce_axis):
    average = jnp.mean(values, axis=reduce_axis, keepdims=True)
    centred = values - average
    variance = jnp.mean(centred * centred, axis=reduce_axis, keepdims=True)
    return centred * lax.rsqrt(variance + epsilon) * norm_gain


def sigmoid(values):
    return 0.5 * jnp.tanh(0.5 * values) + 0.5


def project_in(pair_state, norm_gain, project, gate_matrix):
    features = pair_state.shape[-1]
    flattened = pair_state.reshape(-1, features).astype(jnp.float32)
    normed = layer_norm(flattened, norm_gain, 1).astype(jnp.bfloat16)
    projected = jnp.einsum("xc,cd->dx", normed, project, preferred_element_type=jnp.float32)
    left_part = jax.nn.sigmoid(projected[:features]) * projected[features : 2 * features]
    right_part = jax.nn.sigmoid(projected[2 * features : 3 * features]) * projected[3 * features :]
    gating = jax.nn.sigmoid(jnp.dot(normed, gate_matrix, preferred_element_type=jnp.float32))
    return left_part.astype(jnp.bfloat16), right_part.astype(jnp.bfloat16), gating


def finish(pair_state, mixture, gating, out_gain, final_matrix):
    features = mixture.shape[0]
    flattened = mixture.astype(jnp.float32)
    normed = layer_norm(flattened, out_gain[:, None], 0).astype(jnp.bfloat16)
    update = jnp.einsum("cx,cd->xd", normed, final_matrix, preferred_element_type=jnp.float32)
    result = pair_state.reshape(-1, features).astype(jnp.float32) + gating * update
    return result.astype(jnp.bfloat16).reshape(pair_state.shape)


def update(incoming, sizes, pair_state, norm_gain, project, gate_matrix, out_gain, final_matrix):
    far, near, col_parts = sizes
    row_count, col_count, features = pair_state.shape
    parts = near * col_parts
    width = features // parts
    left_part, right_part, gating = project_in(pair_state, norm_gain, project, gate_matrix)
    both = jnp.stack([left_part.reshape(parts, width, -1), right_part.reshape(parts, width, -1)], axis=1)
    both = lax.all_to_all(both, EVERY, split_axis=0, concat_axis=0, tiled=True)
    both = both.reshape(near, col_parts, 2, width, row_count, col_count)
    both = both.transpose(2, 3, 0, 4, 1, 5).reshape(2, width, near * row_count, col_parts * col_count)
    left_part, right_part = both[0], both[1]
    if incoming:
        mixture = jnp.einsum("cki,ckj->cij", left_part, right_part, preferred_element_type=jnp.float32)
        if far > 1:
            mixture = lax.psum_scatter(mixture, "far", scatter_dimension=1, tiled=True)
    else:
        if far > 1:
            right_part = lax.all_gather(right_part, "far", axis=1, tiled=True)
        mixture = jnp.einsum("cik,cjk->cij", left_part, right_part, preferred_element_type=jnp.float32)
    mixture = mixture.astype(jnp.bfloat16).reshape(width, near, row_count, col_parts, col_count)
    mixture = mixture.transpose(1, 3, 0, 2, 4).reshape(parts, width, row_count * col_count)
    mixture = lax.all_to_all(mixture, EVERY, split_axis=0, concat_axis=0, tiled=True)
    return finish(pair_state, mixture.reshape(features, -1), gating, out_gain, final_matrix)


def split_rows(row_parts, col_parts, features, least):
    near = row_parts
    while near > 1 and (row_parts % near or features % (near * col_parts) or features < least * near * col_parts):
        near -= 1
    return row_parts // near, near


def emit_projections(normed, rows_ref, out_refs):
    step = normed.shape[0]
    half = rows_ref.shape[0] // 2
    group = 256 if step % 256 == 0 else LANES
    for begin in range(0, step, group):
        projected = lax.dot_general(
            rows_ref[...], normed[begin : begin + group, :], (((1,), (1,)), ((), ())), preferred_element_type=jnp.float32
        )
        gated = sigmoid(projected[:half, :]) * projected[half:, :]
        at = 0
        for ref in out_refs:
            parts, width, _ = ref.shape
            for part in range(parts):
                ref[part, :, begin : begin + group] = gated[at : at + width, :].astype(ref.dtype)
                at += width


def project_kernel(state_ref, gain_ref, rows_ref, *out_refs):
    normed = layer_norm(state_ref[...].astype(jnp.float32), gain_ref[...], 1).astype(jnp.bfloat16)
    emit_projections(normed, rows_ref, out_refs)


def finish_kernel(pieces, onward, *refs):
    mix_refs, refs = refs[:pieces], refs[pieces:]
    state_ref, gain_ref, gate_ref, out_gain_ref, final_ref = refs[:5]
    state = state_ref[...].astype(jnp.float32)
    normed = layer_norm(state, gain_ref[...], 1).astype(jnp.bfloat16)
    gating = sigmoid(jnp.dot(normed, gate_ref[...], preferred_element_type=jnp.float32))
    mixed = jnp.concatenate(
        [ref[part].astype(jnp.float32) for ref in mix_refs for part in range(ref.shape[0])], axis=0
    )
    mixed = layer_norm(mixed, out_gain_ref[...], 0).astype(jnp.bfloat16)
    change = lax.dot_general(
        mixed, final_ref[...], (((0,), (0,)), ((), ())), preferred_element_type=jnp.float32
    )
    result = (state + gating * change).astype(jnp.bfloat16)
    if onward:
        next_gain, rows_ref, middle_ref = refs[5:8]
        middle_ref[...] = result
        normed = layer_norm(result.astype(jnp.float32), next_gain[...], 1).astype(jnp.bfloat16)
        emit_projections(normed, rows_ref, refs[8:])
    else:
        refs[5][...] = result


def whole_spec(array):
    return pl.BlockSpec(array.shape, lambda step: (0,) * array.ndim)


def row_step(positions):
    step = positions
    for candidate in range(LANES, 2304 + 1, LANES):
        if positions % candidate == 0:
            step = candidate
    return step


def run_projections(state, gain, rows, out_shapes):
    positions, features = state.shape
    step = row_step(positions)
    weights = (gain[None, :], rows)
    return pl.pallas_call(
        project_kernel,
        grid=(positions // step,),
        in_specs=[pl.BlockSpec((step, features), lambda i: (i, 0))] + [whole_spec(w) for w in weights],
        out_specs=[pl.BlockSpec((*shape, step), lambda i: (0, 0, i)) for shape in out_shapes],
        out_shape=[jax.ShapeDtypeStruct((*shape, positions), jnp.bfloat16) for shape in out_shapes],
        compiler_params=pltpu.CompilerParams(vmem_limit_bytes=BUDGET),
        name="project",
    )(state, *weights)


def run_finish(mixes, state, gain, gate_matrix, out_gain, final_matrix, onward=None):
    positions, features = state.shape
    step = row_step(positions)
    weights = (gain[None, :], gate_matrix, out_gain[:, None], final_matrix)
    out_shape = [jax.ShapeDtypeStruct((positions, features), jnp.bfloat16)]
    out_specs = [pl.BlockSpec((step, features), lambda i: (i, 0))]
    if onward is not None:
        next_gain, rows, out_shapes = onward
        weights += (next_gain[None, :], rows)
        out_shape += [jax.ShapeDtypeStruct((*shape, positions), jnp.bfloat16) for shape in out_shapes]
        out_specs += [pl.BlockSpec((*shape, step), lambda i: (0, 0, i)) for shape in out_shapes]
    return pl.pallas_call(
        functools.partial(finish_kernel, len(mixes), onward is not None),
        grid=(positions // step,),
        in_specs=[pl.BlockSpec((*m.shape[:2], step), lambda i: (0, 0, i)) for m in mixes]
        + [pl.BlockSpec((step, features), lambda i: (i, 0))]
        + [whole_spec(w) for w in weights],
        out_specs=out_specs,
        out_shape=out_shape,
        compiler_params=pltpu.CompilerParams(vmem_limit_bytes=BUDGET),
        name="finish",
    )(*(pltpu.with_memory_space_constraint(m, pltpu.HBM) for m in mixes), state, *weights)


class Folds:
    def __init__(self, row_count, col_count):
        turn = 1
        while (turn * col_count) % LANES:
            turn *= 2
        self.turn, self.tiles = turn, turn * col_count // LANES
        self.cols, self.rows = col_count, row_count
        self.groups = row_count // turn
        self.lane_rows = row_count * col_count // LANES

    def fits(self):
        return self.cols <= LANES and self.rows % self.turn == 0 and self.groups % 8 == 0

    def split(self, lane_rows, clear=False):
        lane = lax.broadcasted_iota(jnp.int32, lane_rows[0].shape, 1)
        out = []
        for phase in range(self.turn):
            first, offset = divmod(phase * self.cols, LANES)
            value = lane_rows[first]
            if offset + self.cols > LANES:
                value = jnp.where(lane >= offset, value, lane_rows[first + 1])
            if offset:
                value = pltpu.roll(value, LANES - offset, 1)
            out.append(jnp.where(lane < self.cols, value, 0.0) if clear else value)
        return out

    def join(self, block_rows):
        lane = lax.broadcasted_iota(jnp.int32, block_rows[0].shape, 1)
        rolled = []
        for phase, value in enumerate(block_rows):
            offset = (phase * self.cols) % LANES
            rolled.append(pltpu.roll(value, offset, 1) if offset else value)
        out = []
        for tile in range(self.tiles):
            value = None
            for phase in range(self.turn):
                begin, end = phase * self.cols - tile * LANES, (phase + 1) * self.cols - tile * LANES
                if end <= 0 or begin >= LANES:
                    continue
                value = rolled[phase] if value is None else jnp.where(lane >= begin, rolled[phase], value)
            out.append(value)
        return out


def stage(source_ref, staged):
    parts, width, positions = source_ref.shape
    rows = parts * width

    @pl.loop(0, positions // LANES, unroll=8)
    def _(tile):
        lanes = pl.ds(pl.multiple_of(tile * LANES, LANES), LANES)
        for part in range(parts):
            staged[pl.ds(tile * rows + part * width, width), :] = source_ref[part, :, lanes].astype(jnp.float32)


def unstage(staged, target_ref, earlier_refs=()):
    parts, height, positions = target_ref.shape
    width = height - sum(ref.shape[1] for ref in earlier_refs)
    rows = parts * width

    @pl.loop(0, positions // LANES, unroll=8)
    def _(tile):
        lanes = pl.ds(pl.multiple_of(tile * LANES, LANES), LANES)
        for part in range(parts):
            values = [ref[part, :, lanes].astype(jnp.float32) for ref in earlier_refs]
            values.append(staged[pl.ds(tile * rows + part * width, width), :])
            values = values[0] if len(values) == 1 else jnp.concatenate(values, axis=0)
            target_ref[part, :, lanes] = values.astype(target_ref.dtype)


def lane_rows_of(folds, rows, row):
    return [pl.ds(row + tile * rows, folds.groups, stride=folds.tiles * rows) for tile in range(folds.tiles)]


def mix_out_kernel(folds, near, cols, width, half_ref, both_ref, there_ref, *refs):
    earlier_refs, (mix_ref, staged, left, right) = refs[:-4], refs[-4:]
    parts = near * cols
    rows = parts * width
    block = folds.rows
    far = cols // near

    stage(both_ref, staged)

    @pl.loop(0, rows, unroll=8)
    def _(step):
        source, channel = step // width, step % width
        row = source * 2 * width + channel
        pieces = folds.split([staged[at, :] for at in lane_rows_of(folds, 2 * rows, row)], clear=True)
        at = (channel * cols + source % cols) * near * block + (source // cols) * block
        left[pl.ds(pl.multiple_of(at, block), block), :] = jnp.concatenate(pieces, axis=0).astype(jnp.bfloat16)

    def place(half, total, shift, height):
        @pl.loop(0, rows, unroll=8)
        def _(step):
            source, channel = step // width, step % width
            row = source * height + shift + channel
            pieces = folds.split([staged[at, :] for at in lane_rows_of(folds, total, row)])
            at = ((channel * cols + source % cols) * far + half) * near * block + (source // cols) * block
            for phase, piece in enumerate(pieces):
                right[pl.ds(at + phase, folds.groups, stride=folds.turn), :] = piece

    place(half_ref[0], 2 * rows, width, 2 * width)
    stage(there_ref, staged)
    place(half_ref[1], rows, 0, width)

    @pl.loop(0, width, unroll=1)
    def _(channel):
        tall = near * block
        lhs = jnp.concatenate(
            [left[pl.ds(pl.multiple_of((channel * cols + col) * tall, block), tall), :] for col in range(cols)], axis=1
        )
        for target in range(cols):
            starts = [((channel * cols + col) * far * near + target) * block for col in range(cols)]
            rhs = jnp.concatenate([right[pl.ds(pl.multiple_of(at, block), block), :] for at in starts], axis=1)
            total = lax.dot_general(
                lhs, rhs.astype(jnp.bfloat16), (((1,), (1,)), ((), ())), preferred_element_type=jnp.float32
            )
            total = jnp.concatenate([total, jnp.zeros((near * block, LANES - block), jnp.float32)], axis=1)
            for piece in range(near):
                groups = folds.groups
                base = piece * block
                lane_rows = folds.join(
                    [total[base + phase * groups : base + (phase + 1) * groups, :] for phase in range(folds.turn)]
                )
                out_row = (piece * cols + target) * width + channel
                for at, value in zip(lane_rows_of(folds, rows, out_row), lane_rows):
                    staged[at, :] = value

    unstage(staged, mix_ref, earlier_refs)


def mix_in_kernel(folds, near, cols, width, half_ref, both_ref, keep_ref, send_ref, staged, left, right, turned, mixed):
    parts = near * cols
    rows = 2 * parts * width
    block = folds.rows

    stage(both_ref, staged)

    for target, shift in ((left, 0), (right, width)):

        @pl.loop(0, parts * width, unroll=8)
        def _(step):
            source, channel = step // width, step % width
            row = source * 2 * width + shift + channel
            pieces = folds.split([staged[at, :] for at in lane_rows_of(folds, rows, row)])
            at = (channel * cols + source % cols) * near * block + (source // cols) * block
            target[pl.ds(pl.multiple_of(at, block), block), :] = jnp.concatenate(pieces, axis=0).astype(jnp.bfloat16)

    out_rows = parts * width
    tall = near * block

    @pl.loop(0, width, unroll=1)
    def _(channel):
        rhs = jnp.concatenate(
            [right[pl.ds(pl.multiple_of((channel * cols + col) * tall, block), tall), :] for col in range(cols)], axis=1
        )
        for upper in range(cols):
            lhs = left[pl.ds(pl.multiple_of((channel * cols + upper) * tall, block), tall), :]
            summed = lax.dot_general(lhs, rhs, (((0,), (0,)), ((), ())), preferred_element_type=jnp.float32)
            half, piece = divmod(upper, near)
            for target in range(cols):
                turned[upper, target] = summed[:, target * LANES : (target + 1) * LANES]
                lane_rows = folds.join(
                    [turned[upper, target, pl.ds(phase, folds.groups, stride=folds.turn), :] for phase in range(folds.turn)]
                )
                out_row = (piece * cols + target) * width + channel
                for at, value in zip(lane_rows_of(folds, out_rows, out_row), lane_rows):
                    mixed[half, at, :] = value

    unstage(mixed.at[half_ref[0]], keep_ref)
    unstage(mixed.at[half_ref[1]], send_ref)


SMEM_SPEC = pl.BlockSpec(memory_space=pltpu.SMEM)
VMEM_SPEC = pl.BlockSpec(memory_space=pltpu.VMEM)


def run_mix_out(folds, near, cols, halves, both, there, earlier=()):
    parts, width, positions = there.shape
    rows = parts * width
    block = folds.rows
    return pl.pallas_call(
        functools.partial(mix_out_kernel, folds, near, cols, width),
        in_specs=[SMEM_SPEC] + [VMEM_SPEC] * (2 + len(earlier)),
        out_specs=VMEM_SPEC,
        out_shape=jax.ShapeDtypeStruct((parts, width + sum(e.shape[1] for e in earlier), positions), jnp.bfloat16),
        scratch_shapes=[
            pltpu.VMEM((2 * rows * folds.lane_rows, LANES), jnp.float32),
            pltpu.VMEM((width * cols * near * block, LANES), jnp.bfloat16),
            pltpu.VMEM((width * cols * cols * block, LANES), jnp.float32),
        ],
        compiler_params=pltpu.CompilerParams(vmem_limit_bytes=BUDGET),
        name="mix_out",
    )(halves, both, there, *earlier)


def add_kernel(*refs):
    target_ref = refs[-1]
    parts = target_ref.shape[0]
    for part in range(parts):
        sums = [kept[part] + got[part].astype(jnp.float32) for kept, got in zip(refs[:-1:2], refs[1:-1:2])]
        target_ref[part] = jnp.concatenate(sums, axis=0).astype(target_ref.dtype)


def run_add(*arrays):
    parts, _, positions = arrays[0].shape
    step = row_step(positions)
    height = sum(array.shape[1] for array in arrays) // 2
    return pl.pallas_call(
        add_kernel,
        grid=(positions // step,),
        in_specs=[pl.BlockSpec((*array.shape[:2], step), lambda i: (0, 0, i)) for array in arrays],
        out_specs=pl.BlockSpec((parts, height, step), lambda i: (0, 0, i)),
        out_shape=jax.ShapeDtypeStruct((parts, height, positions), jnp.bfloat16),
        compiler_params=pltpu.CompilerParams(vmem_limit_bytes=BUDGET),
        name="add",
    )(*arrays)


def run_mix_in(folds, near, cols, halves, both):
    parts, width, positions = both.shape
    rows, width = parts * width, width // 2
    block = folds.rows
    return pl.pallas_call(
        functools.partial(mix_in_kernel, folds, near, cols, width),
        in_specs=[SMEM_SPEC, VMEM_SPEC],
        out_specs=[VMEM_SPEC, VMEM_SPEC],
        out_shape=[
            jax.ShapeDtypeStruct((parts, width, positions), jnp.float32),
            jax.ShapeDtypeStruct((parts, width, positions), jnp.bfloat16),
        ],
        scratch_shapes=[
            pltpu.VMEM((rows * folds.lane_rows, LANES), jnp.float32),
            pltpu.VMEM((width * cols * near * block, LANES), jnp.bfloat16),
            pltpu.VMEM((width * cols * near * block, LANES), jnp.bfloat16),
            pltpu.VMEM((cols, cols, LANES, LANES), jnp.float32),
            pltpu.VMEM((2, rows // 2 * folds.lane_rows, LANES), jnp.float32),
        ],
        compiler_params=pltpu.CompilerParams(vmem_limit_bytes=BUDGET),
        name="mix_in",
    )(halves, both)


SHARES = (1, 2, 2, 2, 1)
GROUPS = ((1, 2), (0, 3, 4))
PIECES = len(SHARES)


def exchange(array):
    return lax.all_to_all(array, EVERY, split_axis=0, concat_axis=0, tiled=True)


def across(array):
    return lax.ppermute(array, "far", ((0, 1), (1, 0)))


def in_halves(sizes, pair_input, weights):
    _, near, cols = sizes
    row_count, col_count, features = pair_input.shape
    parts = near * cols
    width = features // parts
    ends = [sum(SHARES[: at + 1]) * width // sum(SHARES) for at in range(PIECES)]
    begins = [0] + ends[:-1]
    folds = Folds(row_count, col_count)
    half = lax.axis_index("far")
    halves = jnp.stack([half, 1 - half]).astype(jnp.int32)

    def rows_of(project, *chosen):
        ga, va, gb, vb = (rows.reshape(parts, width, features) for rows in jnp.split(project.T, 4, axis=0))

        def ordered(left, right):
            rows = [array[:, begins[piece] : ends[piece]] for piece in chosen for array in (left, right)]
            pairs = [jnp.concatenate(rows[at : at + 2], axis=1).reshape(-1, features) for at in range(0, len(rows), 2)]
            return pairs

        return jnp.concatenate(ordered(ga, gb) + ordered(va, vb))

    def in_groups(array):
        rows = array.reshape(parts, width, -1)
        ordered = [
            jnp.concatenate([rows[:, begins[piece] : ends[piece]] for piece in group], axis=1).reshape(-1, rows.shape[-1])
            for group in GROUPS
        ]
        return jnp.concatenate(ordered).reshape(array.shape)

    gain_1, project_1, gate_1, norm_1, final_1, gain_2, project_2, gate_2, norm_2, final_2 = weights
    state = pair_input.reshape(-1, features)

    shapes = [(parts, 2 * (end - begin)) for begin, end in zip(begins, ends)]
    rest = range(1, PIECES)
    both, mixed, mixes = [], [None] * PIECES, []
    out = run_projections(state, gain_1, rows_of(project_1, 0), shapes[:1])
    out += run_projections(state, gain_1, rows_of(project_1, *rest), shapes[1:])
    for piece in range(PIECES):
        both.append(exchange(out[piece]))
    for piece in range(PIECES):
        group = next(group for group in GROUPS if piece in group)
        there = across(both[piece][:, both[piece].shape[1] // 2 :, :])
        earlier = [mixed[other] for other in group[:-1]] if piece == group[-1] else ()
        mixed[piece] = run_mix_out(folds, near, cols, halves, both[piece], there, earlier)
        if piece == group[-1]:
            mixes.append(exchange(mixed[piece]))
    onward = (gain_2, rows_of(project_2, 0), shapes[:1])
    middle, *out = run_finish(mixes, state, gain_1, gate_1, in_groups(norm_1), in_groups(final_1), onward)
    out += run_projections(middle, gain_2, rows_of(project_2, *rest), shapes[1:])
    both, parted, mixes = [], [], []
    for piece in range(PIECES):
        both.append(exchange(out[piece]))
    for piece in range(PIECES):
        kept, sent = run_mix_in(folds, near, cols, halves, both[piece])
        parted.append((kept, across(sent)))
    for group in GROUPS:
        summed = run_add(*(array for piece in group for array in parted[piece]))
        mixes.append(exchange(summed))
    result = run_finish(mixes, middle, gain_2, gate_2, in_groups(norm_2), in_groups(final_2))[0]
    return result.reshape(pair_input.shape)


def solution(mesh):
    row_parts, col_parts = mesh.shape["dap"], mesh.shape["chan"] * mesh.shape["sub"]

    def whole(pair_input, *weights):
        features = pair_input.shape[-1]
        block_rows = pair_input.shape[0] // (mesh.shape["groups"] * row_parts)
        block_cols = pair_input.shape[1] // col_parts
        halved = (
            row_parts % 2 == 0
            and row_parts == col_parts
            and block_rows == block_cols
            and Folds(block_rows, block_cols).fits()
            and features == LANES
            and features % (row_parts // 2 * col_parts * sum(SHARES)) == 0
        )
        if halved:
            far, near = 2, row_parts // 2
        else:
            far, near = split_rows(row_parts, col_parts, features, 8)
        sizes = (far, near, col_parts)
        finer = Mesh(
            mesh.devices.reshape(mesh.shape["groups"], far, near, mesh.shape["chan"], mesh.shape["sub"]),
            ("groups", "far", "near", "chan", "sub"),
        )

        def shards(pair_input, *weights):
            if halved:
                return in_halves(sizes, pair_input, weights)
            middle = update(False, sizes, pair_input, *weights[:5])
            return update(True, sizes, middle, *weights[5:])

        pair_spec = P(("groups", "far", "near"), ("chan", "sub"), None)
        mapped = jax.shard_map(
            shards,
            mesh=finer,
            in_specs=(pair_spec,) + (P(),) * 10,
            out_specs=pair_spec,
            check_vma=False,
        )
        return mapped(pair_input, *weights)

    return whole
```

```python
import functools

import jax
import jax.numpy as jnp
from jax import lax
from jax.experimental import pallas as pl
from jax.experimental.pallas import tpu as pltpu
from jax.sharding import Mesh
from jax.sharding import PartitionSpec as P


epsilon = 1e-05
EVERY = ("near", "chan", "sub")
LANES = 128
BUDGET = 56 << 20


def layer_norm(values, norm_gain, reduce_axis):
    average = jnp.mean(values, axis=reduce_axis, keepdims=True)
    centred = values - average
    variance = jnp.mean(centred * centred, axis=reduce_axis, keepdims=True)
    return centred * lax.rsqrt(variance + epsilon) * norm_gain


def sigmoid(values):
    return 0.5 * jnp.tanh(0.5 * values) + 0.5


def project_in(pair_state, norm_gain, project, gate_matrix):
    features = pair_state.shape[-1]
    flattened = pair_state.reshape(-1, features).astype(jnp.float32)
    normed = layer_norm(flattened, norm_gain, 1).astype(jnp.bfloat16)
    projected = jnp.einsum("xc,cd->dx", normed, project, preferred_element_type=jnp.float32)
    left_part = jax.nn.sigmoid(projected[:features]) * projected[features : 2 * features]
    right_part = jax.nn.sigmoid(projected[2 * features : 3 * features]) * projected[3 * features :]
    gating = jax.nn.sigmoid(jnp.dot(normed, gate_matrix, preferred_element_type=jnp.float32))
    return left_part.astype(jnp.bfloat16), right_part.astype(jnp.bfloat16), gating


def finish(pair_state, mixture, gating, out_gain, final_matrix):
    features = mixture.shape[0]
    flattened = mixture.astype(jnp.float32)
    normed = layer_norm(flattened, out_gain[:, None], 0).astype(jnp.bfloat16)
    update = jnp.einsum("cx,cd->xd", normed, final_matrix, preferred_element_type=jnp.float32)
    result = pair_state.reshape(-1, features).astype(jnp.float32) + gating * update
    return result.astype(jnp.bfloat16).reshape(pair_state.shape)


def update(incoming, sizes, pair_state, norm_gain, project, gate_matrix, out_gain, final_matrix):
    far, near, col_parts = sizes
    row_count, col_count, features = pair_state.shape
    parts = near * col_parts
    width = features // parts
    left_part, right_part, gating = project_in(pair_state, norm_gain, project, gate_matrix)
    both = jnp.stack([left_part.reshape(parts, width, -1), right_part.reshape(parts, width, -1)], axis=1)
    both = lax.all_to_all(both, EVERY, split_axis=0, concat_axis=0, tiled=True)
    both = both.reshape(near, col_parts, 2, width, row_count, col_count)
    both = both.transpose(2, 3, 0, 4, 1, 5).reshape(2, width, near * row_count, col_parts * col_count)
    left_part, right_part = both[0], both[1]
    if incoming:
        mixture = jnp.einsum("cki,ckj->cij", left_part, right_part, preferred_element_type=jnp.float32)
        if far > 1:
            mixture = lax.psum_scatter(mixture, "far", scatter_dimension=1, tiled=True)
    else:
        if far > 1:
            right_part = lax.all_gather(right_part, "far", axis=1, tiled=True)
        mixture = jnp.einsum("cik,cjk->cij", left_part, right_part, preferred_element_type=jnp.float32)
    mixture = mixture.astype(jnp.bfloat16).reshape(width, near, row_count, col_parts, col_count)
    mixture = mixture.transpose(1, 3, 0, 2, 4).reshape(parts, width, row_count * col_count)
    mixture = lax.all_to_all(mixture, EVERY, split_axis=0, concat_axis=0, tiled=True)
    return finish(pair_state, mixture.reshape(features, -1), gating, out_gain, final_matrix)


def split_rows(row_parts, col_parts, features, least):
    near = row_parts
    while near > 1 and (row_parts % near or features % (near * col_parts) or features < least * near * col_parts):
        near -= 1
    return row_parts // near, near


def emit_projections(normed, rows_ref, out_refs):
    step = normed.shape[0]
    half = rows_ref.shape[0] // 2
    group = 256 if step % 256 == 0 else LANES
    for begin in range(0, step, group):
        projected = lax.dot_general(
            rows_ref[...], normed[begin : begin + group, :], (((1,), (1,)), ((), ())), preferred_element_type=jnp.float32
        )
        gated = sigmoid(projected[:half, :]) * projected[half:, :]
        at = 0
        for ref in out_refs:
            parts, width, _ = ref.shape
            for part in range(parts):
                ref[part, :, begin : begin + group] = gated[at : at + width, :].astype(ref.dtype)
                at += width


def project_kernel(state_ref, gain_ref, rows_ref, *out_refs):
    normed = layer_norm(state_ref[...].astype(jnp.float32), gain_ref[...], 1).astype(jnp.bfloat16)
    emit_projections(normed, rows_ref, out_refs)


def finish_kernel(pieces, onward, *refs):
    mix_refs, refs = refs[:pieces], refs[pieces:]
    state_ref, gain_ref, gate_ref, out_gain_ref, final_ref = refs[:5]
    state = state_ref[...].astype(jnp.float32)
    normed = layer_norm(state, gain_ref[...], 1).astype(jnp.bfloat16)
    gating = sigmoid(jnp.dot(normed, gate_ref[...], preferred_element_type=jnp.float32))
    mixed = jnp.concatenate(
        [ref[part].astype(jnp.float32) for ref in mix_refs for part in range(ref.shape[0])], axis=0
    )
    mixed = layer_norm(mixed, out_gain_ref[...], 0).astype(jnp.bfloat16)
    change = lax.dot_general(
        mixed, final_ref[...], (((0,), (0,)), ((), ())), preferred_element_type=jnp.float32
    )
    result = (state + gating * change).astype(jnp.bfloat16)
    if onward:
        next_gain, rows_ref, middle_ref = refs[5:8]
        middle_ref[...] = result
        normed = layer_norm(result.astype(jnp.float32), next_gain[...], 1).astype(jnp.bfloat16)
        emit_projections(normed, rows_ref, refs[8:])
    else:
        refs[5][...] = result


def whole_spec(array):
    return pl.BlockSpec(array.shape, lambda step: (0,) * array.ndim)


def row_step(positions):
    step = positions
    for candidate in range(LANES, 2304 + 1, LANES):
        if positions % candidate == 0:
            step = candidate
    return step


def run_projections(state, gain, rows, out_shapes):
    positions, features = state.shape
    step = row_step(positions)
    weights = (gain[None, :], rows)
    return pl.pallas_call(
        project_kernel,
        grid=(positions // step,),
        in_specs=[pl.BlockSpec((step, features), lambda i: (i, 0))] + [whole_spec(w) for w in weights],
        out_specs=[pl.BlockSpec((*shape, step), lambda i: (0, 0, i)) for shape in out_shapes],
        out_shape=[jax.ShapeDtypeStruct((*shape, positions), jnp.bfloat16) for shape in out_shapes],
        compiler_params=pltpu.CompilerParams(vmem_limit_bytes=BUDGET),
        name="project",
    )(state, *weights)


def run_finish(mixes, state, gain, gate_matrix, out_gain, final_matrix, onward=None):
    positions, features = state.shape
    step = row_step(positions)
    weights = (gain[None, :], gate_matrix, out_gain[:, None], final_matrix)
    out_shape = [jax.ShapeDtypeStruct((positions, features), jnp.bfloat16)]
    out_specs = [pl.BlockSpec((step, features), lambda i: (i, 0))]
    if onward is not None:
        next_gain, rows, out_shapes = onward
        weights += (next_gain[None, :], rows)
        out_shape += [jax.ShapeDtypeStruct((*shape, positions), jnp.bfloat16) for shape in out_shapes]
        out_specs += [pl.BlockSpec((*shape, step), lambda i: (0, 0, i)) for shape in out_shapes]
    return pl.pallas_call(
        functools.partial(finish_kernel, len(mixes), onward is not None),
        grid=(positions // step,),
        in_specs=[pl.BlockSpec((*m.shape[:2], step), lambda i: (0, 0, i)) for m in mixes]
        + [pl.BlockSpec((step, features), lambda i: (i, 0))]
        + [whole_spec(w) for w in weights],
        out_specs=out_specs,
        out_shape=out_shape,
        compiler_params=pltpu.CompilerParams(vmem_limit_bytes=BUDGET),
        name="finish",
    )(*(pltpu.with_memory_space_constraint(m, pltpu.HBM) for m in mixes), state, *weights)


class Folds:
    def __init__(self, row_count, col_count):
        turn = 1
        while (turn * col_count) % LANES:
            turn *= 2
        self.turn, self.tiles = turn, turn * col_count // LANES
        self.cols, self.rows = col_count, row_count
        self.groups = row_count // turn
        self.lane_rows = row_count * col_count // LANES

    def fits(self):
        return self.cols <= LANES and self.rows % self.turn == 0 and self.groups % 8 == 0

    def split(self, lane_rows, clear=False):
        lane = lax.broadcasted_iota(jnp.int32, lane_rows[0].shape, 1)
        out = []
        for phase in range(self.turn):
            first, offset = divmod(phase * self.cols, LANES)
            value = lane_rows[first]
            if offset + self.cols > LANES:
                value = jnp.where(lane >= offset, value, lane_rows[first + 1])
            if offset:
                value = pltpu.roll(value, LANES - offset, 1)
            out.append(jnp.where(lane < self.cols, value, 0.0) if clear else value)
        return out

    def join(self, block_rows):
        lane = lax.broadcasted_iota(jnp.int32, block_rows[0].shape, 1)
        rolled = []
        for phase, value in enumerate(block_rows):
            offset = (phase * self.cols) % LANES
            rolled.append(pltpu.roll(value, offset, 1) if offset else value)
        out = []
        for tile in range(self.tiles):
            value = None
            for phase in range(self.turn):
                begin, end = phase * self.cols - tile * LANES, (phase + 1) * self.cols - tile * LANES
                if end <= 0 or begin >= LANES:
                    continue
                value = rolled[phase] if value is None else jnp.where(lane >= begin, rolled[phase], value)
            out.append(value)
        return out


def stage(source_ref, staged):
    parts, width, positions = source_ref.shape
    rows = parts * width

    @pl.loop(0, positions // LANES, unroll=8)
    def _(tile):
        lanes = pl.ds(pl.multiple_of(tile * LANES, LANES), LANES)
        for part in range(parts):
            staged[pl.ds(tile * rows + part * width, width), :] = source_ref[part, :, lanes].astype(jnp.float32)


def unstage(staged, target_ref, earlier_refs=()):
    parts, height, positions = target_ref.shape
    width = height - sum(ref.shape[1] for ref in earlier_refs)
    rows = parts * width

    @pl.loop(0, positions // LANES, unroll=8)
    def _(tile):
        lanes = pl.ds(pl.multiple_of(tile * LANES, LANES), LANES)
        for part in range(parts):
            values = [ref[part, :, lanes].astype(jnp.float32) for ref in earlier_refs]
            values.append(staged[pl.ds(tile * rows + part * width, width), :])
            values = values[0] if len(values) == 1 else jnp.concatenate(values, axis=0)
            target_ref[part, :, lanes] = values.astype(target_ref.dtype)


def lane_rows_of(folds, rows, row):
    return [pl.ds(row + tile * rows, folds.groups, stride=folds.tiles * rows) for tile in range(folds.tiles)]


def mix_out_kernel(folds, near, cols, width, half_ref, left_ref, right_ref, there_ref, *refs):
    earlier_refs, (mix_ref, staged, left, right) = refs[:-4], refs[-4:]
    parts = near * cols
    rows = parts * width
    block = folds.rows
    far = cols // near

    def unfold(ref, shift, store):
        height = ref.shape[1]
        stage(ref, staged)

        @pl.loop(0, rows, unroll=8)
        def _(step):
            source, channel = step // width, step % width
            row = source * height + shift + channel
            store(source, channel, [staged[at, :] for at in lane_rows_of(folds, parts * height, row)])

    def store_left(source, channel, lane_rows):
        pieces = folds.split(lane_rows, clear=True)
        at = (channel * cols + source % cols) * near * block + (source // cols) * block
        left[pl.ds(pl.multiple_of(at, block), block), :] = jnp.concatenate(pieces, axis=0).astype(jnp.bfloat16)

    def store_right(half):
        def store(source, channel, lane_rows):
            at = ((channel * cols + source % cols) * far + half) * near * block + (source // cols) * block
            for phase, piece in enumerate(folds.split(lane_rows)):
                right[pl.ds(at + phase, folds.groups, stride=folds.turn), :] = piece

        return store

    unfold(left_ref, 0, store_left)
    unfold(right_ref, right_ref.shape[1] - width, store_right(half_ref[0]))
    unfold(there_ref, 0, store_right(half_ref[1]))

    @pl.loop(0, width, unroll=1)
    def _(channel):
        tall = near * block
        lhs = jnp.concatenate(
            [left[pl.ds(pl.multiple_of((channel * cols + col) * tall, block), tall), :] for col in range(cols)], axis=1
        )
        for target in range(cols):
            starts = [((channel * cols + col) * far * near + target) * block for col in range(cols)]
            rhs = jnp.concatenate([right[pl.ds(pl.multiple_of(at, block), block), :] for at in starts], axis=1)
            total = lax.dot_general(
                lhs, rhs.astype(jnp.bfloat16), (((1,), (1,)), ((), ())), preferred_element_type=jnp.float32
            )
            total = jnp.concatenate([total, jnp.zeros((near * block, LANES - block), jnp.float32)], axis=1)
            for piece in range(near):
                groups = folds.groups
                base = piece * block
                lane_rows = folds.join(
                    [total[base + phase * groups : base + (phase + 1) * groups, :] for phase in range(folds.turn)]
                )
                out_row = (piece * cols + target) * width + channel
                for at, value in zip(lane_rows_of(folds, rows, out_row), lane_rows):
                    staged[at, :] = value

    unstage(staged, mix_ref, earlier_refs)


def mix_in_kernel(folds, near, cols, width, half_ref, both_ref, keep_ref, send_ref, staged, left, right, turned, mixed):
    parts = near * cols
    rows = 2 * parts * width
    block = folds.rows

    stage(both_ref, staged)

    for target, shift in ((left, 0), (right, width)):

        @pl.loop(0, parts * width, unroll=8)
        def _(step):
            source, channel = step // width, step % width
            row = source * 2 * width + shift + channel
            pieces = folds.split([staged[at, :] for at in lane_rows_of(folds, rows, row)])
            at = (channel * cols + source % cols) * near * block + (source // cols) * block
            target[pl.ds(pl.multiple_of(at, block), block), :] = jnp.concatenate(pieces, axis=0).astype(jnp.bfloat16)

    out_rows = parts * width
    tall = near * block

    @pl.loop(0, width, unroll=1)
    def _(channel):
        rhs = jnp.concatenate(
            [right[pl.ds(pl.multiple_of((channel * cols + col) * tall, block), tall), :] for col in range(cols)], axis=1
        )
        for upper in range(cols):
            lhs = left[pl.ds(pl.multiple_of((channel * cols + upper) * tall, block), tall), :]
            summed = lax.dot_general(lhs, rhs, (((0,), (0,)), ((), ())), preferred_element_type=jnp.float32)
            half, piece = divmod(upper, near)
            for target in range(cols):
                turned[upper, target] = summed[:, target * LANES : (target + 1) * LANES]
                lane_rows = folds.join(
                    [turned[upper, target, pl.ds(phase, folds.groups, stride=folds.turn), :] for phase in range(folds.turn)]
                )
                out_row = (piece * cols + target) * width + channel
                for at, value in zip(lane_rows_of(folds, out_rows, out_row), lane_rows):
                    mixed[half, at, :] = value

    unstage(mixed.at[half_ref[0]], keep_ref)
    unstage(mixed.at[half_ref[1]], send_ref)


SMEM_SPEC = pl.BlockSpec(memory_space=pltpu.SMEM)
VMEM_SPEC = pl.BlockSpec(memory_space=pltpu.VMEM)


def run_mix_out(folds, near, cols, halves, left, right, there, earlier=()):
    parts, width, positions = there.shape
    rows = parts * width
    block = folds.rows
    return pl.pallas_call(
        functools.partial(mix_out_kernel, folds, near, cols, width),
        in_specs=[SMEM_SPEC] + [VMEM_SPEC] * (3 + len(earlier)),
        out_specs=VMEM_SPEC,
        out_shape=jax.ShapeDtypeStruct((parts, width + sum(e.shape[1] for e in earlier), positions), jnp.bfloat16),
        scratch_shapes=[
            pltpu.VMEM((2 * rows * folds.lane_rows, LANES), jnp.float32),
            pltpu.VMEM((width * cols * near * block, LANES), jnp.bfloat16),
            pltpu.VMEM((width * cols * cols * block, LANES), jnp.float32),
        ],
        compiler_params=pltpu.CompilerParams(vmem_limit_bytes=BUDGET),
        name="mix_out",
    )(halves, left, right, there, *earlier)


def add_kernel(*refs):
    target_ref = refs[-1]
    parts = target_ref.shape[0]
    for part in range(parts):
        sums = [kept[part] + got[part].astype(jnp.float32) for kept, got in zip(refs[:-1:2], refs[1:-1:2])]
        target_ref[part] = jnp.concatenate(sums, axis=0).astype(target_ref.dtype)


def run_add(*arrays):
    parts, _, positions = arrays[0].shape
    step = row_step(positions)
    height = sum(array.shape[1] for array in arrays) // 2
    return pl.pallas_call(
        add_kernel,
        grid=(positions // step,),
        in_specs=[pl.BlockSpec((*array.shape[:2], step), lambda i: (0, 0, i)) for array in arrays],
        out_specs=pl.BlockSpec((parts, height, step), lambda i: (0, 0, i)),
        out_shape=jax.ShapeDtypeStruct((parts, height, positions), jnp.bfloat16),
        compiler_params=pltpu.CompilerParams(vmem_limit_bytes=BUDGET),
        name="add",
    )(*arrays)


def run_mix_in(folds, near, cols, halves, both):
    parts, width, positions = both.shape
    rows, width = parts * width, width // 2
    block = folds.rows
    return pl.pallas_call(
        functools.partial(mix_in_kernel, folds, near, cols, width),
        in_specs=[SMEM_SPEC, VMEM_SPEC],
        out_specs=[VMEM_SPEC, VMEM_SPEC],
        out_shape=[
            jax.ShapeDtypeStruct((parts, width, positions), jnp.float32),
            jax.ShapeDtypeStruct((parts, width, positions), jnp.bfloat16),
        ],
        scratch_shapes=[
            pltpu.VMEM((rows * folds.lane_rows, LANES), jnp.float32),
            pltpu.VMEM((width * cols * near * block, LANES), jnp.bfloat16),
            pltpu.VMEM((width * cols * near * block, LANES), jnp.bfloat16),
            pltpu.VMEM((cols, cols, LANES, LANES), jnp.float32),
            pltpu.VMEM((2, rows // 2 * folds.lane_rows, LANES), jnp.float32),
        ],
        compiler_params=pltpu.CompilerParams(vmem_limit_bytes=BUDGET),
        name="mix_in",
    )(halves, both)


SHARES = (1, 1, 1, 1)
GROUPS = ((0, 1), (2, 3))
PIECES = len(SHARES)


def exchange(array):
    return lax.all_to_all(array, EVERY, split_axis=0, concat_axis=0, tiled=True)


def across(array):
    return lax.ppermute(array, "far", ((0, 1), (1, 0)))


def in_halves(sizes, pair_input, weights):
    _, near, cols = sizes
    row_count, col_count, features = pair_input.shape
    parts = near * cols
    width = features // parts
    ends = [sum(SHARES[: at + 1]) * width // sum(SHARES) for at in range(PIECES)]
    begins = [0] + ends[:-1]
    folds = Folds(row_count, col_count)
    half = lax.axis_index("far")
    halves = jnp.stack([half, 1 - half]).astype(jnp.int32)

    def rows_of(project, *arrays):
        ga, va, gb, vb = (rows.reshape(parts, width, features) for rows in jnp.split(project.T, 4, axis=0))

        def ordered(left, right):
            return [
                jnp.concatenate(
                    [rows[:, begins[piece] : ends[piece]] for rows, piece in zip((left, right), pair) if piece is not None],
                    axis=1,
                ).reshape(-1, features)
                for pair in arrays
            ]

        return jnp.concatenate(ordered(ga, gb) + ordered(va, vb))

    def shapes_of(*arrays):
        return [
            (parts, sum(ends[piece] - begins[piece] for piece in pair if piece is not None)) for pair in arrays
        ]

    def in_groups(array):
        rows = array.reshape(parts, width, -1)
        ordered = [
            jnp.concatenate([rows[:, begins[piece] : ends[piece]] for piece in group], axis=1).reshape(-1, rows.shape[-1])
            for group in GROUPS
        ]
        return jnp.concatenate(ordered).reshape(array.shape)

    gain_1, project_1, gate_1, norm_1, final_1, gain_2, project_2, gate_2, norm_2, final_2 = weights
    state = pair_input.reshape(-1, features)

    ahead = [(None, 0)] + [(piece, piece + 1) for piece in range(PIECES - 1)] + [(PIECES - 1, None)]
    level = [(piece, piece) for piece in range(PIECES)]
    sent, mixed, mixes = [], [None] * PIECES, []
    out = run_projections(state, gain_1, rows_of(project_1, *ahead[:1]), shapes_of(*ahead[:1]))
    out += run_projections(state, gain_1, rows_of(project_1, *ahead[1:]), shapes_of(*ahead[1:]))
    for array in out:
        sent.append(exchange(array))
    for piece in range(PIECES):
        group = next(group for group in GROUPS if piece in group)
        right, left = sent[piece], sent[piece + 1]
        there = across(right[:, right.shape[1] - (ends[piece] - begins[piece]) :, :])
        earlier = [mixed[other] for other in group[:-1]] if piece == group[-1] else ()
        mixed[piece] = run_mix_out(folds, near, cols, halves, left, right, there, earlier)
        if piece == group[-1]:
            mixes.append(exchange(mixed[piece]))
    onward = (gain_2, rows_of(project_2, *level[:1]), shapes_of(*level[:1]))
    middle, *out = run_finish(mixes, state, gain_1, gate_1, in_groups(norm_1), in_groups(final_1), onward)
    out += run_projections(middle, gain_2, rows_of(project_2, *level[1:]), shapes_of(*level[1:]))
    both, parted, mixes = [], [], []
    for piece in range(PIECES):
        both.append(exchange(out[piece]))
    for piece in range(PIECES):
        kept, sent = run_mix_in(folds, near, cols, halves, both[piece])
        parted.append((kept, across(sent)))
    for group in GROUPS:
        summed = run_add(*(array for piece in group for array in parted[piece]))
        mixes.append(exchange(summed))
    result = run_finish(mixes, middle, gain_2, gate_2, in_groups(norm_2), in_groups(final_2))[0]
    return result.reshape(pair_input.shape)


def solution(mesh):
    row_parts, col_parts = mesh.shape["dap"], mesh.shape["chan"] * mesh.shape["sub"]

    def whole(pair_input, *weights):
        features = pair_input.shape[-1]
        block_rows = pair_input.shape[0] // (mesh.shape["groups"] * row_parts)
        block_cols = pair_input.shape[1] // col_parts
        halved = (
            row_parts % 2 == 0
            and row_parts == col_parts
            and block_rows == block_cols
            and Folds(block_rows, block_cols).fits()
            and features == LANES
            and features % (row_parts // 2 * col_parts * sum(SHARES)) == 0
        )
        if halved:
            far, near = 2, row_parts // 2
        else:
            far, near = split_rows(row_parts, col_parts, features, 8)
        sizes = (far, near, col_parts)
        finer = Mesh(
            mesh.devices.reshape(mesh.shape["groups"], far, near, mesh.shape["chan"], mesh.shape["sub"]),
            ("groups", "far", "near", "chan", "sub"),
        )

        def shards(pair_input, *weights):
            if halved:
                return in_halves(sizes, pair_input, weights)
            middle = update(False, sizes, pair_input, *weights[:5])
            return update(True, sizes, middle, *weights[5:])

        pair_spec = P(("groups", "far", "near"), ("chan", "sub"), None)
        mapped = jax.shard_map(
            shards,
            mesh=finer,
            in_specs=(pair_spec,) + (P(),) * 10,
            out_specs=pair_spec,
            check_vma=False,
        )
        return mapped(pair_input, *weights)

    return whole
```

```python
import functools

import jax
import jax.numpy as jnp
from jax import lax
from jax.experimental import pallas as pl
from jax.experimental.pallas import tpu as pltpu
from jax.sharding import Mesh
from jax.sharding import PartitionSpec as P


epsilon = 1e-05
EVERY = ("near", "chan", "sub")
LANES = 128
BUDGET = 56 << 20


def layer_norm(values, norm_gain, reduce_axis):
    average = jnp.mean(values, axis=reduce_axis, keepdims=True)
    centred = values - average
    variance = jnp.mean(centred * centred, axis=reduce_axis, keepdims=True)
    return centred * lax.rsqrt(variance + epsilon) * norm_gain


def sigmoid(values):
    return 0.5 * jnp.tanh(0.5 * values) + 0.5


def project_in(pair_state, norm_gain, project, gate_matrix):
    features = pair_state.shape[-1]
    flattened = pair_state.reshape(-1, features).astype(jnp.float32)
    normed = layer_norm(flattened, norm_gain, 1).astype(jnp.bfloat16)
    projected = jnp.einsum("xc,cd->dx", normed, project, preferred_element_type=jnp.float32)
    left_part = jax.nn.sigmoid(projected[:features]) * projected[features : 2 * features]
    right_part = jax.nn.sigmoid(projected[2 * features : 3 * features]) * projected[3 * features :]
    gating = jax.nn.sigmoid(jnp.dot(normed, gate_matrix, preferred_element_type=jnp.float32))
    return left_part.astype(jnp.bfloat16), right_part.astype(jnp.bfloat16), gating


def finish(pair_state, mixture, gating, out_gain, final_matrix):
    features = mixture.shape[0]
    flattened = mixture.astype(jnp.float32)
    normed = layer_norm(flattened, out_gain[:, None], 0).astype(jnp.bfloat16)
    update = jnp.einsum("cx,cd->xd", normed, final_matrix, preferred_element_type=jnp.float32)
    result = pair_state.reshape(-1, features).astype(jnp.float32) + gating * update
    return result.astype(jnp.bfloat16).reshape(pair_state.shape)


def update(incoming, sizes, pair_state, norm_gain, project, gate_matrix, out_gain, final_matrix):
    far, near, col_parts = sizes
    row_count, col_count, features = pair_state.shape
    parts = near * col_parts
    width = features // parts
    left_part, right_part, gating = project_in(pair_state, norm_gain, project, gate_matrix)
    both = jnp.stack([left_part.reshape(parts, width, -1), right_part.reshape(parts, width, -1)], axis=1)
    both = lax.all_to_all(both, EVERY, split_axis=0, concat_axis=0, tiled=True)
    both = both.reshape(near, col_parts, 2, width, row_count, col_count)
    both = both.transpose(2, 3, 0, 4, 1, 5).reshape(2, width, near * row_count, col_parts * col_count)
    left_part, right_part = both[0], both[1]
    if incoming:
        mixture = jnp.einsum("cki,ckj->cij", left_part, right_part, preferred_element_type=jnp.float32)
        if far > 1:
            mixture = lax.psum_scatter(mixture, "far", scatter_dimension=1, tiled=True)
    else:
        if far > 1:
            right_part = lax.all_gather(right_part, "far", axis=1, tiled=True)
        mixture = jnp.einsum("cik,cjk->cij", left_part, right_part, preferred_element_type=jnp.float32)
    mixture = mixture.astype(jnp.bfloat16).reshape(width, near, row_count, col_parts, col_count)
    mixture = mixture.transpose(1, 3, 0, 2, 4).reshape(parts, width, row_count * col_count)
    mixture = lax.all_to_all(mixture, EVERY, split_axis=0, concat_axis=0, tiled=True)
    return finish(pair_state, mixture.reshape(features, -1), gating, out_gain, final_matrix)


def split_rows(row_parts, col_parts, features, least):
    near = row_parts
    while near > 1 and (row_parts % near or features % (near * col_parts) or features < least * near * col_parts):
        near -= 1
    return row_parts // near, near


def emit_projections(normed, rows_ref, out_refs):
    step = normed.shape[0]
    half = rows_ref.shape[0] // 2
    group = 256 if step % 256 == 0 else LANES
    for begin in range(0, step, group):
        projected = lax.dot_general(
            rows_ref[...], normed[begin : begin + group, :], (((1,), (1,)), ((), ())), preferred_element_type=jnp.float32
        )
        gated = sigmoid(projected[:half, :]) * projected[half:, :]
        at = 0
        for ref in out_refs:
            parts, width, _ = ref.shape
            for part in range(parts):
                ref[part, :, begin : begin + group] = gated[at : at + width, :].astype(ref.dtype)
                at += width


def project_kernel(state_ref, gain_ref, rows_ref, *out_refs):
    normed = layer_norm(state_ref[...].astype(jnp.float32), gain_ref[...], 1).astype(jnp.bfloat16)
    emit_projections(normed, rows_ref, out_refs)


def finish_kernel(pieces, onward, *refs):
    mix_refs, refs = refs[:pieces], refs[pieces:]
    state_ref, gain_ref, gate_ref, out_gain_ref, final_ref = refs[:5]
    state = state_ref[...].astype(jnp.float32)
    normed = layer_norm(state, gain_ref[...], 1).astype(jnp.bfloat16)
    gating = sigmoid(jnp.dot(normed, gate_ref[...], preferred_element_type=jnp.float32))
    mixed = jnp.concatenate(
        [ref[part].astype(jnp.float32) for ref in mix_refs for part in range(ref.shape[0])], axis=0
    )
    mixed = layer_norm(mixed, out_gain_ref[...], 0).astype(jnp.bfloat16)
    change = lax.dot_general(
        mixed, final_ref[...], (((0,), (0,)), ((), ())), preferred_element_type=jnp.float32
    )
    result = (state + gating * change).astype(jnp.bfloat16)
    if onward:
        next_gain, rows_ref, middle_ref = refs[5:8]
        middle_ref[...] = result
        normed = layer_norm(result.astype(jnp.float32), next_gain[...], 1).astype(jnp.bfloat16)
        emit_projections(normed, rows_ref, refs[8:])
    else:
        refs[5][...] = result


def whole_spec(array):
    return pl.BlockSpec(array.shape, lambda step: (0,) * array.ndim)


def row_step(positions):
    step = positions
    for candidate in range(LANES, 2304 + 1, LANES):
        if positions % candidate == 0:
            step = candidate
    return step


def run_projections(state, gain, rows, out_shapes):
    positions, features = state.shape
    step = row_step(positions)
    weights = (gain[None, :], rows)
    return pl.pallas_call(
        project_kernel,
        grid=(positions // step,),
        in_specs=[pl.BlockSpec((step, features), lambda i: (i, 0))] + [whole_spec(w) for w in weights],
        out_specs=[pl.BlockSpec((*shape, step), lambda i: (0, 0, i)) for shape in out_shapes],
        out_shape=[jax.ShapeDtypeStruct((*shape, positions), jnp.bfloat16) for shape in out_shapes],
        compiler_params=pltpu.CompilerParams(vmem_limit_bytes=BUDGET),
        name="project",
    )(state, *weights)


def run_finish(mixes, state, gain, gate_matrix, out_gain, final_matrix, onward=None):
    positions, features = state.shape
    step = row_step(positions)
    weights = (gain[None, :], gate_matrix, out_gain[:, None], final_matrix)
    out_shape = [jax.ShapeDtypeStruct((positions, features), jnp.bfloat16)]
    out_specs = [pl.BlockSpec((step, features), lambda i: (i, 0))]
    if onward is not None:
        next_gain, rows, out_shapes = onward
        weights += (next_gain[None, :], rows)
        out_shape += [jax.ShapeDtypeStruct((*shape, positions), jnp.bfloat16) for shape in out_shapes]
        out_specs += [pl.BlockSpec((*shape, step), lambda i: (0, 0, i)) for shape in out_shapes]
    return pl.pallas_call(
        functools.partial(finish_kernel, len(mixes), onward is not None),
        grid=(positions // step,),
        in_specs=[pl.BlockSpec((*m.shape[:2], step), lambda i: (0, 0, i)) for m in mixes]
        + [pl.BlockSpec((step, features), lambda i: (i, 0))]
        + [whole_spec(w) for w in weights],
        out_specs=out_specs,
        out_shape=out_shape,
        compiler_params=pltpu.CompilerParams(vmem_limit_bytes=BUDGET),
        name="finish",
    )(*(pltpu.with_memory_space_constraint(m, pltpu.HBM) for m in mixes), state, *weights)


class Folds:
    def __init__(self, row_count, col_count):
        turn = 1
        while (turn * col_count) % LANES:
            turn *= 2
        self.turn, self.tiles = turn, turn * col_count // LANES
        self.cols, self.rows = col_count, row_count
        self.groups = row_count // turn
        self.lane_rows = row_count * col_count // LANES

    def fits(self):
        return self.cols <= LANES and self.rows % self.turn == 0 and self.groups % 8 == 0

    def split(self, lane_rows, clear=False):
        lane = lax.broadcasted_iota(jnp.int32, lane_rows[0].shape, 1)
        out = []
        for phase in range(self.turn):
            first, offset = divmod(phase * self.cols, LANES)
            value = lane_rows[first]
            if offset + self.cols > LANES:
                value = jnp.where(lane >= offset, value, lane_rows[first + 1])
            if offset:
                value = pltpu.roll(value, LANES - offset, 1)
            out.append(jnp.where(lane < self.cols, value, 0.0) if clear else value)
        return out

    def join(self, block_rows):
        lane = lax.broadcasted_iota(jnp.int32, block_rows[0].shape, 1)
        rolled = []
        for phase, value in enumerate(block_rows):
            offset = (phase * self.cols) % LANES
            rolled.append(pltpu.roll(value, offset, 1) if offset else value)
        out = []
        for tile in range(self.tiles):
            value = None
            for phase in range(self.turn):
                begin, end = phase * self.cols - tile * LANES, (phase + 1) * self.cols - tile * LANES
                if end <= 0 or begin >= LANES:
                    continue
                value = rolled[phase] if value is None else jnp.where(lane >= begin, rolled[phase], value)
            out.append(value)
        return out


def stage(source_ref, staged):
    parts, width, positions = source_ref.shape
    rows = parts * width

    @pl.loop(0, positions // LANES, unroll=8)
    def _(tile):
        lanes = pl.ds(pl.multiple_of(tile * LANES, LANES), LANES)
        for part in range(parts):
            staged[pl.ds(tile * rows + part * width, width), :] = source_ref[part, :, lanes].astype(jnp.float32)


def unstage(staged, target_ref, earlier_refs=()):
    parts, height, positions = target_ref.shape
    width = height - sum(ref.shape[1] for ref in earlier_refs)
    rows = parts * width

    @pl.loop(0, positions // LANES, unroll=8)
    def _(tile):
        lanes = pl.ds(pl.multiple_of(tile * LANES, LANES), LANES)
        for part in range(parts):
            values = [ref[part, :, lanes].astype(jnp.float32) for ref in earlier_refs]
            values.append(staged[pl.ds(tile * rows + part * width, width), :])
            values = values[0] if len(values) == 1 else jnp.concatenate(values, axis=0)
            target_ref[part, :, lanes] = values.astype(target_ref.dtype)


def lane_rows_of(folds, rows, row):
    return [pl.ds(row + tile * rows, folds.groups, stride=folds.tiles * rows) for tile in range(folds.tiles)]


def mix_out_kernel(folds, near, cols, width, stages, half_ref, *refs):
    parts = near * cols
    rows = parts * width
    block = folds.rows
    tall = near * block
    earlier_refs, near_ref = (), None
    if stages == (0, 1):
        left_ref, right_ref, there_ref, *earlier_refs, mix_ref, staged, right, folded, left = refs
    elif stages == (0,):
        left_ref, right_ref, mix_ref, left, staged, right, folded = refs
    else:
        left, near_ref, there_ref, *earlier_refs, mix_ref, staged, right, folded = refs

    def unfold(ref, shift, store):
        height = ref.shape[1]
        stage(ref, staged)

        @pl.loop(0, rows, unroll=8)
        def _(step):
            source, channel = step // width, step % width
            row = source * height + shift + channel
            store(source, channel, [staged[at, :] for at in lane_rows_of(folds, parts * height, row)])

    def store_left(source, channel, lane_rows):
        pieces = folds.split(lane_rows, clear=True)
        at = (channel * cols + source % cols) * tall + (source // cols) * block
        left[pl.ds(pl.multiple_of(at, block), block), :] = jnp.concatenate(pieces, axis=0).astype(jnp.bfloat16)

    def store_right(source, channel, lane_rows):
        at = (channel * cols + source % cols) * tall + (source // cols) * block
        for phase, piece in enumerate(folds.split(lane_rows)):
            right[pl.ds(at + phase, folds.groups, stride=folds.turn), :] = piece

    def products(half):
        @pl.loop(0, width)
        def _(channel):
            starts = [(channel * cols + col) * tall for col in range(cols)]
            lhs = jnp.concatenate([left[pl.ds(pl.multiple_of(at, block), tall), :] for at in starts], axis=1)
            for offset in range(near):
                at = [pl.multiple_of(start + offset * block, block) for start in starts]
                rhs = jnp.concatenate([right[pl.ds(begin, block), :] for begin in at], axis=1).astype(jnp.bfloat16)
                total = lax.dot_general(lhs, rhs, (((1,), (1,)), ((), ())), preferred_element_type=jnp.float32)
                total = jnp.concatenate([total, jnp.zeros((tall, LANES - block), jnp.float32)], axis=1)
                for piece in range(near):
                    lane_rows = folds.join(
                        [
                            total[piece * block + phase * folds.groups : piece * block + (phase + 1) * folds.groups, :]
                            for phase in range(folds.turn)
                        ]
                    )
                    out_row = (piece * cols + half * near + offset) * width + channel
                    for lanes, value in zip(lane_rows_of(folds, rows, out_row), lane_rows):
                        folded[lanes, :] = value

    if 0 in stages:
        unfold(left_ref, 0, store_left)
        unfold(right_ref, right_ref.shape[1] - width, store_right)
        products(half_ref[0])
    if 1 in stages:
        unfold(there_ref, 0, store_right)
        products(half_ref[1])

    @pl.loop(0, mix_ref.shape[2] // LANES, unroll=8)
    def _(tile):
        lanes = pl.ds(pl.multiple_of(tile * LANES, LANES), LANES)
        for part in range(parts):
            value = folded[pl.ds(tile * rows + part * width, width), :]
            if near_ref is not None:
                mine = half_ref[0] == part % cols // near
                value = jnp.where(mine, near_ref[part, :, lanes].astype(jnp.float32), value)
            values = [ref[part, :, lanes].astype(jnp.float32) for ref in earlier_refs] + [value]
            values = values[0] if len(values) == 1 else jnp.concatenate(values, axis=0)
            mix_ref[part, :, lanes] = values.astype(mix_ref.dtype)


def mix_in_kernel(folds, near, cols, width, half_ref, both_ref, keep_ref, send_ref, staged, left, right, turned, mixed):
    parts = near * cols
    rows = 2 * parts * width
    block = folds.rows

    stage(both_ref, staged)

    for target, shift in ((left, 0), (right, width)):

        @pl.loop(0, parts * width, unroll=8)
        def _(step):
            source, channel = step // width, step % width
            row = source * 2 * width + shift + channel
            pieces = folds.split([staged[at, :] for at in lane_rows_of(folds, rows, row)])
            at = (channel * cols + source % cols) * near * block + (source // cols) * block
            target[pl.ds(pl.multiple_of(at, block), block), :] = jnp.concatenate(pieces, axis=0).astype(jnp.bfloat16)

    out_rows = parts * width
    tall = near * block

    @pl.loop(0, width, unroll=1)
    def _(channel):
        rhs = jnp.concatenate(
            [right[pl.ds(pl.multiple_of((channel * cols + col) * tall, block), tall), :] for col in range(cols)], axis=1
        )
        for upper in range(cols):
            lhs = left[pl.ds(pl.multiple_of((channel * cols + upper) * tall, block), tall), :]
            summed = lax.dot_general(lhs, rhs, (((0,), (0,)), ((), ())), preferred_element_type=jnp.float32)
            half, piece = divmod(upper, near)
            for target in range(cols):
                turned[upper, target] = summed[:, target * LANES : (target + 1) * LANES]
                lane_rows = folds.join(
                    [turned[upper, target, pl.ds(phase, folds.groups, stride=folds.turn), :] for phase in range(folds.turn)]
                )
                out_row = (piece * cols + target) * width + channel
                for at, value in zip(lane_rows_of(folds, out_rows, out_row), lane_rows):
                    mixed[half, at, :] = value

    unstage(mixed.at[half_ref[0]], keep_ref)
    unstage(mixed.at[half_ref[1]], send_ref)


SMEM_SPEC = pl.BlockSpec(memory_space=pltpu.SMEM)
VMEM_SPEC = pl.BlockSpec(memory_space=pltpu.VMEM)


def run_mix_out(folds, near, cols, width, stages, halves, *arrays, earlier=()):
    parts, _, positions = arrays[-1].shape
    rows = parts * width
    tall = width * cols * near * folds.rows
    out_shape = [jax.ShapeDtypeStruct((parts, width + sum(e.shape[1] for e in earlier), positions), jnp.bfloat16)]
    scratch = [
        pltpu.VMEM((2 * rows * folds.lane_rows, LANES), jnp.float32),
        pltpu.VMEM((tall, LANES), jnp.float32),
        pltpu.VMEM((rows * folds.lane_rows, LANES), jnp.float32),
    ]
    if stages == (0,):
        out_shape.append(jax.ShapeDtypeStruct((tall, LANES), jnp.bfloat16))
    elif stages == (0, 1):
        scratch.append(pltpu.VMEM((tall, LANES), jnp.bfloat16))
    return pl.pallas_call(
        functools.partial(mix_out_kernel, folds, near, cols, width, stages),
        in_specs=[SMEM_SPEC] + [VMEM_SPEC] * (len(arrays) + len(earlier)),
        out_specs=[VMEM_SPEC] * len(out_shape),
        out_shape=out_shape,
        scratch_shapes=scratch,
        compiler_params=pltpu.CompilerParams(vmem_limit_bytes=BUDGET),
        name="mix_out",
    )(halves, *arrays, *earlier)


def add_kernel(*refs):
    target_ref = refs[-1]
    parts = target_ref.shape[0]
    for part in range(parts):
        sums = [kept[part] + got[part].astype(jnp.float32) for kept, got in zip(refs[:-1:2], refs[1:-1:2])]
        target_ref[part] = jnp.concatenate(sums, axis=0).astype(target_ref.dtype)


def run_add(*arrays):
    parts, _, positions = arrays[0].shape
    step = row_step(positions)
    height = sum(array.shape[1] for array in arrays) // 2
    return pl.pallas_call(
        add_kernel,
        grid=(positions // step,),
        in_specs=[pl.BlockSpec((*array.shape[:2], step), lambda i: (0, 0, i)) for array in arrays],
        out_specs=pl.BlockSpec((parts, height, step), lambda i: (0, 0, i)),
        out_shape=jax.ShapeDtypeStruct((parts, height, positions), jnp.bfloat16),
        compiler_params=pltpu.CompilerParams(vmem_limit_bytes=BUDGET),
        name="add",
    )(*arrays)


def run_mix_in(folds, near, cols, halves, both):
    parts, width, positions = both.shape
    rows, width = parts * width, width // 2
    block = folds.rows
    return pl.pallas_call(
        functools.partial(mix_in_kernel, folds, near, cols, width),
        in_specs=[SMEM_SPEC, VMEM_SPEC],
        out_specs=[VMEM_SPEC, VMEM_SPEC],
        out_shape=[
            jax.ShapeDtypeStruct((parts, width, positions), jnp.float32),
            jax.ShapeDtypeStruct((parts, width, positions), jnp.bfloat16),
        ],
        scratch_shapes=[
            pltpu.VMEM((rows * folds.lane_rows, LANES), jnp.float32),
            pltpu.VMEM((width * cols * near * block, LANES), jnp.bfloat16),
            pltpu.VMEM((width * cols * near * block, LANES), jnp.bfloat16),
            pltpu.VMEM((cols, cols, LANES, LANES), jnp.float32),
            pltpu.VMEM((2, rows // 2 * folds.lane_rows, LANES), jnp.float32),
        ],
        compiler_params=pltpu.CompilerParams(vmem_limit_bytes=BUDGET),
        name="mix_in",
    )(halves, both)


SHARES = (1, 1, 1, 1)
GROUPS = ((0, 1), (2, 3))
PIECES = len(SHARES)


def exchange(array):
    return lax.all_to_all(array, EVERY, split_axis=0, concat_axis=0, tiled=True)


def across(array):
    return lax.ppermute(array, "far", ((0, 1), (1, 0)))


def in_halves(sizes, pair_input, weights):
    _, near, cols = sizes
    row_count, col_count, features = pair_input.shape
    parts = near * cols
    width = features // parts
    ends = [sum(SHARES[: at + 1]) * width // sum(SHARES) for at in range(PIECES)]
    begins = [0] + ends[:-1]
    folds = Folds(row_count, col_count)
    half = lax.axis_index("far")
    halves = jnp.stack([half, 1 - half]).astype(jnp.int32)

    def rows_of(project, *arrays):
        ga, va, gb, vb = (rows.reshape(parts, width, features) for rows in jnp.split(project.T, 4, axis=0))

        def ordered(left, right):
            return [
                jnp.concatenate(
                    [rows[:, begins[piece] : ends[piece]] for rows, piece in zip((left, right), pair) if piece is not None],
                    axis=1,
                ).reshape(-1, features)
                for pair in arrays
            ]

        return jnp.concatenate(ordered(ga, gb) + ordered(va, vb))

    def shapes_of(*arrays):
        return [
            (parts, sum(ends[piece] - begins[piece] for piece in pair if piece is not None)) for pair in arrays
        ]

    def in_groups(array):
        rows = array.reshape(parts, width, -1)
        ordered = [
            jnp.concatenate([rows[:, begins[piece] : ends[piece]] for piece in group], axis=1).reshape(-1, rows.shape[-1])
            for group in GROUPS
        ]
        return jnp.concatenate(ordered).reshape(array.shape)

    gain_1, project_1, gate_1, norm_1, final_1, gain_2, project_2, gate_2, norm_2, final_2 = weights
    state = pair_input.reshape(-1, features)

    ahead = [(None, 0)] + [(piece, piece + 1) for piece in range(PIECES - 1)] + [(PIECES - 1, None)]
    level = [(piece, piece) for piece in range(PIECES)]
    sent, mixed, mixes = [], [None] * PIECES, []
    out = run_projections(state, gain_1, rows_of(project_1, *ahead[:1]), shapes_of(*ahead[:1]))
    out += run_projections(state, gain_1, rows_of(project_1, *ahead[1:]), shapes_of(*ahead[1:]))
    for array in out:
        sent.append(exchange(array))
    for piece in range(PIECES):
        group = next(group for group in GROUPS if piece in group)
        right, left = sent[piece], sent[piece + 1]
        there = across(right[:, right.shape[1] - (ends[piece] - begins[piece]) :, :])
        earlier = [mixed[other] for other in group[:-1]] if piece == group[-1] else ()
        mix = functools.partial(run_mix_out, folds, near, cols, ends[piece] - begins[piece])
        if piece < PIECES - 1:
            mixed[piece] = mix((0, 1), halves, left, right, there, earlier=earlier)[0]
        else:
            mine, unfolded = mix((0,), halves, left, right)
            mixed[piece] = mix((1,), halves, unfolded, mine, there, earlier=earlier)[0]
        if piece == group[-1]:
            mixes.append(exchange(mixed[piece]))
    onward = (gain_2, rows_of(project_2, *level[:1]), shapes_of(*level[:1]))
    middle, *out = run_finish(mixes, state, gain_1, gate_1, in_groups(norm_1), in_groups(final_1), onward)
    out += run_projections(middle, gain_2, rows_of(project_2, *level[1:]), shapes_of(*level[1:]))
    both, parted, mixes = [], [], []
    for piece in range(PIECES):
        both.append(exchange(out[piece]))
    for piece in range(PIECES):
        kept, sent = run_mix_in(folds, near, cols, halves, both[piece])
        parted.append((kept, across(sent)))
    for group in GROUPS:
        summed = run_add(*(array for piece in group for array in parted[piece]))
        mixes.append(exchange(summed))
    result = run_finish(mixes, middle, gain_2, gate_2, in_groups(norm_2), in_groups(final_2))[0]
    return result.reshape(pair_input.shape)


def solution(mesh):
    row_parts, col_parts = mesh.shape["dap"], mesh.shape["chan"] * mesh.shape["sub"]

    def whole(pair_input, *weights):
        features = pair_input.shape[-1]
        block_rows = pair_input.shape[0] // (mesh.shape["groups"] * row_parts)
        block_cols = pair_input.shape[1] // col_parts
        halved = (
            row_parts % 2 == 0
            and row_parts == col_parts
            and block_rows == block_cols
            and Folds(block_rows, block_cols).fits()
            and features == LANES
            and features % (row_parts // 2 * col_parts * sum(SHARES)) == 0
        )
        if halved:
            far, near = 2, row_parts // 2
        else:
            far, near = split_rows(row_parts, col_parts, features, 8)
        sizes = (far, near, col_parts)
        finer = Mesh(
            mesh.devices.reshape(mesh.shape["groups"], far, near, mesh.shape["chan"], mesh.shape["sub"]),
            ("groups", "far", "near", "chan", "sub"),
        )

        def shards(pair_input, *weights):
            if halved:
                return in_halves(sizes, pair_input, weights)
            middle = update(False, sizes, pair_input, *weights[:5])
            return update(True, sizes, middle, *weights[5:])

        pair_spec = P(("groups", "far", "near"), ("chan", "sub"), None)
        mapped = jax.shard_map(
            shards,
            mesh=finer,
            in_specs=(pair_spec,) + (P(),) * 10,
            out_specs=pair_spec,
            check_vma=False,
        )
        return mapped(pair_input, *weights)

    return whole
```

```python
import functools

import jax
import jax.numpy as jnp
from jax import lax
from jax.experimental import pallas as pl
from jax.experimental.pallas import tpu as pltpu
from jax.sharding import Mesh
from jax.sharding import PartitionSpec as P


epsilon = 1e-05
EVERY = ("near", "chan", "sub")
LANES = 128
BUDGET = 56 << 20


def layer_norm(values, norm_gain, reduce_axis):
    average = jnp.mean(values, axis=reduce_axis, keepdims=True)
    centred = values - average
    variance = jnp.mean(centred * centred, axis=reduce_axis, keepdims=True)
    return centred * lax.rsqrt(variance + epsilon) * norm_gain


def sigmoid(values):
    return 0.5 * jnp.tanh(0.5 * values) + 0.5


def project_in(pair_state, norm_gain, project, gate_matrix):
    features = pair_state.shape[-1]
    flattened = pair_state.reshape(-1, features).astype(jnp.float32)
    normed = layer_norm(flattened, norm_gain, 1).astype(jnp.bfloat16)
    projected = jnp.einsum("xc,cd->dx", normed, project, preferred_element_type=jnp.float32)
    left_part = jax.nn.sigmoid(projected[:features]) * projected[features : 2 * features]
    right_part = jax.nn.sigmoid(projected[2 * features : 3 * features]) * projected[3 * features :]
    gating = jax.nn.sigmoid(jnp.dot(normed, gate_matrix, preferred_element_type=jnp.float32))
    return left_part.astype(jnp.bfloat16), right_part.astype(jnp.bfloat16), gating


def finish(pair_state, mixture, gating, out_gain, final_matrix):
    features = mixture.shape[0]
    flattened = mixture.astype(jnp.float32)
    normed = layer_norm(flattened, out_gain[:, None], 0).astype(jnp.bfloat16)
    update = jnp.einsum("cx,cd->xd", normed, final_matrix, preferred_element_type=jnp.float32)
    result = pair_state.reshape(-1, features).astype(jnp.float32) + gating * update
    return result.astype(jnp.bfloat16).reshape(pair_state.shape)


def update(incoming, sizes, pair_state, norm_gain, project, gate_matrix, out_gain, final_matrix):
    far, near, col_parts = sizes
    row_count, col_count, features = pair_state.shape
    parts = near * col_parts
    width = features // parts
    left_part, right_part, gating = project_in(pair_state, norm_gain, project, gate_matrix)
    both = jnp.stack([left_part.reshape(parts, width, -1), right_part.reshape(parts, width, -1)], axis=1)
    both = lax.all_to_all(both, EVERY, split_axis=0, concat_axis=0, tiled=True)
    both = both.reshape(near, col_parts, 2, width, row_count, col_count)
    both = both.transpose(2, 3, 0, 4, 1, 5).reshape(2, width, near * row_count, col_parts * col_count)
    left_part, right_part = both[0], both[1]
    if incoming:
        mixture = jnp.einsum("cki,ckj->cij", left_part, right_part, preferred_element_type=jnp.float32)
        if far > 1:
            mixture = lax.psum_scatter(mixture, "far", scatter_dimension=1, tiled=True)
    else:
        if far > 1:
            right_part = lax.all_gather(right_part, "far", axis=1, tiled=True)
        mixture = jnp.einsum("cik,cjk->cij", left_part, right_part, preferred_element_type=jnp.float32)
    mixture = mixture.astype(jnp.bfloat16).reshape(width, near, row_count, col_parts, col_count)
    mixture = mixture.transpose(1, 3, 0, 2, 4).reshape(parts, width, row_count * col_count)
    mixture = lax.all_to_all(mixture, EVERY, split_axis=0, concat_axis=0, tiled=True)
    return finish(pair_state, mixture.reshape(features, -1), gating, out_gain, final_matrix)


def split_rows(row_parts, col_parts, features, least):
    near = row_parts
    while near > 1 and (row_parts % near or features % (near * col_parts) or features < least * near * col_parts):
        near -= 1
    return row_parts // near, near


SMEM_SPEC = pl.BlockSpec(memory_space=pltpu.SMEM)
VMEM_SPEC = pl.BlockSpec(memory_space=pltpu.VMEM)


def near_core(array):
    return pltpu.with_memory_space_constraint(array, pltpu.VMEM)


def step_lanes(span):
    return pl.ds(pl.multiple_of(pl.program_id(0) * span, span), span)


def emit_projections(normed, rows_ref, out_refs):
    step = normed.shape[0]
    half = rows_ref.shape[0] // 2
    group = 256 if step % 256 == 0 else LANES
    for begin in range(0, step, group):
        projected = lax.dot_general(
            rows_ref[...], normed[begin : begin + group, :], (((1,), (1,)), ((), ())), preferred_element_type=jnp.float32
        )
        gated = sigmoid(projected[:half, :]) * projected[half:, :]
        at = 0
        for ref in out_refs:
            parts, width, _ = ref.shape
            for part in range(parts):
                ref[part, :, begin : begin + group] = gated[at : at + width, :].astype(ref.dtype)
                at += width


def project_kernel(state_ref, gain_ref, rows_ref, *out_refs):
    normed = layer_norm(state_ref[...].astype(jnp.float32), gain_ref[...], 1).astype(jnp.bfloat16)
    emit_projections(normed, rows_ref, out_refs)


def finish_kernel(pieces, onward, *refs):
    mix_refs, refs = refs[:pieces], refs[pieces:]
    state_ref, gain_ref, gate_ref, out_gain_ref, final_ref = refs[:5]
    state = state_ref[...].astype(jnp.float32)
    normed = layer_norm(state, gain_ref[...], 1).astype(jnp.bfloat16)
    gating = sigmoid(jnp.dot(normed, gate_ref[...], preferred_element_type=jnp.float32))
    lanes = step_lanes(state.shape[0])
    mixed = jnp.concatenate(
        [ref[part, :, lanes].astype(jnp.float32) for ref in mix_refs for part in range(ref.shape[0])], axis=0
    )
    mixed = layer_norm(mixed, out_gain_ref[...], 0).astype(jnp.bfloat16)
    change = lax.dot_general(
        mixed, final_ref[...], (((0,), (0,)), ((), ())), preferred_element_type=jnp.float32
    )
    result = (state + gating * change).astype(jnp.bfloat16)
    if onward:
        next_gain, rows_ref, middle_ref = refs[5:8]
        middle_ref[...] = result
        normed = layer_norm(result.astype(jnp.float32), next_gain[...], 1).astype(jnp.bfloat16)
        emit_projections(normed, rows_ref, refs[8:])
    else:
        refs[5][...] = result


def whole_spec(array):
    return pl.BlockSpec(array.shape, lambda step: (0,) * array.ndim)


def row_step(positions):
    step = positions
    for candidate in range(LANES, 2304 + 1, LANES):
        if positions % candidate == 0:
            step = candidate
    return step


def run_projections(state, gain, rows, out_shapes):
    positions, features = state.shape
    step = row_step(positions)
    weights = (gain[None, :], rows)
    return pl.pallas_call(
        project_kernel,
        grid=(positions // step,),
        in_specs=[pl.BlockSpec((step, features), lambda i: (i, 0))] + [whole_spec(w) for w in weights],
        out_specs=[pl.BlockSpec((*shape, step), lambda i: (0, 0, i)) for shape in out_shapes],
        out_shape=[jax.ShapeDtypeStruct((*shape, positions), jnp.bfloat16) for shape in out_shapes],
        compiler_params=pltpu.CompilerParams(vmem_limit_bytes=BUDGET),
        name="project",
    )(state, *weights)


def run_finish(mixes, state, gain, gate_matrix, out_gain, final_matrix, onward=None):
    positions, features = state.shape
    step = row_step(positions)
    weights = (gain[None, :], gate_matrix, out_gain[:, None], final_matrix)
    out_shape = [jax.ShapeDtypeStruct((positions, features), jnp.bfloat16)]
    out_specs = [pl.BlockSpec((step, features), lambda i: (i, 0))]
    if onward is not None:
        next_gain, rows, out_shapes = onward
        weights += (next_gain[None, :], rows)
        out_shape += [jax.ShapeDtypeStruct((*shape, positions), jnp.bfloat16) for shape in out_shapes]
        out_specs += [pl.BlockSpec((*shape, step), lambda i: (0, 0, i)) for shape in out_shapes]
    return pl.pallas_call(
        functools.partial(finish_kernel, len(mixes), onward is not None),
        grid=(positions // step,),
        in_specs=[VMEM_SPEC] * len(mixes)
        + [pl.BlockSpec((step, features), lambda i: (i, 0))]
        + [whole_spec(w) for w in weights],
        out_specs=out_specs,
        out_shape=out_shape,
        compiler_params=pltpu.CompilerParams(vmem_limit_bytes=BUDGET),
        name="finish",
    )(*map(near_core, mixes), state, *weights)


class Folds:
    def __init__(self, row_count, col_count):
        turn = 1
        while (turn * col_count) % LANES:
            turn *= 2
        self.turn, self.tiles = turn, turn * col_count // LANES
        self.cols, self.rows = col_count, row_count
        self.groups = row_count // turn
        self.lane_rows = row_count * col_count // LANES

    def fits(self):
        return self.cols <= LANES and self.rows % self.turn == 0 and self.groups % 8 == 0

    def split(self, lane_rows, clear=False):
        lane = lax.broadcasted_iota(jnp.int32, lane_rows[0].shape, 1)
        out = []
        for phase in range(self.turn):
            first, offset = divmod(phase * self.cols, LANES)
            value = lane_rows[first]
            if offset + self.cols > LANES:
                value = jnp.where(lane >= offset, value, lane_rows[first + 1])
            if offset:
                value = pltpu.roll(value, LANES - offset, 1)
            out.append(jnp.where(lane < self.cols, value, 0.0) if clear else value)
        return out

    def join(self, block_rows):
        lane = lax.broadcasted_iota(jnp.int32, block_rows[0].shape, 1)
        rolled = []
        for phase, value in enumerate(block_rows):
            offset = (phase * self.cols) % LANES
            rolled.append(pltpu.roll(value, offset, 1) if offset else value)
        out = []
        for tile in range(self.tiles):
            value = None
            for phase in range(self.turn):
                begin, end = phase * self.cols - tile * LANES, (phase + 1) * self.cols - tile * LANES
                if end <= 0 or begin >= LANES:
                    continue
                value = rolled[phase] if value is None else jnp.where(lane >= begin, rolled[phase], value)
            out.append(value)
        return out


def stage(source_ref, staged):
    parts, width, positions = source_ref.shape
    rows = parts * width

    @pl.loop(0, positions // LANES, unroll=8)
    def _(tile):
        lanes = pl.ds(pl.multiple_of(tile * LANES, LANES), LANES)
        for part in range(parts):
            staged[pl.ds(tile * rows + part * width, width), :] = source_ref[part, :, lanes].astype(jnp.float32)


def unstage(staged, target_ref, earlier_refs=()):
    parts, height, positions = target_ref.shape
    width = height - sum(ref.shape[1] for ref in earlier_refs)
    rows = parts * width

    @pl.loop(0, positions // LANES, unroll=8)
    def _(tile):
        lanes = pl.ds(pl.multiple_of(tile * LANES, LANES), LANES)
        for part in range(parts):
            values = [ref[part, :, lanes].astype(jnp.float32) for ref in earlier_refs]
            values.append(staged[pl.ds(tile * rows + part * width, width), :])
            values = values[0] if len(values) == 1 else jnp.concatenate(values, axis=0)
            target_ref[part, :, lanes] = values.astype(target_ref.dtype)


def lane_rows_of(folds, rows, row):
    return [pl.ds(row + tile * rows, folds.groups, stride=folds.tiles * rows) for tile in range(folds.tiles)]


def mix_out_kernel(folds, near, cols, width, stages, half_ref, *refs):
    parts = near * cols
    rows = parts * width
    block = folds.rows
    tall = near * block
    earlier_refs, near_ref = (), None
    if stages == (0, 1):
        left_ref, right_ref, there_ref, *earlier_refs, mix_ref, staged, right, folded, left = refs
    elif stages == (0,):
        left_ref, right_ref, mix_ref, left, staged, right, folded = refs
    else:
        left, near_ref, there_ref, *earlier_refs, mix_ref, staged, right, folded = refs

    def unfold(ref, shift, store):
        height = ref.shape[1]
        stage(ref, staged)

        @pl.loop(0, rows, unroll=8)
        def _(step):
            source, channel = step // width, step % width
            row = source * height + shift + channel
            store(source, channel, [staged[at, :] for at in lane_rows_of(folds, parts * height, row)])

    def store_left(source, channel, lane_rows):
        pieces = folds.split(lane_rows, clear=True)
        at = (channel * cols + source % cols) * tall + (source // cols) * block
        left[pl.ds(pl.multiple_of(at, block), block), :] = jnp.concatenate(pieces, axis=0).astype(jnp.bfloat16)

    def store_right(source, channel, lane_rows):
        at = (channel * cols + source % cols) * tall + (source // cols) * block
        for phase, piece in enumerate(folds.split(lane_rows)):
            right[pl.ds(at + phase, folds.groups, stride=folds.turn), :] = piece

    def products(half):
        @pl.loop(0, width)
        def _(channel):
            starts = [(channel * cols + col) * tall for col in range(cols)]
            lhs = jnp.concatenate([left[pl.ds(pl.multiple_of(at, block), tall), :] for at in starts], axis=1)
            for offset in range(near):
                at = [pl.multiple_of(start + offset * block, block) for start in starts]
                rhs = jnp.concatenate([right[pl.ds(begin, block), :] for begin in at], axis=1).astype(jnp.bfloat16)
                total = lax.dot_general(lhs, rhs, (((1,), (1,)), ((), ())), preferred_element_type=jnp.float32)
                total = jnp.concatenate([total, jnp.zeros((tall, LANES - block), jnp.float32)], axis=1)
                for piece in range(near):
                    lane_rows = folds.join(
                        [
                            total[piece * block + phase * folds.groups : piece * block + (phase + 1) * folds.groups, :]
                            for phase in range(folds.turn)
                        ]
                    )
                    out_row = (piece * cols + half * near + offset) * width + channel
                    for lanes, value in zip(lane_rows_of(folds, rows, out_row), lane_rows):
                        folded[lanes, :] = value

    if 0 in stages:
        unfold(left_ref, 0, store_left)
        unfold(right_ref, right_ref.shape[1] - width, store_right)
        products(half_ref[0])
    if 1 in stages:
        unfold(there_ref, 0, store_right)
        products(half_ref[1])

    @pl.loop(0, mix_ref.shape[2] // LANES, unroll=8)
    def _(tile):
        lanes = pl.ds(pl.multiple_of(tile * LANES, LANES), LANES)
        for part in range(parts):
            value = folded[pl.ds(tile * rows + part * width, width), :]
            if near_ref is not None:
                mine = half_ref[0] == part % cols // near
                value = jnp.where(mine, near_ref[part, :, lanes].astype(jnp.float32), value)
            values = [ref[part, :, lanes].astype(jnp.float32) for ref in earlier_refs] + [value]
            values = values[0] if len(values) == 1 else jnp.concatenate(values, axis=0)
            mix_ref[part, :, lanes] = values.astype(mix_ref.dtype)


def mix_in_kernel(folds, near, cols, width, half_ref, both_ref, keep_ref, send_ref, staged, left, right, turned, mixed):
    parts = near * cols
    rows = 2 * parts * width
    block = folds.rows

    stage(both_ref, staged)

    for target, shift in ((left, 0), (right, width)):

        @pl.loop(0, parts * width, unroll=8)
        def _(step):
            source, channel = step // width, step % width
            row = source * 2 * width + shift + channel
            pieces = folds.split([staged[at, :] for at in lane_rows_of(folds, rows, row)])
            at = (channel * cols + source % cols) * near * block + (source // cols) * block
            target[pl.ds(pl.multiple_of(at, block), block), :] = jnp.concatenate(pieces, axis=0).astype(jnp.bfloat16)

    out_rows = parts * width
    tall = near * block

    @pl.loop(0, width, unroll=1)
    def _(channel):
        rhs = jnp.concatenate(
            [right[pl.ds(pl.multiple_of((channel * cols + col) * tall, block), tall), :] for col in range(cols)], axis=1
        )
        for upper in range(cols):
            lhs = left[pl.ds(pl.multiple_of((channel * cols + upper) * tall, block), tall), :]
            summed = lax.dot_general(lhs, rhs, (((0,), (0,)), ((), ())), preferred_element_type=jnp.float32)
            half, piece = divmod(upper, near)
            for target in range(cols):
                turned[upper, target] = summed[:, target * LANES : (target + 1) * LANES]
                lane_rows = folds.join(
                    [turned[upper, target, pl.ds(phase, folds.groups, stride=folds.turn), :] for phase in range(folds.turn)]
                )
                out_row = (piece * cols + target) * width + channel
                for at, value in zip(lane_rows_of(folds, out_rows, out_row), lane_rows):
                    mixed[half, at, :] = value

    unstage(mixed.at[half_ref[0]], keep_ref)
    unstage(mixed.at[half_ref[1]], send_ref)


def run_mix_out(folds, near, cols, width, stages, halves, *arrays, mine=None, earlier=()):
    parts, _, positions = arrays[-1].shape
    rows = parts * width
    tall = width * cols * near * folds.rows
    out_shape = [jax.ShapeDtypeStruct((parts, width + sum(e.shape[1] for e in earlier), positions), jnp.bfloat16)]
    scratch = [
        pltpu.VMEM((2 * rows * folds.lane_rows, LANES), jnp.float32),
        pltpu.VMEM((tall, LANES), jnp.float32),
        pltpu.VMEM((rows * folds.lane_rows, LANES), jnp.float32),
    ]
    if stages == (0,):
        out_shape.append(jax.ShapeDtypeStruct((tall, LANES), jnp.bfloat16))
    elif stages == (0, 1):
        scratch.append(pltpu.VMEM((tall, LANES), jnp.bfloat16))
    return pl.pallas_call(
        functools.partial(mix_out_kernel, folds, near, cols, width, stages),
        in_specs=[SMEM_SPEC] + [VMEM_SPEC] * (len(arrays) + len(earlier)),
        out_specs=[VMEM_SPEC] * len(out_shape),
        out_shape=out_shape,
        scratch_shapes=scratch,
        compiler_params=pltpu.CompilerParams(vmem_limit_bytes=BUDGET),
        name="mix_out",
    )(halves, *(array if array.ndim < 3 or array is mine else near_core(array) for array in arrays), *earlier)


def add_kernel(*refs):
    target_ref = refs[-1]
    parts = target_ref.shape[0]
    lanes = step_lanes(target_ref.shape[2])
    for part in range(parts):
        sums = [kept[part] + got[part, :, lanes].astype(jnp.float32) for kept, got in zip(refs[:-1:2], refs[1:-1:2])]
        target_ref[part] = jnp.concatenate(sums, axis=0).astype(target_ref.dtype)


def run_add(*arrays):
    parts, _, positions = arrays[0].shape
    step = row_step(positions)
    height = sum(array.shape[1] for array in arrays) // 2
    return pl.pallas_call(
        add_kernel,
        grid=(positions // step,),
        in_specs=[pl.BlockSpec((*array.shape[:2], step), lambda i: (0, 0, i)) if at % 2 == 0 else VMEM_SPEC for at, array in enumerate(arrays)],
        out_specs=pl.BlockSpec((parts, height, step), lambda i: (0, 0, i)),
        out_shape=jax.ShapeDtypeStruct((parts, height, positions), jnp.bfloat16),
        compiler_params=pltpu.CompilerParams(vmem_limit_bytes=BUDGET),
        name="add",
    )(*(near_core(array) if at % 2 else array for at, array in enumerate(arrays)))


def run_mix_in(folds, near, cols, halves, both):
    parts, width, positions = both.shape
    rows, width = parts * width, width // 2
    block = folds.rows
    return pl.pallas_call(
        functools.partial(mix_in_kernel, folds, near, cols, width),
        in_specs=[SMEM_SPEC, VMEM_SPEC],
        out_specs=[VMEM_SPEC, VMEM_SPEC],
        out_shape=[
            jax.ShapeDtypeStruct((parts, width, positions), jnp.float32),
            jax.ShapeDtypeStruct((parts, width, positions), jnp.bfloat16),
        ],
        scratch_shapes=[
            pltpu.VMEM((rows * folds.lane_rows, LANES), jnp.float32),
            pltpu.VMEM((width * cols * near * block, LANES), jnp.bfloat16),
            pltpu.VMEM((width * cols * near * block, LANES), jnp.bfloat16),
            pltpu.VMEM((cols, cols, LANES, LANES), jnp.float32),
            pltpu.VMEM((2, rows // 2 * folds.lane_rows, LANES), jnp.float32),
        ],
        compiler_params=pltpu.CompilerParams(vmem_limit_bytes=BUDGET),
        name="mix_in",
    )(halves, near_core(both))


SHARES = (1, 1, 1, 1)
GROUPS = ((0, 1), (2, 3))
PIECES = len(SHARES)


def exchange(array):
    return lax.all_to_all(array, EVERY, split_axis=0, concat_axis=0, tiled=True)


def across(array):
    return lax.ppermute(array, "far", ((0, 1), (1, 0)))


def in_halves(sizes, pair_input, weights):
    _, near, cols = sizes
    row_count, col_count, features = pair_input.shape
    parts = near * cols
    width = features // parts
    ends = [sum(SHARES[: at + 1]) * width // sum(SHARES) for at in range(PIECES)]
    begins = [0] + ends[:-1]
    folds = Folds(row_count, col_count)
    half = lax.axis_index("far")
    halves = jnp.stack([half, 1 - half]).astype(jnp.int32)

    def rows_of(project, *arrays):
        ga, va, gb, vb = (rows.reshape(parts, width, features) for rows in jnp.split(project.T, 4, axis=0))

        def ordered(left, right):
            return [
                jnp.concatenate(
                    [rows[:, begins[piece] : ends[piece]] for rows, piece in zip((left, right), pair) if piece is not None],
                    axis=1,
                ).reshape(-1, features)
                for pair in arrays
            ]

        return jnp.concatenate(ordered(ga, gb) + ordered(va, vb))

    def shapes_of(*arrays):
        return [
            (parts, sum(ends[piece] - begins[piece] for piece in pair if piece is not None)) for pair in arrays
        ]

    def in_groups(array):
        rows = array.reshape(parts, width, -1)
        ordered = [
            jnp.concatenate([rows[:, begins[piece] : ends[piece]] for piece in group], axis=1).reshape(-1, rows.shape[-1])
            for group in GROUPS
        ]
        return jnp.concatenate(ordered).reshape(array.shape)

    gain_1, project_1, gate_1, norm_1, final_1, gain_2, project_2, gate_2, norm_2, final_2 = weights
    state = pair_input.reshape(-1, features)

    ahead = [(None, 0)] + [(piece, piece + 1) for piece in range(PIECES - 1)] + [(PIECES - 1, None)]
    level = [(piece, piece) for piece in range(PIECES)]
    sent, mixed, mixes = [], [None] * PIECES, []
    out = run_projections(state, gain_1, rows_of(project_1, *ahead[:1]), shapes_of(*ahead[:1]))
    out += run_projections(state, gain_1, rows_of(project_1, *ahead[1:]), shapes_of(*ahead[1:]))
    for array in out:
        sent.append(exchange(array))
    for piece in range(PIECES):
        group = next(group for group in GROUPS if piece in group)
        right, left = sent[piece], sent[piece + 1]
        there = across(right[:, right.shape[1] - (ends[piece] - begins[piece]) :, :])
        earlier = [mixed[other] for other in group[:-1]] if piece == group[-1] else ()
        mix = functools.partial(run_mix_out, folds, near, cols, ends[piece] - begins[piece])
        if piece < PIECES - 1:
            mixed[piece] = mix((0, 1), halves, left, right, there, earlier=earlier)[0]
        else:
            mine, unfolded = mix((0,), halves, left, right)
            mixed[piece] = mix((1,), halves, unfolded, mine, there, mine=mine, earlier=earlier)[0]
        if piece == group[-1]:
            mixes.append(exchange(mixed[piece]))
    onward = (gain_2, rows_of(project_2, *level[:1]), shapes_of(*level[:1]))
    middle, *out = run_finish(mixes, state, gain_1, gate_1, in_groups(norm_1), in_groups(final_1), onward)
    out += run_projections(middle, gain_2, rows_of(project_2, *level[1:]), shapes_of(*level[1:]))
    both, parted, mixes = [], [], []
    for piece in range(PIECES):
        both.append(exchange(out[piece]))
    for piece in range(PIECES):
        kept, sent = run_mix_in(folds, near, cols, halves, both[piece])
        parted.append((kept, across(sent)))
    for group in GROUPS:
        summed = run_add(*(array for piece in group for array in parted[piece]))
        mixes.append(exchange(summed))
    result = run_finish(mixes, middle, gain_2, gate_2, in_groups(norm_2), in_groups(final_2))[0]
    return result.reshape(pair_input.shape)


def solution(mesh):
    row_parts, col_parts = mesh.shape["dap"], mesh.shape["chan"] * mesh.shape["sub"]

    def whole(pair_input, *weights):
        features = pair_input.shape[-1]
        block_rows = pair_input.shape[0] // (mesh.shape["groups"] * row_parts)
        block_cols = pair_input.shape[1] // col_parts
        halved = (
            row_parts % 2 == 0
            and row_parts == col_parts
            and block_rows == block_cols
            and Folds(block_rows, block_cols).fits()
            and features == LANES
            and features % (row_parts // 2 * col_parts * sum(SHARES)) == 0
        )
        if halved:
            far, near = 2, row_parts // 2
        else:
            far, near = split_rows(row_parts, col_parts, features, 8)
        sizes = (far, near, col_parts)
        finer = Mesh(
            mesh.devices.reshape(mesh.shape["groups"], far, near, mesh.shape["chan"], mesh.shape["sub"]),
            ("groups", "far", "near", "chan", "sub"),
        )

        def shards(pair_input, *weights):
            if halved:
                return in_halves(sizes, pair_input, weights)
            middle = update(False, sizes, pair_input, *weights[:5])
            return update(True, sizes, middle, *weights[5:])

        pair_spec = P(("groups", "far", "near"), ("chan", "sub"), None)
        mapped = jax.shard_map(
            shards,
            mesh=finer,
            in_specs=(pair_spec,) + (P(),) * 10,
            out_specs=pair_spec,
            check_vma=False,
        )
        return mapped(pair_input, *weights)

    return whole
```

```python
import functools

import jax
import jax.numpy as jnp
from jax import lax
from jax.experimental import pallas as pl
from jax.experimental.pallas import tpu as pltpu
from jax.sharding import Mesh
from jax.sharding import PartitionSpec as P


epsilon = 1e-05
EVERY = ("near", "chan", "sub")
LANES = 128
BUDGET = 56 << 20


def layer_norm(values, norm_gain, reduce_axis):
    average = jnp.mean(values, axis=reduce_axis, keepdims=True)
    centred = values - average
    variance = jnp.mean(centred * centred, axis=reduce_axis, keepdims=True)
    return centred * lax.rsqrt(variance + epsilon) * norm_gain


def sigmoid(values):
    return 0.5 * jnp.tanh(0.5 * values) + 0.5


def project_in(pair_state, norm_gain, project, gate_matrix):
    features = pair_state.shape[-1]
    flattened = pair_state.reshape(-1, features).astype(jnp.float32)
    normed = layer_norm(flattened, norm_gain, 1).astype(jnp.bfloat16)
    projected = jnp.einsum("xc,cd->dx", normed, project, preferred_element_type=jnp.float32)
    left_part = jax.nn.sigmoid(projected[:features]) * projected[features : 2 * features]
    right_part = jax.nn.sigmoid(projected[2 * features : 3 * features]) * projected[3 * features :]
    gating = jax.nn.sigmoid(jnp.dot(normed, gate_matrix, preferred_element_type=jnp.float32))
    return left_part.astype(jnp.bfloat16), right_part.astype(jnp.bfloat16), gating


def finish(pair_state, mixture, gating, out_gain, final_matrix):
    features = mixture.shape[0]
    flattened = mixture.astype(jnp.float32)
    normed = layer_norm(flattened, out_gain[:, None], 0).astype(jnp.bfloat16)
    update = jnp.einsum("cx,cd->xd", normed, final_matrix, preferred_element_type=jnp.float32)
    result = pair_state.reshape(-1, features).astype(jnp.float32) + gating * update
    return result.astype(jnp.bfloat16).reshape(pair_state.shape)


def update(incoming, sizes, pair_state, norm_gain, project, gate_matrix, out_gain, final_matrix):
    far, near, col_parts = sizes
    row_count, col_count, features = pair_state.shape
    parts = near * col_parts
    width = features // parts
    left_part, right_part, gating = project_in(pair_state, norm_gain, project, gate_matrix)
    both = jnp.stack([left_part.reshape(parts, width, -1), right_part.reshape(parts, width, -1)], axis=1)
    both = lax.all_to_all(both, EVERY, split_axis=0, concat_axis=0, tiled=True)
    both = both.reshape(near, col_parts, 2, width, row_count, col_count)
    both = both.transpose(2, 3, 0, 4, 1, 5).reshape(2, width, near * row_count, col_parts * col_count)
    left_part, right_part = both[0], both[1]
    if incoming:
        mixture = jnp.einsum("cki,ckj->cij", left_part, right_part, preferred_element_type=jnp.float32)
        if far > 1:
            mixture = lax.psum_scatter(mixture, "far", scatter_dimension=1, tiled=True)
    else:
        if far > 1:
            right_part = lax.all_gather(right_part, "far", axis=1, tiled=True)
        mixture = jnp.einsum("cik,cjk->cij", left_part, right_part, preferred_element_type=jnp.float32)
    mixture = mixture.astype(jnp.bfloat16).reshape(width, near, row_count, col_parts, col_count)
    mixture = mixture.transpose(1, 3, 0, 2, 4).reshape(parts, width, row_count * col_count)
    mixture = lax.all_to_all(mixture, EVERY, split_axis=0, concat_axis=0, tiled=True)
    return finish(pair_state, mixture.reshape(features, -1), gating, out_gain, final_matrix)


def split_rows(row_parts, col_parts, features, least):
    near = row_parts
    while near > 1 and (row_parts % near or features % (near * col_parts) or features < least * near * col_parts):
        near -= 1
    return row_parts // near, near


SMEM_SPEC = pl.BlockSpec(memory_space=pltpu.SMEM)
VMEM_SPEC = pl.BlockSpec(memory_space=pltpu.VMEM)


def lane_norm(values, norm_gain):
    lanes = values.shape[1]
    mean = jnp.dot(values, jnp.full((lanes, lanes), 1 / lanes, jnp.bfloat16), preferred_element_type=jnp.float32)
    centred = values.astype(jnp.float32) - mean
    variance = jnp.mean(centred * centred, axis=1, keepdims=True)
    return centred * lax.rsqrt(variance + epsilon) * norm_gain


def near_core(array):
    return pltpu.with_memory_space_constraint(array, pltpu.VMEM)


def step_lanes(span):
    return pl.ds(pl.multiple_of(pl.program_id(0) * span, span), span)


def emit_projections(normed, rows_ref, out_refs):
    step = normed.shape[0]
    half = rows_ref.shape[0] // 2
    group = 256 if step % 256 == 0 else LANES
    for begin in range(0, step, group):
        projected = lax.dot_general(
            rows_ref[...], normed[begin : begin + group, :], (((1,), (1,)), ((), ())), preferred_element_type=jnp.float32
        )
        gated = sigmoid(projected[:half, :]) * projected[half:, :]
        at = 0
        for ref in out_refs:
            parts, width, _ = ref.shape
            for part in range(parts):
                ref[part, :, begin : begin + group] = gated[at : at + width, :].astype(ref.dtype)
                at += width


def project_kernel(state_ref, gain_ref, rows_ref, *out_refs):
    normed = lane_norm(state_ref[...], gain_ref[...]).astype(jnp.bfloat16)
    emit_projections(normed, rows_ref, out_refs)


def finish_kernel(pieces, onward, *refs):
    mix_refs, refs = refs[:pieces], refs[pieces:]
    state_ref, gain_ref, gate_ref, out_gain_ref, final_ref = refs[:5]
    state = state_ref[...].astype(jnp.float32)
    normed = lane_norm(state_ref[...], gain_ref[...]).astype(jnp.bfloat16)
    gating = sigmoid(jnp.dot(normed, gate_ref[...], preferred_element_type=jnp.float32))
    lanes = step_lanes(state.shape[0])
    mixed = jnp.concatenate(
        [ref[part, :, lanes].astype(jnp.float32) for ref in mix_refs for part in range(ref.shape[0])], axis=0
    )
    mixed = layer_norm(mixed, out_gain_ref[...], 0).astype(jnp.bfloat16)
    change = lax.dot_general(
        mixed, final_ref[...], (((0,), (0,)), ((), ())), preferred_element_type=jnp.float32
    )
    result = (state + gating * change).astype(jnp.bfloat16)
    if onward:
        next_gain, rows_ref, middle_ref = refs[5:8]
        middle_ref[...] = result
        normed = lane_norm(result, next_gain[...]).astype(jnp.bfloat16)
        emit_projections(normed, rows_ref, refs[8:])
    else:
        refs[5][...] = result


def whole_spec(array):
    return pl.BlockSpec(array.shape, lambda step: (0,) * array.ndim)


def row_step(positions):
    step = positions
    for candidate in range(LANES, 2304 + 1, LANES):
        if positions % candidate == 0:
            step = candidate
    return step


def run_projections(state, gain, rows, out_shapes):
    positions, features = state.shape
    step = row_step(positions)
    weights = (gain[None, :], rows)
    return pl.pallas_call(
        project_kernel,
        grid=(positions // step,),
        in_specs=[pl.BlockSpec((step, features), lambda i: (i, 0))] + [whole_spec(w) for w in weights],
        out_specs=[pl.BlockSpec((*shape, step), lambda i: (0, 0, i)) for shape in out_shapes],
        out_shape=[jax.ShapeDtypeStruct((*shape, positions), jnp.bfloat16) for shape in out_shapes],
        compiler_params=pltpu.CompilerParams(vmem_limit_bytes=BUDGET),
        name="project",
    )(state, *weights)


def run_finish(mixes, state, gain, gate_matrix, out_gain, final_matrix, onward=None):
    positions, features = state.shape
    step = row_step(positions)
    weights = (gain[None, :], gate_matrix, out_gain[:, None], final_matrix)
    out_shape = [jax.ShapeDtypeStruct((positions, features), jnp.bfloat16)]
    out_specs = [pl.BlockSpec((step, features), lambda i: (i, 0))]
    if onward is not None:
        next_gain, rows, out_shapes = onward
        weights += (next_gain[None, :], rows)
        out_shape += [jax.ShapeDtypeStruct((*shape, positions), jnp.bfloat16) for shape in out_shapes]
        out_specs += [pl.BlockSpec((*shape, step), lambda i: (0, 0, i)) for shape in out_shapes]
    return pl.pallas_call(
        functools.partial(finish_kernel, len(mixes), onward is not None),
        grid=(positions // step,),
        in_specs=[VMEM_SPEC] * len(mixes)
        + [pl.BlockSpec((step, features), lambda i: (i, 0))]
        + [whole_spec(w) for w in weights],
        out_specs=out_specs,
        out_shape=out_shape,
        compiler_params=pltpu.CompilerParams(vmem_limit_bytes=BUDGET),
        name="finish",
    )(*map(near_core, mixes), state, *weights)


class Folds:
    def __init__(self, row_count, col_count):
        turn = 1
        while (turn * col_count) % LANES:
            turn *= 2
        self.turn, self.tiles = turn, turn * col_count // LANES
        self.cols, self.rows = col_count, row_count
        self.groups = row_count // turn
        self.lane_rows = row_count * col_count // LANES

    def fits(self):
        return self.cols <= LANES and self.rows % self.turn == 0 and self.groups % 8 == 0

    def split(self, lane_rows, clear=False):
        lane = lax.broadcasted_iota(jnp.int32, lane_rows[0].shape, 1)
        out = []
        for phase in range(self.turn):
            first, offset = divmod(phase * self.cols, LANES)
            value = lane_rows[first]
            if offset + self.cols > LANES:
                value = jnp.where(lane >= offset, value, lane_rows[first + 1])
            if offset:
                value = pltpu.roll(value, LANES - offset, 1)
            out.append(jnp.where(lane < self.cols, value, 0.0) if clear else value)
        return out

    def join(self, block_rows):
        lane = lax.broadcasted_iota(jnp.int32, block_rows[0].shape, 1)
        rolled = []
        for phase, value in enumerate(block_rows):
            offset = (phase * self.cols) % LANES
            rolled.append(pltpu.roll(value, offset, 1) if offset else value)
        out = []
        for tile in range(self.tiles):
            value = None
            for phase in range(self.turn):
                begin, end = phase * self.cols - tile * LANES, (phase + 1) * self.cols - tile * LANES
                if end <= 0 or begin >= LANES:
                    continue
                value = rolled[phase] if value is None else jnp.where(lane >= begin, rolled[phase], value)
            out.append(value)
        return out


def stage(source_ref, staged):
    parts, width, positions = source_ref.shape
    rows = parts * width

    @pl.loop(0, positions // LANES, unroll=8)
    def _(tile):
        lanes = pl.ds(pl.multiple_of(tile * LANES, LANES), LANES)
        for part in range(parts):
            staged[pl.ds(tile * rows + part * width, width), :] = source_ref[part, :, lanes].astype(jnp.float32)


def unstage(staged, target_ref, earlier_refs=()):
    parts, height, positions = target_ref.shape
    width = height - sum(ref.shape[1] for ref in earlier_refs)
    rows = parts * width

    @pl.loop(0, positions // LANES, unroll=8)
    def _(tile):
        lanes = pl.ds(pl.multiple_of(tile * LANES, LANES), LANES)
        for part in range(parts):
            values = [ref[part, :, lanes].astype(jnp.float32) for ref in earlier_refs]
            values.append(staged[pl.ds(tile * rows + part * width, width), :])
            values = values[0] if len(values) == 1 else jnp.concatenate(values, axis=0)
            target_ref[part, :, lanes] = values.astype(target_ref.dtype)


def lane_rows_of(folds, rows, row):
    return [pl.ds(row + tile * rows, folds.groups, stride=folds.tiles * rows) for tile in range(folds.tiles)]


def mix_out_kernel(folds, near, cols, width, stages, half_ref, *refs):
    parts = near * cols
    rows = parts * width
    block = folds.rows
    tall = near * block
    earlier_refs, near_ref = (), None
    if stages == (0, 1):
        left_ref, right_ref, there_ref, *earlier_refs, mix_ref, staged, right, folded, left = refs
    elif stages == (0,):
        left_ref, right_ref, mix_ref, left, staged, right, folded = refs
    else:
        left, near_ref, there_ref, *earlier_refs, mix_ref, staged, right, folded = refs

    def unfold(ref, shift, store):
        height = ref.shape[1]
        stage(ref, staged)

        @pl.loop(0, rows, unroll=8)
        def _(step):
            source, channel = step // width, step % width
            row = source * height + shift + channel
            store(source, channel, [staged[at, :] for at in lane_rows_of(folds, parts * height, row)])

    def store_left(source, channel, lane_rows):
        pieces = folds.split(lane_rows, clear=True)
        at = (channel * cols + source % cols) * tall + (source // cols) * block
        left[pl.ds(pl.multiple_of(at, block), block), :] = jnp.concatenate(pieces, axis=0).astype(jnp.bfloat16)

    def store_right(source, channel, lane_rows):
        at = (channel * cols + source % cols) * tall + (source // cols) * block
        for phase, piece in enumerate(folds.split(lane_rows)):
            right[pl.ds(at + phase, folds.groups, stride=folds.turn), :] = piece

    def products(half):
        @pl.loop(0, width)
        def _(channel):
            starts = [(channel * cols + col) * tall for col in range(cols)]
            lhs = jnp.concatenate([left[pl.ds(pl.multiple_of(at, block), tall), :] for at in starts], axis=1)
            for offset in range(near):
                at = [pl.multiple_of(start + offset * block, block) for start in starts]
                rhs = jnp.concatenate([right[pl.ds(begin, block), :] for begin in at], axis=1).astype(jnp.bfloat16)
                total = lax.dot_general(lhs, rhs, (((1,), (1,)), ((), ())), preferred_element_type=jnp.float32)
                total = jnp.concatenate([total, jnp.zeros((tall, LANES - block), jnp.float32)], axis=1)
                for piece in range(near):
                    lane_rows = folds.join(
                        [
                            total[piece * block + phase * folds.groups : piece * block + (phase + 1) * folds.groups, :]
                            for phase in range(folds.turn)
                        ]
                    )
                    out_row = (piece * cols + half * near + offset) * width + channel
                    for lanes, value in zip(lane_rows_of(folds, rows, out_row), lane_rows):
                        folded[lanes, :] = value

    if 0 in stages:
        unfold(left_ref, 0, store_left)
        unfold(right_ref, right_ref.shape[1] - width, store_right)
        products(half_ref[0])
    if 1 in stages:
        unfold(there_ref, 0, store_right)
        products(half_ref[1])

    @pl.loop(0, mix_ref.shape[2] // LANES, unroll=8)
    def _(tile):
        lanes = pl.ds(pl.multiple_of(tile * LANES, LANES), LANES)
        for part in range(parts):
            value = folded[pl.ds(tile * rows + part * width, width), :]
            if near_ref is not None:
                mine = half_ref[0] == part % cols // near
                value = jnp.where(mine, near_ref[part, :, lanes].astype(jnp.float32), value)
            values = [ref[part, :, lanes].astype(jnp.float32) for ref in earlier_refs] + [value]
            values = values[0] if len(values) == 1 else jnp.concatenate(values, axis=0)
            mix_ref[part, :, lanes] = values.astype(mix_ref.dtype)


def mix_in_kernel(folds, near, cols, width, stages, half_ref, both_ref, *refs):
    targets, (staged, left, right, turned, mixed) = refs[:-5], refs[-5:]
    parts = near * cols
    block = folds.rows
    tall = near * block
    out_rows = parts * width

    stage(both_ref, staged)

    def unfold(target, source, channel, shift):
        row = source * 2 * width + shift + channel
        pieces = folds.split([staged[at, :] for at in lane_rows_of(folds, 2 * out_rows, row)])
        at = (channel * cols + source % cols) * tall + (source // cols) * block
        target[pl.ds(pl.multiple_of(at, block), block), :] = jnp.concatenate(pieces, axis=0).astype(jnp.bfloat16)

    @pl.loop(0, parts * width, unroll=8)
    def _(at):
        unfold(right, at // width, at % width, width)

    for which, target_ref in zip(stages, targets):
        half = half_ref[which]

        @pl.loop(0, near * near * width, unroll=8)
        def _(at):
            place, channel = at // width, at % width
            unfold(left, place // near * cols + half * near + place % near, channel, 0)

        @pl.loop(0, width)
        def _(channel):
            starts = [pl.multiple_of((channel * cols + col) * tall, block) for col in range(cols)]
            rhs = jnp.concatenate([right[pl.ds(start, tall), :] for start in starts], axis=1)
            for piece in range(near):
                start = pl.multiple_of((channel * cols + half * near + piece) * tall, block)
                summed = lax.dot_general(
                    left[pl.ds(start, tall), :], rhs, (((0,), (0,)), ((), ())), preferred_element_type=jnp.float32
                )
                for target in range(cols):
                    turned[piece, target] = summed[:, target * LANES : (target + 1) * LANES]
                    lane_rows = folds.join(
                        [
                            turned[piece, target, pl.ds(phase, folds.groups, stride=folds.turn), :]
                            for phase in range(folds.turn)
                        ]
                    )
                    out_row = (piece * cols + target) * width + channel
                    for lanes, value in zip(lane_rows_of(folds, out_rows, out_row), lane_rows):
                        mixed[lanes, :] = value

        unstage(mixed, target_ref)


def run_mix_out(folds, near, cols, width, stages, halves, *arrays, mine=None, earlier=()):
    parts, _, positions = arrays[-1].shape
    rows = parts * width
    tall = width * cols * near * folds.rows
    out_shape = [jax.ShapeDtypeStruct((parts, width + sum(e.shape[1] for e in earlier), positions), jnp.bfloat16)]
    scratch = [
        pltpu.VMEM((2 * rows * folds.lane_rows, LANES), jnp.float32),
        pltpu.VMEM((tall, LANES), jnp.float32),
        pltpu.VMEM((rows * folds.lane_rows, LANES), jnp.float32),
    ]
    if stages == (0,):
        out_shape.append(jax.ShapeDtypeStruct((tall, LANES), jnp.bfloat16))
    elif stages == (0, 1):
        scratch.append(pltpu.VMEM((tall, LANES), jnp.bfloat16))
    return pl.pallas_call(
        functools.partial(mix_out_kernel, folds, near, cols, width, stages),
        in_specs=[SMEM_SPEC] + [VMEM_SPEC] * (len(arrays) + len(earlier)),
        out_specs=[VMEM_SPEC] * len(out_shape),
        out_shape=out_shape,
        scratch_shapes=scratch,
        compiler_params=pltpu.CompilerParams(vmem_limit_bytes=BUDGET),
        name="mix_out",
    )(halves, *(array if array.ndim < 3 or array is mine else near_core(array) for array in arrays), *earlier)


def add_kernel(*refs):
    target_ref = refs[-1]
    parts = target_ref.shape[0]
    lanes = step_lanes(target_ref.shape[2])
    for part in range(parts):
        sums = [kept[part] + got[part, :, lanes].astype(jnp.float32) for kept, got in zip(refs[:-1:2], refs[1:-1:2])]
        target_ref[part] = jnp.concatenate(sums, axis=0).astype(target_ref.dtype)


def run_add(*arrays):
    parts, _, positions = arrays[0].shape
    step = positions // 2 if positions % (2 * LANES) == 0 else positions
    height = sum(array.shape[1] for array in arrays) // 2
    return pl.pallas_call(
        add_kernel,
        grid=(positions // step,),
        in_specs=[pl.BlockSpec((*array.shape[:2], step), lambda i: (0, 0, i)) if at % 2 == 0 else VMEM_SPEC for at, array in enumerate(arrays)],
        out_specs=pl.BlockSpec((parts, height, step), lambda i: (0, 0, i)),
        out_shape=jax.ShapeDtypeStruct((parts, height, positions), jnp.bfloat16),
        compiler_params=pltpu.CompilerParams(vmem_limit_bytes=BUDGET),
        name="add",
    )(*(near_core(array) if at % 2 else array for at, array in enumerate(arrays)))


def run_mix_in(folds, near, cols, stages, halves, both):
    parts, width, positions = both.shape
    rows, width = parts * width, width // 2
    tall = width * cols * near * folds.rows
    types = (jnp.float32, jnp.bfloat16)
    return pl.pallas_call(
        functools.partial(mix_in_kernel, folds, near, cols, width, stages),
        in_specs=[SMEM_SPEC, VMEM_SPEC],
        out_specs=[VMEM_SPEC] * len(stages),
        out_shape=[jax.ShapeDtypeStruct((parts, width, positions), types[which]) for which in stages],
        scratch_shapes=[
            pltpu.VMEM((rows * folds.lane_rows, LANES), jnp.float32),
            pltpu.VMEM((tall, LANES), jnp.bfloat16),
            pltpu.VMEM((tall, LANES), jnp.bfloat16),
            pltpu.VMEM((near, cols, LANES, LANES), jnp.float32),
            pltpu.VMEM((rows // 2 * folds.lane_rows, LANES), jnp.float32),
        ],
        compiler_params=pltpu.CompilerParams(vmem_limit_bytes=BUDGET),
        name="mix_in",
    )(halves, near_core(both))


SHARES = (1, 1, 1, 1)
GROUPS = ((0, 1), (2, 3))
PIECES = len(SHARES)


def exchange(array):
    return lax.all_to_all(array, EVERY, split_axis=0, concat_axis=0, tiled=True)


def across(array):
    return lax.ppermute(array, "far", ((0, 1), (1, 0)))


def in_halves(sizes, pair_input, weights):
    _, near, cols = sizes
    row_count, col_count, features = pair_input.shape
    parts = near * cols
    width = features // parts
    ends = [sum(SHARES[: at + 1]) * width // sum(SHARES) for at in range(PIECES)]
    begins = [0] + ends[:-1]
    folds = Folds(row_count, col_count)
    half = lax.axis_index("far")
    halves = jnp.stack([half, 1 - half]).astype(jnp.int32)

    def rows_of(project, *arrays):
        ga, va, gb, vb = (rows.reshape(parts, width, features) for rows in jnp.split(project.T, 4, axis=0))

        def ordered(left, right):
            return [
                jnp.concatenate(
                    [rows[:, begins[piece] : ends[piece]] for rows, piece in zip((left, right), pair) if piece is not None],
                    axis=1,
                ).reshape(-1, features)
                for pair in arrays
            ]

        return jnp.concatenate(ordered(ga, gb) + ordered(va, vb))

    def shapes_of(*arrays):
        return [
            (parts, sum(ends[piece] - begins[piece] for piece in pair if piece is not None)) for pair in arrays
        ]

    def in_groups(array):
        rows = array.reshape(parts, width, -1)
        ordered = [
            jnp.concatenate([rows[:, begins[piece] : ends[piece]] for piece in group], axis=1).reshape(-1, rows.shape[-1])
            for group in GROUPS
        ]
        return jnp.concatenate(ordered).reshape(array.shape)

    gain_1, project_1, gate_1, norm_1, final_1, gain_2, project_2, gate_2, norm_2, final_2 = weights
    state = pair_input.reshape(-1, features)

    ahead = [(None, 0)] + [(piece, piece + 1) for piece in range(PIECES - 1)] + [(PIECES - 1, None)]
    level = [(piece, piece) for piece in range(PIECES)]
    sent, mixed, mixes = [], [None] * PIECES, []
    out = run_projections(state, gain_1, rows_of(project_1, *ahead[:1]), shapes_of(*ahead[:1]))
    out += run_projections(state, gain_1, rows_of(project_1, *ahead[1:]), shapes_of(*ahead[1:]))
    for array in out:
        sent.append(exchange(array))
    for piece in range(PIECES):
        group = next(group for group in GROUPS if piece in group)
        right, left = sent[piece], sent[piece + 1]
        there = across(right[:, right.shape[1] - (ends[piece] - begins[piece]) :, :])
        earlier = [mixed[other] for other in group[:-1]] if piece == group[-1] else ()
        mix = functools.partial(run_mix_out, folds, near, cols, ends[piece] - begins[piece])
        if piece < PIECES - 1:
            mixed[piece] = mix((0, 1), halves, left, right, there, earlier=earlier)[0]
        else:
            mine, unfolded = mix((0,), halves, left, right)
            mixed[piece] = mix((1,), halves, unfolded, mine, there, mine=mine, earlier=earlier)[0]
        if piece == group[-1]:
            mixes.append(exchange(mixed[piece]))
    onward = (gain_2, rows_of(project_2, *level[:1]), shapes_of(*level[:1]))
    middle, *out = run_finish(mixes, state, gain_1, gate_1, in_groups(norm_1), in_groups(final_1), onward)
    out += run_projections(middle, gain_2, rows_of(project_2, *level[1:]), shapes_of(*level[1:]))
    both, parted, mixes = [], [], []
    for piece in range(PIECES):
        both.append(exchange(out[piece]))
    for piece in range(PIECES):
        mix = functools.partial(run_mix_in, folds, near, cols)
        sent = mix((1,), halves, both[piece])[0]
        kept = mix((0,), halves, both[piece])[0]
        parted.append((kept, across(sent)))
    for group in GROUPS:
        summed = run_add(*(array for piece in group for array in parted[piece]))
        mixes.append(exchange(summed))
    result = run_finish(mixes, middle, gain_2, gate_2, in_groups(norm_2), in_groups(final_2))[0]
    return result.reshape(pair_input.shape)


def solution(mesh):
    row_parts, col_parts = mesh.shape["dap"], mesh.shape["chan"] * mesh.shape["sub"]

    def whole(pair_input, *weights):
        features = pair_input.shape[-1]
        block_rows = pair_input.shape[0] // (mesh.shape["groups"] * row_parts)
        block_cols = pair_input.shape[1] // col_parts
        halved = (
            row_parts % 2 == 0
            and row_parts == col_parts
            and block_rows == block_cols
            and Folds(block_rows, block_cols).fits()
            and features == LANES
            and features % (row_parts // 2 * col_parts * sum(SHARES)) == 0
        )
        if halved:
            far, near = 2, row_parts // 2
        else:
            far, near = split_rows(row_parts, col_parts, features, 8)
        sizes = (far, near, col_parts)
        finer = Mesh(
            mesh.devices.reshape(mesh.shape["groups"], far, near, mesh.shape["chan"], mesh.shape["sub"]),
            ("groups", "far", "near", "chan", "sub"),
        )

        def shards(pair_input, *weights):
            if halved:
                return in_halves(sizes, pair_input, weights)
            middle = update(False, sizes, pair_input, *weights[:5])
            return update(True, sizes, middle, *weights[5:])

        pair_spec = P(("groups", "far", "near"), ("chan", "sub"), None)
        mapped = jax.shard_map(
            shards,
            mesh=finer,
            in_specs=(pair_spec,) + (P(),) * 10,
            out_specs=pair_spec,
            check_vma=False,
        )
        return mapped(pair_input, *weights)

    return whole
```

```python
import functools

import jax
import jax.numpy as jnp
from jax import lax
from jax.experimental import pallas as pl
from jax.experimental.pallas import tpu as pltpu
from jax.sharding import Mesh
from jax.sharding import PartitionSpec as P


epsilon = 1e-05
EVERY = ("near", "chan", "sub")
LANES = 128
BUDGET = 56 << 20


def layer_norm(values, norm_gain, reduce_axis):
    average = jnp.mean(values, axis=reduce_axis, keepdims=True)
    centred = values - average
    variance = jnp.mean(centred * centred, axis=reduce_axis, keepdims=True)
    return centred * lax.rsqrt(variance + epsilon) * norm_gain


def sigmoid(values):
    return 0.5 * jnp.tanh(0.5 * values) + 0.5


def project_in(pair_state, norm_gain, project, gate_matrix):
    features = pair_state.shape[-1]
    flattened = pair_state.reshape(-1, features).astype(jnp.float32)
    normed = layer_norm(flattened, norm_gain, 1).astype(jnp.bfloat16)
    projected = jnp.einsum("xc,cd->dx", normed, project, preferred_element_type=jnp.float32)
    left_part = jax.nn.sigmoid(projected[:features]) * projected[features : 2 * features]
    right_part = jax.nn.sigmoid(projected[2 * features : 3 * features]) * projected[3 * features :]
    gating = jax.nn.sigmoid(jnp.dot(normed, gate_matrix, preferred_element_type=jnp.float32))
    return left_part.astype(jnp.bfloat16), right_part.astype(jnp.bfloat16), gating


def finish(pair_state, mixture, gating, out_gain, final_matrix):
    features = mixture.shape[0]
    flattened = mixture.astype(jnp.float32)
    normed = layer_norm(flattened, out_gain[:, None], 0).astype(jnp.bfloat16)
    update = jnp.einsum("cx,cd->xd", normed, final_matrix, preferred_element_type=jnp.float32)
    result = pair_state.reshape(-1, features).astype(jnp.float32) + gating * update
    return result.astype(jnp.bfloat16).reshape(pair_state.shape)


def update(incoming, sizes, pair_state, norm_gain, project, gate_matrix, out_gain, final_matrix):
    far, near, col_parts = sizes
    row_count, col_count, features = pair_state.shape
    parts = near * col_parts
    width = features // parts
    left_part, right_part, gating = project_in(pair_state, norm_gain, project, gate_matrix)
    both = jnp.stack([left_part.reshape(parts, width, -1), right_part.reshape(parts, width, -1)], axis=1)
    both = lax.all_to_all(both, EVERY, split_axis=0, concat_axis=0, tiled=True)
    both = both.reshape(near, col_parts, 2, width, row_count, col_count)
    both = both.transpose(2, 3, 0, 4, 1, 5).reshape(2, width, near * row_count, col_parts * col_count)
    left_part, right_part = both[0], both[1]
    if incoming:
        mixture = jnp.einsum("cki,ckj->cij", left_part, right_part, preferred_element_type=jnp.float32)
        if far > 1:
            mixture = lax.psum_scatter(mixture, "far", scatter_dimension=1, tiled=True)
    else:
        if far > 1:
            right_part = lax.all_gather(right_part, "far", axis=1, tiled=True)
        mixture = jnp.einsum("cik,cjk->cij", left_part, right_part, preferred_element_type=jnp.float32)
    mixture = mixture.astype(jnp.bfloat16).reshape(width, near, row_count, col_parts, col_count)
    mixture = mixture.transpose(1, 3, 0, 2, 4).reshape(parts, width, row_count * col_count)
    mixture = lax.all_to_all(mixture, EVERY, split_axis=0, concat_axis=0, tiled=True)
    return finish(pair_state, mixture.reshape(features, -1), gating, out_gain, final_matrix)


def split_rows(row_parts, col_parts, features, least):
    near = row_parts
    while near > 1 and (row_parts % near or features % (near * col_parts) or features < least * near * col_parts):
        near -= 1
    return row_parts // near, near


SMEM_SPEC = pl.BlockSpec(memory_space=pltpu.SMEM)
VMEM_SPEC = pl.BlockSpec(memory_space=pltpu.VMEM)


def lane_norm(values, norm_gain):
    lanes = values.shape[1]
    mean = jnp.dot(values, jnp.full((lanes, lanes), 1 / lanes, jnp.bfloat16), preferred_element_type=jnp.float32)
    centred = values.astype(jnp.float32) - mean
    variance = jnp.mean(centred * centred, axis=1, keepdims=True)
    return centred * lax.rsqrt(variance + epsilon) * norm_gain


def near_core(array):
    return pltpu.with_memory_space_constraint(array, pltpu.VMEM)


def step_lanes(span):
    return pl.ds(pl.multiple_of(pl.program_id(0) * span, span), span)


def emit_projections(normed, rows_ref, out_refs):
    step = normed.shape[0]
    half = rows_ref.shape[0] // 2
    group = 256 if step % 256 == 0 else LANES
    for begin in range(0, step, group):
        projected = lax.dot_general(
            rows_ref[...], normed[begin : begin + group, :], (((1,), (1,)), ((), ())), preferred_element_type=jnp.float32
        )
        gated = sigmoid(projected[:half, :]) * projected[half:, :]
        at = 0
        for ref in out_refs:
            parts, width, _ = ref.shape
            for part in range(parts):
                ref[part, :, begin : begin + group] = gated[at : at + width, :].astype(ref.dtype)
                at += width


def project_kernel(state_ref, gain_ref, rows_ref, *out_refs):
    normed = lane_norm(state_ref[...], gain_ref[...]).astype(jnp.bfloat16)
    emit_projections(normed, rows_ref, out_refs)


def finish_kernel(pieces, onward, *refs):
    mix_refs, refs = refs[:pieces], refs[pieces:]
    state_ref, gain_ref, gate_ref, out_gain_ref, final_ref = refs[:5]
    state = state_ref[...].astype(jnp.float32)
    normed = lane_norm(state_ref[...], gain_ref[...]).astype(jnp.bfloat16)
    gating = sigmoid(jnp.dot(normed, gate_ref[...], preferred_element_type=jnp.float32))
    lanes = step_lanes(state.shape[0])
    mixed = jnp.concatenate(
        [ref[part, :, lanes].astype(jnp.float32) for ref in mix_refs for part in range(ref.shape[0])], axis=0
    )
    mixed = layer_norm(mixed, out_gain_ref[...], 0).astype(jnp.bfloat16)
    change = lax.dot_general(
        mixed, final_ref[...], (((0,), (0,)), ((), ())), preferred_element_type=jnp.float32
    )
    result = (state + gating * change).astype(jnp.bfloat16)
    if onward:
        next_gain, rows_ref, middle_ref = refs[5:8]
        middle_ref[...] = result
        normed = lane_norm(result, next_gain[...]).astype(jnp.bfloat16)
        emit_projections(normed, rows_ref, refs[8:])
    else:
        refs[5][...] = result


def whole_spec(array):
    return pl.BlockSpec(array.shape, lambda step: (0,) * array.ndim)


def row_step(positions):
    step = positions
    for candidate in range(LANES, 2304 + 1, LANES):
        if positions % candidate == 0:
            step = candidate
    return step


def run_projections(state, gain, rows, out_shapes):
    positions, features = state.shape
    step = row_step(positions)
    weights = (gain[None, :], rows)
    return pl.pallas_call(
        project_kernel,
        grid=(positions // step,),
        in_specs=[pl.BlockSpec((step, features), lambda i: (i, 0))] + [whole_spec(w) for w in weights],
        out_specs=[pl.BlockSpec((*shape, step), lambda i: (0, 0, i)) for shape in out_shapes],
        out_shape=[jax.ShapeDtypeStruct((*shape, positions), jnp.bfloat16) for shape in out_shapes],
        compiler_params=pltpu.CompilerParams(vmem_limit_bytes=BUDGET),
        name="project",
    )(state, *weights)


def run_finish(mixes, state, gain, gate_matrix, out_gain, final_matrix, onward=None):
    positions, features = state.shape
    step = row_step(positions)
    weights = (gain[None, :], gate_matrix, out_gain[:, None], final_matrix)
    out_shape = [jax.ShapeDtypeStruct((positions, features), jnp.bfloat16)]
    out_specs = [pl.BlockSpec((step, features), lambda i: (i, 0))]
    if onward is not None:
        next_gain, rows, out_shapes = onward
        weights += (next_gain[None, :], rows)
        out_shape += [jax.ShapeDtypeStruct((*shape, positions), jnp.bfloat16) for shape in out_shapes]
        out_specs += [pl.BlockSpec((*shape, step), lambda i: (0, 0, i)) for shape in out_shapes]
    return pl.pallas_call(
        functools.partial(finish_kernel, len(mixes), onward is not None),
        grid=(positions // step,),
        in_specs=[VMEM_SPEC] * len(mixes)
        + [pl.BlockSpec((step, features), lambda i: (i, 0))]
        + [whole_spec(w) for w in weights],
        out_specs=out_specs,
        out_shape=out_shape,
        compiler_params=pltpu.CompilerParams(vmem_limit_bytes=BUDGET),
        name="finish",
    )(*map(near_core, mixes), state, *weights)


class Folds:
    def __init__(self, row_count, col_count):
        turn = 1
        while (turn * col_count) % LANES:
            turn *= 2
        self.turn, self.tiles = turn, turn * col_count // LANES
        self.cols, self.rows = col_count, row_count
        self.groups = row_count // turn
        self.lane_rows = row_count * col_count // LANES

    def fits(self):
        return self.cols <= LANES and self.rows % self.turn == 0 and self.groups % 8 == 0

    def split(self, lane_rows, clear=False):
        lane = lax.broadcasted_iota(jnp.int32, lane_rows[0].shape, 1)
        out = []
        for phase in range(self.turn):
            first, offset = divmod(phase * self.cols, LANES)
            value = lane_rows[first]
            if offset + self.cols > LANES:
                value = jnp.where(lane >= offset, value, lane_rows[first + 1])
            if offset:
                value = pltpu.roll(value, LANES - offset, 1)
            out.append(jnp.where(lane < self.cols, value, 0.0) if clear else value)
        return out

    def join(self, block_rows):
        lane = lax.broadcasted_iota(jnp.int32, block_rows[0].shape, 1)
        rolled = []
        for phase, value in enumerate(block_rows):
            offset = (phase * self.cols) % LANES
            rolled.append(pltpu.roll(value, offset, 1) if offset else value)
        out = []
        for tile in range(self.tiles):
            value = None
            for phase in range(self.turn):
                begin, end = phase * self.cols - tile * LANES, (phase + 1) * self.cols - tile * LANES
                if end <= 0 or begin >= LANES:
                    continue
                value = rolled[phase] if value is None else jnp.where(lane >= begin, rolled[phase], value)
            out.append(value)
        return out


def stage(source_ref, staged):
    parts, width, positions = source_ref.shape
    rows = parts * width

    @pl.loop(0, positions // LANES, unroll=8)
    def _(tile):
        lanes = pl.ds(pl.multiple_of(tile * LANES, LANES), LANES)
        for part in range(parts):
            staged[pl.ds(tile * rows + part * width, width), :] = source_ref[part, :, lanes].astype(jnp.float32)


def unstage(staged, target_ref, earlier_refs=()):
    parts, height, positions = target_ref.shape
    width = height - sum(ref.shape[1] for ref in earlier_refs)
    rows = parts * width

    @pl.loop(0, positions // LANES, unroll=8)
    def _(tile):
        lanes = pl.ds(pl.multiple_of(tile * LANES, LANES), LANES)
        for part in range(parts):
            values = [ref[part, :, lanes].astype(jnp.float32) for ref in earlier_refs]
            values.append(staged[pl.ds(tile * rows + part * width, width), :])
            values = values[0] if len(values) == 1 else jnp.concatenate(values, axis=0)
            target_ref[part, :, lanes] = values.astype(target_ref.dtype)


def lane_rows_of(folds, rows, row):
    return [pl.ds(row + tile * rows, folds.groups, stride=folds.tiles * rows) for tile in range(folds.tiles)]


def mix_out_kernel(folds, near, cols, width, stages, half_ref, *refs):
    parts = near * cols
    rows = parts * width
    block = folds.rows
    tall = near * block
    earlier_refs, near_ref = (), None
    if stages == (0, 1):
        left_ref, right_ref, there_ref, *earlier_refs, mix_ref, staged, right, folded, left = refs
    elif stages == (0,):
        left_ref, right_ref, mix_ref, left, staged, right, folded = refs
    else:
        left, near_ref, there_ref, *earlier_refs, mix_ref, staged, right, folded = refs

    def unfold(ref, shift, store):
        height = ref.shape[1]
        stage(ref, staged)

        @pl.loop(0, rows, unroll=8)
        def _(step):
            source, channel = step // width, step % width
            row = source * height + shift + channel
            store(source, channel, [staged[at, :] for at in lane_rows_of(folds, parts * height, row)])

    def store_left(source, channel, lane_rows):
        pieces = folds.split(lane_rows, clear=True)
        at = (channel * cols + source % cols) * tall + (source // cols) * block
        left[pl.ds(pl.multiple_of(at, block), block), :] = jnp.concatenate(pieces, axis=0).astype(jnp.bfloat16)

    def store_right(source, channel, lane_rows):
        at = (channel * cols + source % cols) * tall + (source // cols) * block
        for phase, piece in enumerate(folds.split(lane_rows)):
            right[pl.ds(at + phase, folds.groups, stride=folds.turn), :] = piece

    def products(half):
        @pl.loop(0, width)
        def _(channel):
            starts = [(channel * cols + col) * tall for col in range(cols)]
            lhs = jnp.concatenate([left[pl.ds(pl.multiple_of(at, block), tall), :] for at in starts], axis=1)
            for offset in range(near):
                at = [pl.multiple_of(start + offset * block, block) for start in starts]
                rhs = jnp.concatenate([right[pl.ds(begin, block), :] for begin in at], axis=1).astype(jnp.bfloat16)
                total = lax.dot_general(lhs, rhs, (((1,), (1,)), ((), ())), preferred_element_type=jnp.float32)
                total = jnp.concatenate([total, jnp.zeros((tall, LANES - block), jnp.float32)], axis=1)
                for piece in range(near):
                    lane_rows = folds.join(
                        [
                            total[piece * block + phase * folds.groups : piece * block + (phase + 1) * folds.groups, :]
                            for phase in range(folds.turn)
                        ]
                    )
                    out_row = (piece * cols + half * near + offset) * width + channel
                    for lanes, value in zip(lane_rows_of(folds, rows, out_row), lane_rows):
                        folded[lanes, :] = value

    if 0 in stages:
        unfold(left_ref, 0, store_left)
        unfold(right_ref, right_ref.shape[1] - width, store_right)
        products(half_ref[0])
    if 1 in stages:
        unfold(there_ref, 0, store_right)
        products(half_ref[1])

    @pl.loop(0, mix_ref.shape[2] // LANES, unroll=8)
    def _(tile):
        lanes = pl.ds(pl.multiple_of(tile * LANES, LANES), LANES)
        for part in range(parts):
            value = folded[pl.ds(tile * rows + part * width, width), :]
            if near_ref is not None:
                mine = half_ref[0] == part % cols // near
                value = jnp.where(mine, near_ref[part, :, lanes].astype(jnp.float32), value)
            values = [ref[part, :, lanes].astype(jnp.float32) for ref in earlier_refs] + [value]
            values = values[0] if len(values) == 1 else jnp.concatenate(values, axis=0)
            mix_ref[part, :, lanes] = values.astype(mix_ref.dtype)


def mix_in_kernel(folds, near, cols, width, stages, half_ref, both_ref, *refs):
    targets, (staged, left, right, turned, mixed) = refs[:-5], refs[-5:]
    parts = near * cols
    block = folds.rows
    tall = near * block
    out_rows = parts * width

    stage(both_ref, staged)

    def unfold(target, source, channel, shift):
        row = source * 2 * width + shift + channel
        pieces = folds.split([staged[at, :] for at in lane_rows_of(folds, 2 * out_rows, row)])
        at = (channel * cols + source % cols) * tall + (source // cols) * block
        target[pl.ds(pl.multiple_of(at, block), block), :] = jnp.concatenate(pieces, axis=0).astype(jnp.bfloat16)

    @pl.loop(0, parts * width, unroll=8)
    def _(at):
        unfold(right, at // width, at % width, width)

    for which, target_ref in zip(stages, targets):
        half = half_ref[which]

        @pl.loop(0, near * near * width, unroll=8)
        def _(at):
            place, channel = at // width, at % width
            unfold(left, place // near * cols + half * near + place % near, channel, 0)

        @pl.loop(0, width)
        def _(channel):
            starts = [pl.multiple_of((channel * cols + col) * tall, block) for col in range(cols)]
            rhs = jnp.concatenate([right[pl.ds(start, tall), :] for start in starts], axis=1)
            for piece in range(near):
                start = pl.multiple_of((channel * cols + half * near + piece) * tall, block)
                summed = lax.dot_general(
                    left[pl.ds(start, tall), :], rhs, (((0,), (0,)), ((), ())), preferred_element_type=jnp.float32
                )
                for target in range(cols):
                    turned[piece, target] = summed[:, target * LANES : (target + 1) * LANES]
                    lane_rows = folds.join(
                        [
                            turned[piece, target, pl.ds(phase, folds.groups, stride=folds.turn), :]
                            for phase in range(folds.turn)
                        ]
                    )
                    out_row = (piece * cols + target) * width + channel
                    for lanes, value in zip(lane_rows_of(folds, out_rows, out_row), lane_rows):
                        mixed[lanes, :] = value

        unstage(mixed, target_ref)


def run_mix_out(folds, near, cols, width, stages, halves, *arrays, mine=None, earlier=()):
    parts, _, positions = arrays[-1].shape
    rows = parts * width
    tall = width * cols * near * folds.rows
    out_shape = [jax.ShapeDtypeStruct((parts, width + sum(e.shape[1] for e in earlier), positions), jnp.bfloat16)]
    scratch = [
        pltpu.VMEM((2 * rows * folds.lane_rows, LANES), jnp.float32),
        pltpu.VMEM((tall, LANES), jnp.float32),
        pltpu.VMEM((rows * folds.lane_rows, LANES), jnp.float32),
    ]
    if stages == (0,):
        out_shape.append(jax.ShapeDtypeStruct((tall, LANES), jnp.bfloat16))
    elif stages == (0, 1):
        scratch.append(pltpu.VMEM((tall, LANES), jnp.bfloat16))
    return pl.pallas_call(
        functools.partial(mix_out_kernel, folds, near, cols, width, stages),
        in_specs=[SMEM_SPEC] + [VMEM_SPEC] * (len(arrays) + len(earlier)),
        out_specs=[VMEM_SPEC] * len(out_shape),
        out_shape=out_shape,
        scratch_shapes=scratch,
        compiler_params=pltpu.CompilerParams(vmem_limit_bytes=BUDGET),
        name="mix_out",
    )(halves, *(array if array.ndim < 3 or array is mine else near_core(array) for array in arrays), *earlier)


def add_kernel(*refs):
    target_ref = refs[-1]
    parts = target_ref.shape[0]
    lanes = step_lanes(target_ref.shape[2])
    for part in range(parts):
        sums = [kept[part] + got[part, :, lanes].astype(jnp.float32) for kept, got in zip(refs[:-1:2], refs[1:-1:2])]
        target_ref[part] = jnp.concatenate(sums, axis=0).astype(target_ref.dtype)


def run_add(*arrays):
    parts, _, positions = arrays[0].shape
    step = positions // 2 if positions % (2 * LANES) == 0 else positions
    height = sum(array.shape[1] for array in arrays) // 2
    return pl.pallas_call(
        add_kernel,
        grid=(positions // step,),
        in_specs=[pl.BlockSpec((*array.shape[:2], step), lambda i: (0, 0, i)) if at % 2 == 0 else VMEM_SPEC for at, array in enumerate(arrays)],
        out_specs=pl.BlockSpec((parts, height, step), lambda i: (0, 0, i)),
        out_shape=jax.ShapeDtypeStruct((parts, height, positions), jnp.bfloat16),
        compiler_params=pltpu.CompilerParams(vmem_limit_bytes=BUDGET),
        name="add",
    )(*(near_core(array) if at % 2 else array for at, array in enumerate(arrays)))


def run_mix_in(folds, near, cols, stages, halves, both):
    parts, width, positions = both.shape
    rows, width = parts * width, width // 2
    tall = width * cols * near * folds.rows
    types = (jnp.float32, jnp.bfloat16)
    return pl.pallas_call(
        functools.partial(mix_in_kernel, folds, near, cols, width, stages),
        in_specs=[SMEM_SPEC, VMEM_SPEC],
        out_specs=[VMEM_SPEC] * len(stages),
        out_shape=[jax.ShapeDtypeStruct((parts, width, positions), types[which]) for which in stages],
        scratch_shapes=[
            pltpu.VMEM((rows * folds.lane_rows, LANES), jnp.float32),
            pltpu.VMEM((tall, LANES), jnp.bfloat16),
            pltpu.VMEM((tall, LANES), jnp.bfloat16),
            pltpu.VMEM((near, cols, LANES, LANES), jnp.float32),
            pltpu.VMEM((rows // 2 * folds.lane_rows, LANES), jnp.float32),
        ],
        compiler_params=pltpu.CompilerParams(vmem_limit_bytes=BUDGET),
        name="mix_in",
    )(halves, near_core(both))


SHARES = (1, 1, 1, 1)
OUT_GROUPS = ((0, 1), (2, 3))
IN_GROUPS = ((0, 1), (2,), (3,))
PIECES = len(SHARES)


def exchange(array):
    return lax.all_to_all(array, EVERY, split_axis=0, concat_axis=0, tiled=True)


def across(array):
    return lax.ppermute(array, "far", ((0, 1), (1, 0)))


def in_halves(sizes, pair_input, weights):
    _, near, cols = sizes
    row_count, col_count, features = pair_input.shape
    parts = near * cols
    width = features // parts
    ends = [sum(SHARES[: at + 1]) * width // sum(SHARES) for at in range(PIECES)]
    begins = [0] + ends[:-1]
    folds = Folds(row_count, col_count)
    half = lax.axis_index("far")
    halves = jnp.stack([half, 1 - half]).astype(jnp.int32)

    def rows_of(project, *arrays):
        ga, va, gb, vb = (rows.reshape(parts, width, features) for rows in jnp.split(project.T, 4, axis=0))

        def ordered(left, right):
            return [
                jnp.concatenate(
                    [rows[:, begins[piece] : ends[piece]] for rows, piece in zip((left, right), pair) if piece is not None],
                    axis=1,
                ).reshape(-1, features)
                for pair in arrays
            ]

        return jnp.concatenate(ordered(ga, gb) + ordered(va, vb))

    def shapes_of(*arrays):
        return [
            (parts, sum(ends[piece] - begins[piece] for piece in pair if piece is not None)) for pair in arrays
        ]

    def in_groups(array, groups):
        rows = array.reshape(parts, width, -1)
        ordered = [
            jnp.concatenate([rows[:, begins[piece] : ends[piece]] for piece in group], axis=1).reshape(-1, rows.shape[-1])
            for group in groups
        ]
        return jnp.concatenate(ordered).reshape(array.shape)

    gain_1, project_1, gate_1, norm_1, final_1, gain_2, project_2, gate_2, norm_2, final_2 = weights
    state = pair_input.reshape(-1, features)

    ahead = [(None, 0)] + [(piece, piece + 1) for piece in range(PIECES - 1)] + [(PIECES - 1, None)]
    level = [(piece, piece) for piece in range(PIECES)]
    sent, mixed, mixes = [], [None] * PIECES, []
    out = run_projections(state, gain_1, rows_of(project_1, *ahead[:1]), shapes_of(*ahead[:1]))
    out += run_projections(state, gain_1, rows_of(project_1, *ahead[1:]), shapes_of(*ahead[1:]))
    for array in out:
        sent.append(exchange(array))
    for piece in range(PIECES):
        group = next(group for group in OUT_GROUPS if piece in group)
        right, left = sent[piece], sent[piece + 1]
        there = across(right[:, right.shape[1] - (ends[piece] - begins[piece]) :, :])
        earlier = [mixed[other] for other in group[:-1]] if piece == group[-1] else ()
        mix = functools.partial(run_mix_out, folds, near, cols, ends[piece] - begins[piece])
        if piece < PIECES - 1:
            mixed[piece] = mix((0, 1), halves, left, right, there, earlier=earlier)[0]
        else:
            mine, unfolded = mix((0,), halves, left, right)
            mixed[piece] = mix((1,), halves, unfolded, mine, there, mine=mine, earlier=earlier)[0]
        if piece == group[-1]:
            mixes.append(exchange(mixed[piece]))
    onward = (gain_2, rows_of(project_2, *level[:1]), shapes_of(*level[:1]))
    middle, *out = run_finish(mixes, state, gain_1, gate_1, in_groups(norm_1, OUT_GROUPS), in_groups(final_1, OUT_GROUPS), onward)
    out += run_projections(middle, gain_2, rows_of(project_2, *level[1:]), shapes_of(*level[1:]))
    both, parted, mixes = [], [], []
    for piece in range(PIECES):
        both.append(exchange(out[piece]))
    for piece in range(PIECES):
        mix = functools.partial(run_mix_in, folds, near, cols)
        sent = mix((1,), halves, both[piece])[0]
        kept = mix((0,), halves, both[piece])[0]
        parted.append((kept, across(sent)))
    for group in IN_GROUPS:
        summed = run_add(*(array for piece in group for array in parted[piece]))
        mixes.append(exchange(summed))
    result = run_finish(mixes, middle, gain_2, gate_2, in_groups(norm_2, IN_GROUPS), in_groups(final_2, IN_GROUPS))[0]
    return result.reshape(pair_input.shape)


def solution(mesh):
    row_parts, col_parts = mesh.shape["dap"], mesh.shape["chan"] * mesh.shape["sub"]

    def whole(pair_input, *weights):
        features = pair_input.shape[-1]
        block_rows = pair_input.shape[0] // (mesh.shape["groups"] * row_parts)
        block_cols = pair_input.shape[1] // col_parts
        halved = (
            row_parts % 2 == 0
            and row_parts == col_parts
            and block_rows == block_cols
            and Folds(block_rows, block_cols).fits()
            and features == LANES
            and features % (row_parts // 2 * col_parts * sum(SHARES)) == 0
        )
        if halved:
            far, near = 2, row_parts // 2
        else:
            far, near = split_rows(row_parts, col_parts, features, 8)
        sizes = (far, near, col_parts)
        finer = Mesh(
            mesh.devices.reshape(mesh.shape["groups"], far, near, mesh.shape["chan"], mesh.shape["sub"]),
            ("groups", "far", "near", "chan", "sub"),
        )

        def shards(pair_input, *weights):
            if halved:
                return in_halves(sizes, pair_input, weights)
            middle = update(False, sizes, pair_input, *weights[:5])
            return update(True, sizes, middle, *weights[5:])

        pair_spec = P(("groups", "far", "near"), ("chan", "sub"), None)
        mapped = jax.shard_map(
            shards,
            mesh=finer,
            in_specs=(pair_spec,) + (P(),) * 10,
            out_specs=pair_spec,
            check_vma=False,
        )
        return mapped(pair_input, *weights)

    return whole
```
